32 devices in a mesh: dp: 8 (over z, x), tensor: 4 (over y, core).
Axes of the slice: x: 2, y: 2, z: 4, core: 2. Of those that a mesh axis runs over, the one named last changes fastest.
Arguments:
- tokens: bfloat16 [8192, 1024], P('dp')
- segments: int32 [8, 1024], P('dp'), may hold values from -1 to 16, as said below
- w_query: bfloat16 [1024, 1024], P(None, 'tensor'), may hold values from -0.1875 to 0.1875
- w_key: bfloat16 [1024, 1024], P(None, 'tensor'), may hold values from -0.1875 to 0.1875
- w_value: bfloat16 [1024, 1024], P(None, 'tensor'), may hold values from -0.1875 to 0.1875
- w_out: bfloat16 [1024, 1024], P(None, 'tensor'), may hold values from -0.1875 to 0.1875
- w_fc1: bfloat16 [1024, 4096], P(None, 'tensor'), may hold values from -0.1875 to 0.1875
- w_fc2: bfloat16 [1024, 4096], P(None, 'tensor'), may hold values from -0.09375 to 0.09375
- ln1_gain: float32 [1024], replicated, may hold values from 0.5 to 1.5
- ln1_bias: float32 [1024], replicated, may hold values from -1.2 to 1.2
- post_gain: float32 [1024], replicated, may hold values from 0.5 to 1.5
- post_bias: float32 [1024], replicated, may hold values from -1.2 to 1.2
- ln2_gain: float32 [1024], replicated, may hold values from 0.5 to 1.5
- ln2_bias: float32 [1024], replicated, may hold values from -1.2 to 1.2
- mid_gain: float32 [4096], P('tensor'), may hold values from 0.5 to 1.5
- mid_bias: float32 [4096], P('tensor'), may hold values from -1.2 to 1.2
- query_bias: float32 [1024], P('tensor'), may hold values from -1.2 to 1.2
- value_bias: float32 [1024], P('tensor'), may hold values from -1.2 to 1.2
- out_bias: float32 [1024], replicated, may hold values from -1.2 to 1.2
- fc1_bias: float32 [4096], P('tensor'), may hold values from -1.2 to 1.2
- fc2_bias: float32 [1024], replicated, may hold values from -1.2 to 1.2
- head_scale: float32 [16], P('tensor'), may hold values from 0.25 to 1.75
- cotangent: bfloat16 [8192, 1024], P('dp'), may hold values from -6 to 6
Outputs:
- output: bfloat16 [8192, 1024], P('dp')
- grad_tokens: float32 [8192, 1024], P('dp')
- grad_w_query: float32 [1024, 1024], P('dp', 'tensor')
- grad_w_key: float32 [1024, 1024], P('dp', 'tensor')
- grad_w_value: float32 [1024, 1024], P('dp', 'tensor')
- grad_w_out: float32 [1024, 1024], P('dp', 'tensor')
- grad_w_fc1: float32 [1024, 4096], P('dp', 'tensor')
- grad_w_fc2: float32 [1024, 4096], P('dp', 'tensor')
- grad_ln1_gain: float32 [1024], replicated
- grad_ln1_bias: float32 [1024], replicated
- grad_post_gain: float32 [1024], replicated
- grad_post_bias: float32 [1024], replicated
- grad_ln2_gain: float32 [1024], replicated
- grad_ln2_bias: float32 [1024], replicated
- grad_mid_gain: float32 [4096], P('tensor')
- grad_mid_bias: float32 [4096], P('tensor')
- grad_query_bias: float32 [1024], P('tensor')
- grad_value_bias: float32 [1024], P('tensor')
- grad_out_bias: float32 [1024], replicated
- grad_fc1_bias: float32 [4096], P('tensor')
- grad_fc2_bias: float32 [1024], replicated
- grad_head_scale: float32 [16], P('tensor')
- rms: float32 [3], replicated
The draws below stay inside these ranges and needn't reach their ends.
Inputs may be any that keep to these rules, and one draw needn't show every extreme that they name: `segments`: each row of 1024 tokens holds whole documents of 60 to 800 tokens, numbered 0, 1, 2 and so on from the row's start, then padding marked -1 where the next document would not fit; the first document always fits. Some row holds only documents of 60 tokens followed by padding.
All inputs are finite; a program needn't handle non-finite values.
Results may differ from the reference program's by a relative error of at most 0.014.
Values sent between devices are 32-bit elements; how exact they have to be, the bound alone decides.
No kernel may reach another device: no remote copies, remote signals or barrier semaphores. Data moves between devices by JAX's collectives and lax.ppermute only.
A program may use at most 128 MiB of HBM per device.

```python
import jax
import jax.numpy as jnp
from jax import lax

D = 1024
HEADS = 16
HEAD_DIM = 64
FF = 4096
SEQ_LEN = 1024
DOC_MIN = 60
DOC_MAX = 800
BATCH = 8
TOKENS = 8192


def draw_segments(key, part):
    lengths = jax.random.randint(key, (BATCH, SEQ_LEN // DOC_MIN + 1), DOC_MIN, DOC_MAX + 1)
    chosen = jax.random.randint(jax.random.fold_in(key, 7), (), 0, BATCH)
    lengths = jnp.where(jnp.arange(BATCH)[:, None] == chosen, DOC_MIN, lengths).astype(jnp.int32)
    ends = jnp.cumsum(lengths, axis=1)
    place = jnp.arange(SEQ_LEN)
    number = jnp.sum((ends[:, None, :] <= place[None, :, None]).astype(jnp.int32), axis=2)
    fitted = jnp.sum((ends <= SEQ_LEN).astype(jnp.int32), axis=1)
    return jnp.where(number < fitted[:, None], number, -1).astype(jnp.int32)


def draw_tokens(key, part):
    first, second = jax.random.split(key)
    base = jax.random.normal(first, (TOKENS, D), jnp.float32)
    rows = jnp.exp(jax.random.uniform(second, (TOKENS, 1), jnp.float32, -0.5, 0.5))
    order = (jnp.arange(TOKENS) // SEQ_LEN).astype(jnp.float32)[:, None]
    rising = 1.0 + 2.0 * order / max(BATCH - 1, 1)
    return (base * rows * rising).astype(jnp.bfloat16)


def level_of(key, dims, shards, smallest, high):
    factor_of, own = 1.0, jax.random.fold_in(key, 6)
    for axis_at, parts in shards:
        draws = jnp.exp(jax.random.uniform(jax.random.fold_in(own, axis_at), (parts,), jnp.float32, smallest / len(shards), high / len(shards)))
        factor_of = factor_of * jnp.repeat(draws, dims[axis_at] // parts).reshape([-1 if axis == axis_at else 1 for axis in range(len(dims))])
    return factor_of


def noise(rng, shape, spread, bound, cuts=(), kind=jnp.bfloat16):
    level = level_of(rng, shape, cuts, -0.22, 0.18) if cuts else 1.0
    drawn = jax.random.normal(rng, shape, jnp.float32) * spread * level
    return jnp.minimum(jnp.maximum(drawn, -bound), bound).astype(kind)


def setup_inputs(seed: int = 0) -> dict:
    keys = jax.random.split(jax.random.key(seed), 24)
    return {
        "tokens": draw_tokens(jax.random.fold_in(keys[23], 71), 0),
        "segments": draw_segments(jax.random.fold_in(keys[23], 71), 0),
        "w_query": noise(keys[2], (D, D), D ** -0.5, 0.1875, ((1, 4),)),
        "w_key": noise(keys[3], (D, D), D ** -0.5, 0.1875, ((1, 4),)),
        "w_value": noise(keys[4], (D, D), D ** -0.5, 0.1875, ((1, 4),)),
        "w_out": noise(keys[5], (D, D), D ** -0.5, 0.1875, ((1, 4),)),
        "w_fc1": noise(keys[6], (D, FF), D ** -0.5, 0.1875, ((1, 4),)),
        "w_fc2": noise(keys[7], (D, FF), FF ** -0.5, 0.09375, ((1, 4),)),
        "ln1_gain": jnp.clip(1.0 + 0.1 * jax.random.normal(keys[8], (D,), jnp.float32), 0.5, 1.5),
        "ln1_bias": noise(keys[9], (D,), 0.3, 1.2, (), jnp.float32),
        "post_gain": jnp.clip(1.0 + 0.1 * jax.random.normal(keys[10], (D,), jnp.float32), 0.5, 1.5),
        "post_bias": noise(keys[11], (D,), 0.3, 1.2, (), jnp.float32),
        "ln2_gain": jnp.clip(1.0 + 0.1 * jax.random.normal(keys[12], (D,), jnp.float32), 0.5, 1.5),
        "ln2_bias": noise(keys[13], (D,), 0.3, 1.2, (), jnp.float32),
        "mid_gain": jnp.clip(1.0 + 0.1 * jax.random.normal(keys[14], (FF,), jnp.float32), 0.5, 1.5),
        "mid_bias": noise(keys[15], (FF,), 0.3, 1.2, ((0, 4),), jnp.float32),
        "query_bias": noise(keys[16], (D,), 0.3, 1.2, ((0, 4),), jnp.float32),
        "value_bias": noise(keys[17], (D,), 0.3, 1.2, ((0, 4),), jnp.float32),
        "out_bias": noise(keys[18], (D,), 0.3, 1.2, (), jnp.float32),
        "fc1_bias": noise(keys[19], (FF,), 0.3, 1.2, ((0, 4),), jnp.float32),
        "fc2_bias": noise(keys[20], (D,), 0.3, 1.2, (), jnp.float32),
        "head_scale": jnp.clip(1.0 + 0.15 * jax.random.normal(keys[21], (HEADS,), jnp.float32), 0.25, 1.75),
        "cotangent": noise(keys[22], (TOKENS, D), 1.0, 6.0, ((0, 8),)),
    }


@jax.custom_vjp
def low(v):
    return lax.optimization_barrier(v.astype(jnp.bfloat16)).astype(jnp.float32)

@jax.custom_vjp
def low_back(v):
    return v

def low_keep(v):
    return (low(v), None)

def low_pass(kept, grad):
    return (grad,)

def back_keep(v):
    return (v, None)

def back_low(kept, grad):
    return (low(grad),)
low.defvjp(low_keep, low_pass)
low_back.defvjp(back_keep, back_low)
epsilon = 1e-05
highest = lax.Precision.HIGHEST

def norm_rows(v, gain, shift):
    mean = lax.optimization_barrier(jnp.mean(v, axis=-1, keepdims=True))
    centred = v - mean
    factor = lax.rsqrt(lax.optimization_barrier(jnp.mean(centred * centred, axis=-1, keepdims=True)) + epsilon)
    return centred * factor * gain + shift

def layer(x, weights, allowed):
    w_query, w_key, w_value, w_out, w_fc1, w_fc2, ln1_gain, ln1_bias, post_gain, post_bias, ln2_gain, ln2_bias, mid_gain, mid_bias, query_bias, value_bias, out_bias, fc1_bias, fc2_bias, head_scale = weights
    length = x.shape[0]
    entry = low(norm_rows(x, ln1_gain, ln1_bias))
    query = low(low_back(jnp.dot(entry, w_query, precision=highest) + query_bias))
    keyed = low(low_back(jnp.dot(entry, w_key, precision=highest)))
    valued = low(low_back(jnp.dot(entry, w_value, precision=highest) + value_bias))
    query4 = query.reshape(length, HEADS, HEAD_DIM)
    key4 = keyed.reshape(length, HEADS, HEAD_DIM)
    value4 = valued.reshape(length, HEADS, HEAD_DIM)
    scores = low_back(jnp.einsum('qhd,khd->hqk', query4, key4, precision=highest) * HEAD_DIM ** (-0.5))
    scores = jnp.where(allowed[None], scores, -1e+30)
    probs = low(jax.nn.softmax(scores, axis=-1))
    attended = low_back(jnp.einsum('hqk,khd->qhd', probs, value4, precision=highest))
    context = low((attended * head_scale[:, None]).reshape(length, HEADS * HEAD_DIM))
    mixed = low_back(jnp.dot(context, w_out.T, precision=highest) + out_bias)
    branch = norm_rows(mixed, post_gain, post_bias)
    stream = x + branch
    inner = low(norm_rows(stream, ln2_gain, ln2_bias))
    hidden = low_back(jnp.dot(inner, w_fc1, precision=highest) + fc1_bias)
    active = jax.nn.gelu(hidden, approximate=True)
    middle = low(norm_rows(active, mid_gain, mid_bias))
    ffn_out = low_back(jnp.dot(middle, w_fc2.T, precision=highest) + fc2_bias)
    return (stream + ffn_out, (branch, ffn_out))

def reference(tokens, segments, w_query, w_key, w_value, w_out, w_fc1, w_fc2, ln1_gain, ln1_bias, post_gain, post_bias, ln2_gain, ln2_bias, mid_gain, mid_bias, query_bias, value_bias, out_bias, fc1_bias, fc2_bias, head_scale, cotangent):
    params = tuple((item.astype(jnp.float32) for item in (w_query, w_key, w_value, w_out, w_fc1, w_fc2, ln1_gain, ln1_bias, post_gain, post_bias, ln2_gain, ln2_bias, mid_gain, mid_bias, query_bias, value_bias, out_bias, fc1_bias, fc2_bias, head_scale)))
    batch = segments.shape[0]
    length = segments.shape[1]
    width = tokens.shape[1]
    inputs = (tokens.astype(jnp.float32).reshape(batch, length, width), segments, cotangent.astype(jnp.float32).reshape(batch, length, width))
    place = jnp.arange(length)

    def step(carry, item):
        totals, stats = carry
        x, seg, upstream = item
        allowed = (seg[:, None] == seg[None, :]) & (place[None, :] <= place[:, None])

        def forward(xin, weights):
            return layer(xin, weights, allowed)
        result, pull, aux = jax.vjp(forward, x, params, has_aux=True)
        grad_x, grads = pull(upstream)
        branch, ffn_out = aux
        valid = (seg >= 0).astype(jnp.float32)[:, None]
        fresh = jnp.stack([jnp.sum(valid * branch * branch), jnp.sum(valid * ffn_out * ffn_out), jnp.sum(valid * result * result), jnp.sum(valid)])
        totals = jax.tree.map(lambda left, right: left + right, totals, grads)
        return ((totals, stats + fresh), (result.astype(jnp.bfloat16), grad_x))
    start = (jax.tree.map(jnp.zeros_like, params), jnp.zeros((4,), jnp.float32))
    (totals, stats), (outputs, grad_x) = lax.scan(step, start, inputs)
    rms = jnp.sqrt(stats[:3] / (stats[3] * D))
    return (outputs.reshape(batch * length, width), grad_x.reshape(batch * length, width), totals[0], totals[1], totals[2], totals[3], totals[4], totals[5], totals[6], totals[7], totals[8], totals[9], totals[10], totals[11], totals[12], totals[13], totals[14], totals[15], totals[16], totals[17], totals[18], totals[19], rms)
```

```python
import functools

import jax
import jax.numpy as jnp
from jax import lax
from jax.experimental import pallas as pl
from jax.experimental.pallas import tpu as pltpu
from jax.sharding import PartitionSpec as P

HEAD_DIM = 64
EPSILON = 1e-05
EXCLUDED = -1e30
LANES = 128
CHUNKS = 2
BF = jnp.bfloat16
F32 = jnp.float32


def dot_nn(a, b):
    return lax.dot_general(a, b, (((1,), (0,)), ((), ())), preferred_element_type=F32)


def dot_nt(a, b):
    return lax.dot_general(a, b, (((1,), (1,)), ((), ())), preferred_element_type=F32)


def dot_tn(a, b):
    return lax.dot_general(a, b, (((0,), (0,)), ((), ())), preferred_element_type=F32)


def normalize(v):
    mean = jnp.mean(v, axis=-1, keepdims=True)
    centred = v - mean
    factor = lax.rsqrt(jnp.mean(centred * centred, axis=-1, keepdims=True) + EPSILON)
    return centred * factor, factor


def norm_back(scaled, normed, factor):
    return factor * (
        scaled
        - jnp.mean(scaled, axis=-1, keepdims=True)
        - normed * jnp.mean(scaled * normed, axis=-1, keepdims=True)
    )


def col_sum(v):
    return jnp.sum(v, axis=0, keepdims=True)


def tanh_inner(v):
    return 0.7978845608028654 * (v + 0.044715 * (v * v * v))


def columns_to_rows(columns):
    n = columns[0].shape[0]
    lane = lax.broadcasted_iota(jnp.int32, (n, LANES), 1)
    tile = jnp.zeros((n, LANES), F32)
    for index, column in enumerate(columns):
        tile = jnp.where(lane == index, column, tile)
    return jnp.transpose(tile)[:8]


def rows_to_columns(rows):
    n = rows[0].shape[1]
    sub = lax.broadcasted_iota(jnp.int32, (LANES, n), 0)
    tile = jnp.zeros((LANES, n), F32)
    for index, row in enumerate(rows):
        tile = jnp.where(sub == index, row, tile)
    tile = jnp.transpose(tile)
    return [tile[:, index : index + 1] for index in range(len(rows))]


def stack_rows(rows, width):
    sub = lax.broadcasted_iota(jnp.int32, (8, width), 0)
    tile = jnp.zeros((8, width), F32)
    for index, row in enumerate(rows):
        tile = jnp.where(sub == index, row, tile)
    return tile


def head_masks(width, kind):
    lane = lax.broadcasted_iota(jnp.int32, (1, width), 1) // HEAD_DIM
    return [(lane == head).astype(F32).astype(kind) for head in range(width // HEAD_DIM)]


def qkv_kernel(tok, gain, bias, wq, wk, wv, qb, vb, entry, q, k, v):
    normed, _ = normalize(tok[...].astype(F32))
    low = (normed * gain[...] + bias[...]).astype(BF)
    entry[...] = low
    q[...] = ((dot_nn(low, wq[...]) + qb[...]) * HEAD_DIM**-0.5).astype(BF)
    k[...] = dot_nn(low, wk[...]).astype(BF)
    v[...] = (dot_nn(low, wv[...]) + vb[...]).astype(BF)


def attend_kernel(first, block, q, k, v, segq, segk, scale, attended, context, logsum):
    rows, width = q.shape
    masks = head_masks(width, BF)
    for at in range(0, rows, block):
        length = first + at + block
        query = q[at : at + block, :]
        keys = k[:length, :]
        (seg,) = rows_to_columns([segq[:, at : at + block].astype(F32)])
        place_q = first + at + lax.broadcasted_iota(jnp.int32, (block, length), 0)
        place_k = lax.broadcasted_iota(jnp.int32, (block, length), 1)
        allowed = (seg == segk[:, :length].astype(F32)) & (place_k <= place_q)
        shift = jnp.where(allowed, 0.0, EXCLUDED)
        total = jnp.zeros((block, width), F32)
        sums = []
        for mask in masks:
            scores = dot_nt(query * mask, keys) + shift
            top = jnp.max(scores, axis=-1, keepdims=True)
            expo = jnp.exp(scores - top)
            norm = jnp.sum(expo, axis=-1, keepdims=True)
            weights = (expo * (1.0 / norm)).astype(BF)
            total = total + dot_nn(weights, v[:length, :] * mask)
            sums.append(top + jnp.log(norm))
        attended[at : at + block, :] = total
        context[at : at + block, :] = (total * scale[...]).astype(BF).astype(F32)
        logsum[:, at : at + block] = columns_to_rows(sums)


def forward_kernel(
    seg, ctx0, ctx1, ctx2, ctx3, wo0, wo1, wo2, wo3, out_bias, tok,
    post_gain, post_bias, ln2_gain, ln2_bias, w_fc1, fc1_bias, cot, w_fc2, mid_gain,
    mixed, stream, inner, hidden, grad_middle, stats, sums,
):
    step = pl.program_id(0)
    mix = (
        (dot_nt(ctx0[...].astype(BF), wo0[...]) + dot_nt(ctx1[...].astype(BF), wo1[...].astype(BF)))
        + (dot_nt(ctx2[...].astype(BF), wo2[...].astype(BF)) + dot_nt(ctx3[...].astype(BF), wo3[...].astype(BF)))
        + out_bias[...]
    )
    mixed[...] = mix
    normed, _ = normalize(mix)
    branch = normed * post_gain[...] + post_bias[...]
    resid = tok[...].astype(F32) + branch
    stream[...] = resid
    normed2, _ = normalize(resid)
    low = (normed2 * ln2_gain[...] + ln2_bias[...]).astype(BF)
    inner[...] = low
    hid = dot_nn(low, w_fc1[...]) + fc1_bias[...]
    hidden[...] = hid
    active = 0.5 * hid * (1.0 + jnp.tanh(tanh_inner(hid)))
    upstream = cot[...]
    grad = dot_nn(upstream, w_fc2[...])
    grad_middle[...] = grad
    scaled = grad * mid_gain[...]
    mean = jnp.mean(active, axis=-1, keepdims=True)
    centred = active - mean
    stats[...] = columns_to_rows(
        [
            mean,
            jnp.sum(centred * centred, axis=-1, keepdims=True),
            jnp.sum(scaled, axis=-1, keepdims=True),
            jnp.sum(scaled * centred, axis=-1, keepdims=True),
        ]
    )
    (place,) = rows_to_columns([seg[...].astype(F32)])
    valid = (place >= 0).astype(F32)
    fresh = stack_rows(
        [col_sum(valid * branch * branch), col_sum(upstream.astype(F32)), col_sum(valid * jnp.ones_like(branch))],
        branch.shape[1],
    )

    @pl.when(step == 0)
    def _():
        sums[...] = fresh

    @pl.when(step != 0)
    def _():
        sums[...] += fresh


def middle_kernel(
    units, order, hidden, grad_middle, st0, st1, st2, st3, mid_gain, mid_bias, w_fc1, w_fc2,
    middle, grad_hidden, ffn_send, ffn_keep, inner_send, inner_keep, sums,
):
    step = pl.program_id(0)
    n = hidden.shape[1]
    stats = (st0, st1, st2, st3)

    def tree(terms):
        return (terms[0] + terms[1]) + (terms[2] + terms[3])

    means = [s[0:1, :] for s in stats]
    mean = tree(means) * (n / units)
    apart = [m - mean for m in means]
    spread = tree([s[1:2, :] + n * (d * d) for s, d in zip(stats, apart)])
    factor = lax.rsqrt(spread / units + EPSILON)
    plain = tree([s[2:3, :] for s in stats]) / units
    along = factor * tree([s[3:4, :] + d * s[2:3, :] for s, d in zip(stats, apart)]) / units
    mean, factor, plain, along = rows_to_columns([mean, factor, plain, along])
    hid = hidden[...]
    bend = jnp.tanh(tanh_inner(hid))
    active = 0.5 * hid * (1.0 + bend)
    slope = 0.5 * (1.0 + bend) + 0.5 * hid * (1.0 - bend * bend) * (
        0.7978845608028654 * (1.0 + 3 * 0.044715 * (hid * hid))
    )
    normed = (active - mean) * factor
    mid = (normed * mid_gain[...] + mid_bias[...]).astype(BF)
    middle[...] = mid
    grad = grad_middle[...]
    low = (factor * (grad * mid_gain[...] - plain - normed * along) * slope).astype(BF)
    grad_hidden[...] = low
    fresh = stack_rows([col_sum(grad * normed), col_sum(grad), col_sum(low.astype(F32))], n)
    ffn = dot_nt(mid, w_fc2[...])
    back = dot_nt(low, w_fc1[...])

    @pl.when(step == 0)
    def _():
        sums[...] = fresh
        ffn_send[...] = ffn
        inner_send[...] = back

    @pl.when(step != 0)
    def _():
        sums[...] += fresh
        ffn_keep[...] = ffn
        inner_keep[...] = back


def stream_kernel(
    order, mine, other, mixed, stream, cot, ln2_gain, post_gain, w_out, attended, scale,
    grad_stream, grad_mixed, grad_attended, delta, sums, head_sums,
):
    step = pl.program_id(0)
    grad = jnp.where(step == 0, mine[...], other[...])
    normed2, factor2 = normalize(stream[...])
    back = cot[...].astype(F32) + norm_back(grad * ln2_gain[...], normed2, factor2)
    grad_stream[...] = back
    normedp, factorp = normalize(mixed[...])
    low = norm_back(back * post_gain[...], normedp, factorp).astype(BF)
    grad_mixed[...] = low
    width = back.shape[1]
    fresh = stack_rows(
        [
            col_sum(grad * normed2),
            col_sum(grad),
            col_sum(back * normedp),
            col_sum(back),
            col_sum(low.astype(F32)),
        ],
        width,
    )
    grad_context = dot_nn(low, w_out[...])
    att = attended[...]
    fresh_head = stack_rows([col_sum(grad_context * att)], att.shape[1])
    low_att = (grad_context * scale[...]).astype(BF)
    grad_attended[...] = low_att
    product = low_att.astype(F32) * att
    delta[...] = columns_to_rows(
        [jnp.sum(product * mask, axis=-1, keepdims=True) for mask in head_masks(att.shape[1], F32)]
    )

    @pl.when(step == 0)
    def _():
        sums[...] = fresh
        head_sums[...] = fresh_head

    @pl.when(step != 0)
    def _():
        sums[...] += fresh
        head_sums[...] += fresh_head


def attend_back_kernel(first, block, last, *refs):
    q, k, v, segq, segk, grads, logsum, delta = refs[:8]
    rest = list(refs[8:])
    if not last:
        key_in, value_in = rest[:2]
        rest = rest[2:]
    grad_q, grad_k, grad_v, sums = rest[:4]
    rest = rest[4:]
    if first:
        key_out, value_out = rest[:2]
        rest = rest[2:]
    key_sum, value_sum, low_probs, low_scores = rest
    rows, width = q.shape
    end = first + rows
    masks = head_masks(width, BF)
    if last:
        key_sum[...] = jnp.zeros_like(key_sum)
        value_sum[...] = jnp.zeros_like(value_sum)
    else:
        key_sum[...] = key_in[...]
        value_sum[...] = value_in[...]
    (seg,) = rows_to_columns([segk[:, :end].astype(F32)])
    query_sum = jnp.zeros((1, width), F32)
    for at in range(0, rows, block):
        length = first + at + block
        query = q[at : at + block, :]
        grad = grads[at : at + block, :]
        place_k = lax.broadcasted_iota(jnp.int32, (length, block), 0)
        place_q = first + at + lax.broadcasted_iota(jnp.int32, (length, block), 1)
        allowed = (seg[:length] == segq[:, at : at + block].astype(F32)) & (place_k <= place_q)
        shift = jnp.where(allowed, 0.0, EXCLUDED)
        queries = [query * mask for mask in masks]
        grad_parts = [grad * mask for mask in masks]
        grad_query = jnp.zeros((block, width), F32)
        for head, mask in enumerate(masks):
            scores = dot_nt(k[:length, :], queries[head]) + shift
            probs = jnp.exp(scores - logsum[head : head + 1, at : at + block])
            low_probs[:length, head * block : (head + 1) * block] = probs.astype(BF)
            grad_probs = dot_nt(v[:length, :], grad_parts[head])
            low = (probs * (grad_probs - delta[head : head + 1, at : at + block])).astype(BF)
            low_scores[:length, head * block : (head + 1) * block] = low
            grad_query = grad_query + dot_tn(low, k[:length, :] * mask)
        value_sum[:length, :] += dot_nn(low_probs[:length, :], jnp.concatenate(grad_parts, axis=0))
        key_sum[:length, :] += dot_nn(low_scores[:length, :], jnp.concatenate(queries, axis=0))
        low_query = (grad_query * HEAD_DIM**-0.5).astype(BF)
        grad_q[at : at + block, :] = low_query
        query_sum = query_sum + col_sum(low_query.astype(F32))
    grad_k[...] = key_sum[first:end, :].astype(BF)
    low_value = value_sum[first:end, :].astype(BF)
    grad_v[...] = low_value
    sums[...] = stack_rows([query_sum, col_sum(low_value.astype(F32))], width)
    if first:
        key_out[...] = key_sum[:first, :]
        value_out[...] = value_sum[:first, :]


def entry_kernel(order, grad_q, grad_k, grad_v, wq, wk, wv, tok, send, keep, sums):
    step = pl.program_id(0)
    part = dot_nt(grad_q[...], wq[...]) + dot_nt(grad_k[...], wk[...]) + dot_nt(grad_v[...], wv[...])
    normed, _ = normalize(tok[...].astype(F32))
    fresh = stack_rows([col_sum(part * normed), col_sum(part)], part.shape[1])

    @pl.when(step == 0)
    def _():
        sums[...] = fresh
        send[...] = part

    @pl.when(step != 0)
    def _():
        sums[...] += fresh
        keep[...] = part


def token_kernel(order, mine, other, tok, grad_stream, gain, *refs):
    out = refs[-1]
    grad = jnp.where(pl.program_id(0) == 0, mine[...], other[...])
    normed, factor = normalize(tok[...].astype(F32))
    out[...] = grad_stream[...] + norm_back(grad * gain[...], normed, factor)


def output_kernel(order, mine, other, stream, bias, seg, *refs):
    out, sums = refs[-2:]
    step = pl.program_id(0)
    ffn = jnp.where(step == 0, mine[...], other[...]) + bias[...]
    result = stream[...] + ffn
    out[...] = result.astype(BF)
    (place,) = rows_to_columns([seg[...].astype(F32)])
    valid = (place >= 0).astype(F32)
    fresh = stack_rows([col_sum(valid * ffn * ffn), col_sum(valid * result * result)], ffn.shape[1])

    @pl.when(step == 0)
    def _():
        sums[...] = fresh

    @pl.when(step != 0)
    def _():
        sums[...] += fresh


def weight_kernel(count, parts, blocks, *refs):
    step = pl.program_id(0)
    lefts = refs[:count]
    rights = [refs[count + i * parts : count + (i + 1) * parts] for i in range(count)]
    send, keep = refs[-2:]
    depth = send.shape[0]

    def fill(target):
        offset = 0
        for part in range(parts):
            total = None
            for left, right in zip(lefts, rights):
                columns = jnp.concatenate(
                    [
                        left[:, pl.ds(pl.multiple_of(blocks[step * depth + j] * LANES, LANES), LANES)]
                        for j in range(depth)
                    ],
                    axis=1,
                )
                term = dot_tn(columns, right[part][...].astype(BF))
                total = term if total is None else total + term
            width = total.shape[1]
            target[:, :, offset : offset + width] = total.reshape(depth, LANES, width)
            offset += width

    @pl.when(step == 0)
    def _():
        fill(send)

    @pl.when(step != 0)
    def _():
        fill(keep)


def call(kernel, grid, ins, outs, prefetch=(), flops=0, scratch=(), aliases=None, vmem=48 << 20, name=None):
    arrays = [item[0] for item in ins]
    moved = sum(a.size * a.dtype.itemsize for a in arrays) + sum(
        functools.reduce(lambda x, y: x * y, shape, 1) * jnp.dtype(kind).itemsize for shape, kind, _, _ in outs
    )
    specs = [
        pl.BlockSpec(memory_space=pl.ANY) if block is None else pl.BlockSpec(block, place) for _, block, place in ins
    ]
    result = pl.pallas_call(
        kernel,
        grid_spec=pltpu.PrefetchScalarGridSpec(
            num_scalar_prefetch=len(prefetch),
            grid=grid,
            in_specs=specs,
            out_specs=[pl.BlockSpec(block, place) for _, _, block, place in outs],
            scratch_shapes=list(scratch),
        ),
        out_shape=[jax.ShapeDtypeStruct(shape, kind) for shape, kind, _, _ in outs],
        input_output_aliases=aliases or {},
        compiler_params=pltpu.CompilerParams(
            dimension_semantics=("arbitrary",) * len(grid), vmem_limit_bytes=vmem
        ),
        cost_estimate=pl.CostEstimate(flops=int(flops), bytes_accessed=int(moved), transcendentals=0),
        name=name,
    )(*prefetch, *arrays)
    return result


def whole(array):
    shape = array.shape
    return (array, shape, lambda *_: (0,) * len(shape))


def swap(value, axis, size, bit):
    return lax.ppermute(value, axis, [(i, i ^ bit) for i in range(size)])


def body(
    dp,
    tp,
    tokens,
    segments,
    w_query,
    w_key,
    w_value,
    w_out,
    w_fc1,
    w_fc2,
    ln1_gain,
    ln1_bias,
    post_gain,
    post_bias,
    ln2_gain,
    ln2_bias,
    mid_gain,
    mid_bias,
    query_bias,
    value_bias,
    out_bias,
    fc1_bias,
    fc2_bias,
    head_scale,
    cotangent,
):
    rows, width = tokens.shape
    hw = w_query.shape[1]
    units = w_fc1.shape[1]
    heads = hw // HEAD_DIM
    size = rows // CHUNKS
    half = size // 2
    block = min(256, size)
    row = lambda v: v.reshape(1, -1)
    seg = segments.reshape(1, rows)
    ln1_g, ln1_b, post_g, post_b = row(ln1_gain), row(ln1_bias), row(post_gain), row(post_bias)
    ln2_g, ln2_b, mid_g, mid_b = row(ln2_gain), row(ln2_bias), row(mid_gain), row(mid_bias)
    q_b, v_b, out_b, fc1_b, fc2_b = row(query_bias), row(value_bias), row(out_bias), row(fc1_bias), row(fc2_bias)
    scale = row(jnp.repeat(head_scale, HEAD_DIM))
    core = lax.axis_index("tensor") & 1
    pair = jnp.arange(2, dtype=jnp.int32)
    own_first = (core + pair) & 1
    own_last = (core + 1 + pair) & 1

    half_rows = width // 2
    side = lax.axis_index("dp") & 1
    wide = w_out.astype(F32)
    part = lax.dynamic_slice_in_dim(wide, side * half_rows, half_rows, 0)
    far_half = swap(part, "tensor", tp, 2)
    far_rest = swap(far_half, "dp", dp, 1)
    w_far = jnp.where(
        side == 0, jnp.concatenate([far_half, far_rest], 0), jnp.concatenate([far_rest, far_half], 0)
    )
    w_near = swap(wide, "tensor", tp, 1)
    w_diag = swap(w_far, "tensor", tp, 1)

    step = min(256, rows)
    entry, query, keys, values = call(
        qkv_kernel,
        (rows // step,),
        [(tokens, (step, width), lambda i: (i, 0))]
        + [whole(a) for a in (ln1_g, ln1_b, w_query, w_key, w_value, q_b, v_b)],
        [((rows, width), BF, (step, width), lambda i: (i, 0))]
        + [((rows, hw), BF, (step, hw), lambda i: (i, 0))] * 3,
        flops=6 * rows * width * hw,
        name="qkv",
    )

    at0 = lambda c: (lambda *_: (c, 0))
    at1 = lambda c: (lambda *_: (0, c))
    order = list(range(CHUNKS))[::-1]
    attended, context, logsum = {}, {}, {}
    for c in order:
        end = (c + 1) * size
        attended[c], context[c], logsum[c] = call(
            functools.partial(attend_kernel, c * size, block),
            (1,),
            [
                (query, (size, hw), at0(c)),
                (keys, (end, hw), at0(0)),
                (values, (end, hw), at0(0)),
                (seg, (1, size), at1(c)),
                (seg, (1, end), at1(0)),
                whole(scale),
            ],
            [((size, hw), F32, (size, hw), at0(0))] * 2 + [((8, size), F32, (8, size), at0(0))],
            flops=4 * size * end * hw * heads,
            name="attend",
        )

    mixed, stream, inner, hidden, grad_mid, stats, fsums = {}, {}, {}, {}, {}, {}, {}
    for c in order:
        near = swap(context[c], "tensor", tp, 1)
        far = swap(context[c], "tensor", tp, 2)
        diag = swap(far, "tensor", tp, 1)
        blk = min(256, size)
        n = size // blk
        sub = lambda shape: (shape, lambda i: (i, 0))
        chunk = lambda a, w: (a, (blk, w), lambda i, n=n, c=c: (c * n + i, 0))
        mixed[c], stream[c], inner[c], hidden[c], grad_mid[c], stats[c], fsums[c] = call(
            forward_kernel,
            (n,),
            [(seg, (1, blk), lambda i, n=n, c=c: (0, c * n + i))]
            + [(a, (blk, hw), lambda i: (i, 0)) for a in (context[c], near, far, diag)]
            + [whole(a) for a in (w_out, w_near, w_far, w_diag, out_b)]
            + [chunk(tokens, width)]
            + [whole(a) for a in (post_g, post_b, ln2_g, ln2_b, w_fc1, fc1_b)]
            + [chunk(cotangent, width)]
            + [whole(a) for a in (w_fc2, mid_g)],
            [((size, width), F32, (blk, width), lambda i: (i, 0))] * 2
            + [((size, width), BF, (blk, width), lambda i: (i, 0))]
            + [((size, units), F32, (blk, units), lambda i: (i, 0))] * 2
            + [((8, size), F32, (8, blk), lambda i: (0, i))]
            + [((8, width), F32, (8, width), lambda i: (0, 0))],
            flops=2 * size * width * (hw * tp + 2 * units),
            name="forward",
        )

    def tensor_sum(send, keep):
        total = keep + swap(send, "tensor", tp, 1)
        total = total + swap(total, "tensor", tp, 2)
        return total, swap(total, "tensor", tp, 1)

    middle, grad_hidden, ffn, grad_in, gsums = {}, {}, {}, {}, {}
    for c in order:
        near = swap(stats[c], "tensor", tp, 1)
        both = swap(jnp.concatenate([stats[c], near], 0), "tensor", tp, 2)
        by_half = lambda a, w: (a, (half, w), lambda i, o: (o[i], 0))
        stat = lambda a, r: (a, (8, half), lambda i, o, r=r: (r, o[i]))
        fixed = lambda w: ((half, w), F32, (half, w), lambda i, o: (0, 0))
        middle[c], grad_hidden[c], fs, fk, gs, gk, gsums[c] = call(
            functools.partial(middle_kernel, units * tp),
            (2,),
            [by_half(hidden[c], units), by_half(grad_mid[c], units)]
            + [stat(stats[c], 0), stat(near, 0), stat(both, 0), stat(both, 1)]
            + [whole(a) for a in (mid_g, mid_b, w_fc1, w_fc2)],
            [((size, units), BF, (half, units), lambda i, o: (o[i], 0))] * 2
            + [fixed(width)] * 4
            + [((8, units), F32, (8, units), lambda i, o: (0, 0))],
            prefetch=(own_last,),
            flops=4 * size * width * units,
            name="middle",
        )
        ffn[c] = (fs, fk)
        grad_in[c] = tensor_sum(gs, gk)

    grad_stream, grad_mixed, grad_q, grad_k, grad_v, grad_ent = {}, {}, {}, {}, {}, {}
    hsums, head_sums, qsums, esums = {}, {}, {}, {}
    carry = None
    for c in order:
        end = (c + 1) * size
        last = c == CHUNKS - 1
        by_half = lambda a, w: (a, (half, w), lambda i, o: (o[i], 0))
        chunk_half = lambda a, w: (a, (half, w), lambda i, o, c=c: (2 * c + o[i], 0))
        grad_stream[c], grad_mixed[c], grad_att, delta, hsums[c], head_sums[c] = call(
            stream_kernel,
            (2,),
            [whole(a) for a in grad_in[c]]
            + [by_half(mixed[c], width), by_half(stream[c], width), chunk_half(cotangent, width)]
            + [whole(a) for a in (ln2_g, post_g, w_out)]
            + [by_half(attended[c], hw), whole(scale)],
            [
                ((size, width), F32, (half, width), lambda i, o: (o[i], 0)),
                ((size, width), BF, (half, width), lambda i, o: (o[i], 0)),
                ((size, hw), BF, (half, hw), lambda i, o: (o[i], 0)),
                ((8, size), F32, (8, half), lambda i, o: (0, o[i])),
                ((8, width), F32, (8, width), lambda i, o: (0, 0)),
                ((8, hw), F32, (8, hw), lambda i, o: (0, 0)),
            ],
            prefetch=(own_first,),
            flops=2 * size * width * hw,
            name="stream",
        )
        results = call(
            functools.partial(attend_back_kernel, c * size, block, last),
            (1,),
            [
                (query, (size, hw), at0(c)),
                (keys, (end, hw), at0(0)),
                (values, (end, hw), at0(0)),
                (seg, (1, size), at1(c)),
                (seg, (1, end), at1(0)),
                whole(grad_att),
                whole(logsum[c]),
                whole(delta),
            ]
            + ([] if last else [whole(a) for a in carry]),
            [((size, hw), BF, (size, hw), at0(0))] * 3
            + [((8, hw), F32, (8, hw), at0(0))]
            + ([((c * size, hw), F32, (c * size, hw), at0(0))] * 2 if c else []),
            scratch=[pltpu.VMEM((end, hw), F32)] * 2 + [pltpu.VMEM((end, heads * block), BF)] * 2,
            flops=10 * size * end * hw * heads,
            name="attend_back",
        )
        grad_q[c], grad_k[c], grad_v[c], qsums[c] = results[:4]
        carry = results[4:]
        es, ek, esums[c] = call(
            entry_kernel,
            (2,),
            [by_half(a, hw) for a in (grad_q[c], grad_k[c], grad_v[c])]
            + [whole(a) for a in (w_query, w_key, w_value)]
            + [chunk_half(tokens, width)],
            [((half, width), F32, (half, width), lambda i, o: (0, 0))] * 2
            + [((8, width), F32, (8, width), lambda i, o: (0, 0))],
            prefetch=(own_last,),
            flops=6 * size * width * hw,
            name="entry",
        )
        grad_ent[c] = tensor_sum(es, ek)

    grad_tokens, output, osums = None, None, {}
    for c in order:
        by_half = lambda a, w: (a, (half, w), lambda i, o: (o[i], 0))
        chunk_half = lambda a, w: (a, (half, w), lambda i, o, c=c: (2 * c + o[i], 0))
        total = tensor_sum(*ffn[c])
        ins = (
            [whole(a) for a in total]
            + [by_half(stream[c], width), whole(fc2_b)]
            + [(seg, (1, half), lambda i, o, c=c: (0, 2 * c + o[i]))]
        )
        aliases = None
        if output is not None:
            aliases = {1 + len(ins): 0}
            ins = ins + [(output, None, None)]
        output, osums[c] = call(
            output_kernel,
            (2,),
            ins,
            [
                ((rows, width), BF, (half, width), lambda i, o, c=c: (2 * c + o[i], 0)),
                ((8, width), F32, (8, width), lambda i, o: (0, 0)),
            ],
            prefetch=(own_first,),
            aliases=aliases,
            name="output",
        )
    for c in order:
        by_half = lambda a, w: (a, (half, w), lambda i, o: (o[i], 0))
        chunk_half = lambda a, w: (a, (half, w), lambda i, o, c=c: (2 * c + o[i], 0))
        ins = (
            [whole(a) for a in grad_ent[c]]
            + [chunk_half(tokens, width), by_half(grad_stream[c], width), whole(ln1_g)]
        )
        aliases = None
        if grad_tokens is not None:
            aliases = {1 + len(ins): 0}
            ins = ins + [(grad_tokens, None, None)]
        (grad_tokens,) = call(
            token_kernel,
            (2,),
            ins,
            [((rows, width), F32, (half, width), lambda i, o, c=c: (2 * c + o[i], 0))],
            prefetch=(own_first,),
            aliases=aliases,
            name="token",
        )

    near_blocks = width // dp == LANES and dp % 2 == 0
    if near_blocks:
        depth = dp // 2
        me = lax.axis_index("dp")
        slot = jnp.arange(dp, dtype=jnp.int32)
        ring_at = (me // 2 - 1 - slot % depth) % depth
        blocks = (2 * ring_at + ((me + 1 + slot // depth) & 1)).astype(jnp.int32)

    def scattered(lefts, rights):
        if not near_blocks:
            left = jnp.concatenate(lefts, 0)
            return [
                lax.psum_scatter(
                    dot_tn(left, jnp.concatenate([r[p] for r in rights], 0).astype(BF)),
                    "dp",
                    scatter_dimension=0,
                    tiled=True,
                )
                for p in range(len(rights[0]))
            ]
        columns = sum(r.shape[1] for r in rights[0])
        send, keep = call(
            functools.partial(weight_kernel, len(lefts), len(rights[0])),
            (2,),
            [whole(a) for a in lefts] + [whole(a) for r in rights for a in r],
            [((depth, LANES, columns), F32, (depth, LANES, columns), lambda i, b: (0, 0, 0))] * 2,
            prefetch=(blocks,),
            flops=2 * rows * width * columns,
            name="weight",
        )
        got = swap(send, "dp", dp, 1)
        ring = [(i, (i + 2) % dp) for i in range(dp)]
        total = keep[0] + got[0]
        for j in range(1, depth):
            total = lax.ppermute(total, "dp", ring) + (keep[j] + got[j])
        cuts, offset = [], 0
        for r in rights[0]:
            cuts.append(total[:, offset : offset + r.shape[1]])
            offset += r.shape[1]
        return cuts

    chunks = range(CHUNKS)
    cot_rows = [cotangent]
    (grad_w_fc2,) = scattered(
        [lax.slice_in_dim(cotangent, c * size, (c + 1) * size, axis=0) for c in chunks], [[middle[c]] for c in chunks]
    )
    (grad_w_fc1,) = scattered([inner[c] for c in chunks], [[grad_hidden[c]] for c in chunks])
    (grad_w_out,) = scattered([grad_mixed[c] for c in chunks], [[context[c]] for c in chunks])
    grad_w_query, grad_w_key, grad_w_value = scattered(
        [lax.slice_in_dim(entry, c * size, (c + 1) * size, axis=0) for c in chunks],
        [[grad_q[c], grad_k[c], grad_v[c]] for c in chunks],
    )

    add = lambda parts: functools.reduce(lambda a, b: a + b, [parts[c] for c in chunks])
    fs, gs, hs, qs, es, os, hd = (add(p) for p in (fsums, gsums, hsums, qsums, esums, osums, head_sums))
    es = es + swap(es, "tensor", tp, 1)
    es = es + swap(es, "tensor", tp, 2)
    packed = jnp.concatenate(
        [hs, gs[:3], es[:2], fs[:3], os[:2], jnp.concatenate([qs[0], qs[1], hd[0], hd[0]]).reshape(1, -1)[:, :width]],
        0,
    )
    if dp & (dp - 1) == 0:
        bit = 1
        while bit < dp:
            packed = packed + swap(packed, "dp", dp, bit)
            bit *= 2
    else:
        packed = lax.psum(packed, "dp")
    tail = packed[18]
    counted = packed[15, 0]
    squares = jnp.stack([jnp.sum(packed[13]), jnp.sum(packed[16]), jnp.sum(packed[17])])
    rms = jnp.sqrt(squares / (counted * width))
    grad_head = jnp.sum(tail[2 * hw : 3 * hw].reshape(heads, HEAD_DIM), axis=1)
    return (
        output,
        grad_tokens,
        grad_w_query,
        grad_w_key,
        grad_w_value,
        grad_w_out,
        grad_w_fc1,
        grad_w_fc2,
        packed[11],
        packed[12],
        packed[2],
        packed[3],
        packed[0],
        packed[1],
        packed[8],
        packed[9],
        tail[:hw],
        tail[hw : 2 * hw],
        packed[4],
        packed[10],
        packed[14],
        grad_head,
        rms,
    )


def solution(mesh):
    cut = P(None, "tensor")
    part = P("tensor")
    rows = P("dp", None)
    both = P("dp", "tensor")
    return jax.shard_map(
        functools.partial(body, mesh.shape["dp"], mesh.shape["tensor"]),
        mesh=mesh,
        in_specs=(rows, rows) + (cut,) * 6 + (P(),) * 6 + (part,) * 4 + (P(), part, P(), part, rows),
        out_specs=(rows, rows) + (both,) * 6 + (P(),) * 6 + (part,) * 4 + (P(), part, P(), part, P()),
        check_vma=False,
    )
```

```python
import functools

import jax
import jax.numpy as jnp
from jax import lax
from jax.experimental import pallas as pl
from jax.experimental.pallas import tpu as pltpu
from jax.sharding import PartitionSpec as P

HEAD_DIM = 64
EPSILON = 1e-05
EXCLUDED = -1e30
LANES = 128
CHUNKS = 2
PAD = 16
BF = jnp.bfloat16
F32 = jnp.float32


def dot_nn(a, b):
    return lax.dot_general(a, b, (((1,), (0,)), ((), ())), preferred_element_type=F32)


def dot_nt(a, b):
    return lax.dot_general(a, b, (((1,), (1,)), ((), ())), preferred_element_type=F32)


def dot_tn(a, b):
    return lax.dot_general(a, b, (((0,), (0,)), ((), ())), preferred_element_type=F32)


def normalize(v):
    mean = jnp.mean(v, axis=-1, keepdims=True)
    centred = v - mean
    factor = lax.rsqrt(jnp.mean(centred * centred, axis=-1, keepdims=True) + EPSILON)
    return centred * factor, factor


def norm_back(scaled, normed, factor):
    return factor * (
        scaled
        - jnp.mean(scaled, axis=-1, keepdims=True)
        - normed * jnp.mean(scaled * normed, axis=-1, keepdims=True)
    )


def col_sum(v):
    return jnp.sum(v, axis=0, keepdims=True)


def tanh_inner(v):
    return 0.7978845608028654 * (v + 0.044715 * (v * v * v))


def columns_to_rows(columns):
    n = columns[0].shape[0]
    lane = lax.broadcasted_iota(jnp.int32, (n, LANES), 1)
    tile = jnp.zeros((n, LANES), F32)
    for index, column in enumerate(columns):
        tile = jnp.where(lane == index, column, tile)
    return jnp.transpose(tile)[:8]


def rows_to_columns(rows):
    n = rows[0].shape[1]
    sub = lax.broadcasted_iota(jnp.int32, (LANES, n), 0)
    tile = jnp.zeros((LANES, n), F32)
    for index, row in enumerate(rows):
        tile = jnp.where(sub == index, row, tile)
    tile = jnp.transpose(tile)
    return [tile[:, index : index + 1] for index in range(len(rows))]


def stack_rows(rows, width):
    sub = lax.broadcasted_iota(jnp.int32, (8, width), 0)
    tile = jnp.zeros((8, width), F32)
    for index, row in enumerate(rows):
        tile = jnp.where(sub == index, row, tile)
    return tile


def head_masks(width, kind):
    lane = lax.broadcasted_iota(jnp.int32, (1, width), 1) // HEAD_DIM
    return [(lane == head).astype(F32).astype(kind) for head in range(width // HEAD_DIM)]


def qkv_kernel(tok, gain, bias, wq, wk, wv, qb, vb, entry, q, k, v):
    normed, _ = normalize(tok[...].astype(F32))
    low = (normed * gain[...] + bias[...]).astype(BF)
    entry[...] = low
    q[...] = ((dot_nn(low, wq[...]) + qb[...]) * HEAD_DIM**-0.5).astype(BF)
    k[...] = dot_nn(low, wk[...]).astype(BF)
    v[...] = (dot_nn(low, wv[...]) + vb[...]).astype(BF)


def attend_kernel(first, block, place, q, k, v, segq, segk, scale, attended, low, mine, theirs, logsum, hold):
    rows, width = q.shape
    half = rows // 2
    masks = head_masks(width, BF)
    for at in range(0, rows, block):
        length = first + at + block
        query = q[at : at + block, :]
        keys = k[:length, :]
        (seg,) = rows_to_columns([segq[:, at : at + block].astype(F32)])
        place_q = first + at + lax.broadcasted_iota(jnp.int32, (block, length), 0)
        place_k = lax.broadcasted_iota(jnp.int32, (block, length), 1)
        allowed = (seg == segk[:, :length].astype(F32)) & (place_k <= place_q)
        shift = jnp.where(allowed, 0.0, EXCLUDED)
        total = jnp.zeros((block, width), F32)
        sums = []
        for mask in masks:
            scores = dot_nt(query * mask, keys) + shift
            top = jnp.max(scores, axis=-1, keepdims=True)
            expo = jnp.exp(scores - top)
            norm = jnp.sum(expo, axis=-1, keepdims=True)
            weights = (expo * (1.0 / norm)).astype(BF)
            total = total + dot_nn(weights, v[:length, :] * mask)
            sums.append(top + jnp.log(norm))
        attended[at : at + block, :] = total
        context = (total * scale[...]).astype(BF)
        low[at : at + block, :] = context
        hold[at : at + block, :] = context.astype(F32)
        logsum[:, at : at + block] = columns_to_rows(sums)
    mine[...] = hold[pl.ds(pl.multiple_of(place[0] * half, half), half), :]
    theirs[...] = hold[pl.ds(pl.multiple_of(place[1] * half, half), half), :]


def pack_kernel(wide, near_out, out_pair, fc1, fc2):
    width, units = near_out.shape[1], fc1.shape[1]
    out_pair[:, :width] = near_out[...]
    out_pair[:, width:] = wide[:, :width].astype(BF)
    fc1[...] = wide[:, width : width + units].astype(BF)
    fc2[...] = wide[:, width + units :].astype(BF)


def far_kernel(side, far_half, far_rest, diag_half, diag_rest, out):
    rows, width = far_half.shape
    here = pl.ds(pl.multiple_of(side[0] * rows, rows), rows)
    there = pl.ds(pl.multiple_of((1 - side[0]) * rows, rows), rows)
    out[here, :width] = far_half[...].astype(BF)
    out[there, :width] = far_rest[...].astype(BF)
    out[here, width:] = diag_half[...].astype(BF)
    out[there, width:] = diag_rest[...].astype(BF)


def upstream_kernel(place, cot, own, near, out):
    units = own.shape[1]
    out[:, :units] = dot_nn(cot[...], own[...])
    out[:, units:] = dot_nn(cot[...], near[...])


def forward_kernel(
    place, seg, ctx_chip, ctx_far, wo_chip, wo_far, out_bias, tok, post_gain, post_bias, ln2_gain, ln2_bias,
    fc1_own, fc1_near, fc1_bias, mid_gain, near, cot, grad_middle,
    mixed, stream, inner, share, hidden, stats, sums,
):
    units = fc1_own.shape[1]
    mix = (
        dot_nt(ctx_chip[...].astype(BF), wo_chip[...]) + dot_nt(ctx_far[...].astype(BF), wo_far[...])
    ) + out_bias[...]
    mixed[...] = mix
    normed, _ = normalize(mix)
    branch = normed * post_gain[...] + post_bias[...]
    resid = tok[...].astype(F32) + branch
    stream[...] = resid
    normed2, _ = normalize(resid)
    low = (normed2 * ln2_gain[...] + ln2_bias[...]).astype(BF)
    inner[...] = low
    share[...] = low.astype(F32)
    actives, scaleds = [], []
    for part, (weight, bias, gain) in enumerate(
        ((fc1_own, fc1_bias[...], mid_gain[...]), (fc1_near, near[0:1, :], near[1:2, :]))
    ):
        hid = dot_nn(low, weight[...]) + bias
        hidden[:, part * units : (part + 1) * units] = hid
        actives.append(0.5 * hid * (1.0 + jnp.tanh(tanh_inner(hid))))
        scaleds.append(grad_middle[:, part * units : (part + 1) * units] * gain)

    def both(left, right):
        return jnp.sum(left, axis=-1, keepdims=True) + jnp.sum(right, axis=-1, keepdims=True)

    mean = both(*actives) / (2 * units)
    centred = [active - mean for active in actives]
    stats[...] = columns_to_rows(
        [
            mean,
            both(*[c * c for c in centred]),
            both(*scaleds),
            both(*[s * c for s, c in zip(scaleds, centred)]),
        ]
    )
    (which,) = rows_to_columns([seg[...].astype(F32)])
    valid = (which >= 0).astype(F32)
    sums[...] = stack_rows(
        [
            col_sum(valid * branch * branch),
            col_sum(cot[...].astype(F32)),
            col_sum(valid * jnp.ones_like(branch)),
        ],
        branch.shape[1],
    )


def middle_kernel(
    total, hidden, grad_middle, st0, st1, mid_gain, mid_bias, near,
    fc1_own, fc1_near, fc2_own, fc2_near,
    middle, grad_hidden, share_mid, share_hid, ffn, back, sums_own, sums_near,
):
    units = fc1_own.shape[1]
    n = 2 * units
    mean = (st0[0:1, :] + st1[0:1, :]) * 0.5
    apart = [s[0:1, :] - mean for s in (st0, st1)]
    spread = (st0[1:2, :] + n * (apart[0] * apart[0])) + (st1[1:2, :] + n * (apart[1] * apart[1]))
    factor = lax.rsqrt(spread / total + EPSILON)
    plain = (st0[2:3, :] + st1[2:3, :]) / total
    along = (st0[3:4, :] + apart[0] * st0[2:3, :]) + (st1[3:4, :] + apart[1] * st1[2:3, :])
    mean, factor, plain, along = rows_to_columns([mean, factor, plain, factor * along / total])
    parts = (
        (mid_gain[...], mid_bias[...], fc1_own, fc2_own, sums_own),
        (near[1:2, :], near[2:3, :], fc1_near, fc2_near, sums_near),
    )
    ffn_parts, back_parts = [], []
    for part, (gain, bias, fc1, fc2, sums) in enumerate(parts):
        hid = hidden[:, part * units : (part + 1) * units]
        bend = jnp.tanh(tanh_inner(hid))
        active = 0.5 * hid * (1.0 + bend)
        slope = 0.5 * (1.0 + bend) + 0.5 * hid * (1.0 - bend * bend) * (
            0.7978845608028654 * (1.0 + 3 * 0.044715 * (hid * hid))
        )
        normed = (active - mean) * factor
        mid = (normed * gain + bias).astype(BF)
        grad = grad_middle[:, part * units : (part + 1) * units]
        low = (factor * (grad * gain - plain - normed * along) * slope).astype(BF)
        if part == 0:
            middle[...] = mid
            grad_hidden[...] = low
        else:
            share_mid[...] = mid.astype(F32)
            share_hid[...] = low.astype(F32)
        sums[...] = stack_rows([col_sum(grad * normed), col_sum(grad), col_sum(low.astype(F32))], units)
        ffn_parts.append(dot_nt(mid, fc2[...]))
        back_parts.append(dot_nt(low, fc1[...]))
    ffn[...] = ffn_parts[0] + ffn_parts[1]
    back[: hidden.shape[0], :] = back_parts[0] + back_parts[1]
    back[hidden.shape[0] :, :] = jnp.zeros((PAD, back.shape[1]), F32)


def stream_kernel(
    place, mine, far, mixed, stream, cot, ln2_gain, post_gain, w_out,
    grad_stream, grad_mixed, wide, context_own, context_near, sums,
):
    grad = mine[: stream.shape[0], :] + far[: stream.shape[0], :]
    normed2, factor2 = normalize(stream[...])
    back = cot[...].astype(F32) + norm_back(grad * ln2_gain[...], normed2, factor2)
    grad_stream[...] = back
    normedp, factorp = normalize(mixed[...])
    low = norm_back(back * post_gain[...], normedp, factorp).astype(BF)
    grad_mixed[...] = low
    wide[...] = low.astype(F32)
    context = dot_nn(low, w_out[...])
    width = context_own.shape[1]
    context_own[...] = context[:, :width]
    context_near[...] = context[:, width:]
    sums[...] = stack_rows(
        [
            col_sum(grad * normed2),
            col_sum(grad),
            col_sum(back * normedp),
            col_sum(back),
            col_sum(low.astype(F32)),
        ],
        back.shape[1],
    )


def attend_back_kernel(first, block, last, place, *refs):
    q, k, v, segq, segk, context_own, context_near, attended, scale, logsum = refs[:10]
    rest = list(refs[10:])
    if not last:
        key_in, value_in = rest[:2]
        rest = rest[2:]
    grad_q, grad_k, grad_v, sums = rest[:4]
    rest = rest[4:]
    if first:
        key_out, value_out = rest[:2]
        rest = rest[2:]
    key_sum, value_sum, low_probs, low_scores, grads = rest
    rows, width = q.shape
    half = rows // 2
    end = first + rows
    masks = head_masks(width, BF)
    wide_masks = head_masks(width, F32)
    if last:
        key_sum[...] = jnp.zeros_like(key_sum)
        value_sum[...] = jnp.zeros_like(value_sum)
    else:
        key_sum[...] = key_in[...]
        value_sum[...] = value_in[...]
    head_sum = jnp.zeros((1, width), F32)
    for part, source in enumerate((context_own, context_near)):
        at = pl.ds(pl.multiple_of(place[part] * half, half), half)
        grad_context = source[...]
        head_sum = head_sum + col_sum(grad_context * attended[at, :])
        grads[at, :] = (grad_context * scale[...]).astype(BF)
    (seg,) = rows_to_columns([segk[:, :end].astype(F32)])
    query_sum = jnp.zeros((1, width), F32)
    for at in range(0, rows, block):
        length = first + at + block
        query = q[at : at + block, :]
        grad = grads[at : at + block, :]
        product = grad.astype(F32) * attended[at : at + block, :]
        delta = columns_to_rows([jnp.sum(product * mask, axis=-1, keepdims=True) for mask in wide_masks])
        place_k = lax.broadcasted_iota(jnp.int32, (length, block), 0)
        place_q = first + at + lax.broadcasted_iota(jnp.int32, (length, block), 1)
        allowed = (seg[:length] == segq[:, at : at + block].astype(F32)) & (place_k <= place_q)
        shift = jnp.where(allowed, 0.0, EXCLUDED)
        queries = [query * mask for mask in masks]
        grad_parts = [grad * mask for mask in masks]
        grad_query = jnp.zeros((block, width), F32)
        for head, mask in enumerate(masks):
            scores = dot_nt(k[:length, :], queries[head]) + shift
            probs = jnp.exp(scores - logsum[head : head + 1, at : at + block])
            low_probs[:length, head * block : (head + 1) * block] = probs.astype(BF)
            grad_probs = dot_nt(v[:length, :], grad_parts[head])
            low = (probs * (grad_probs - delta[head : head + 1, :])).astype(BF)
            low_scores[:length, head * block : (head + 1) * block] = low
            grad_query = grad_query + dot_tn(low, k[:length, :] * mask)
        value_sum[:length, :] += dot_nn(low_probs[:length, :], jnp.concatenate(grad_parts, axis=0))
        key_sum[:length, :] += dot_nn(low_scores[:length, :], jnp.concatenate(queries, axis=0))
        low_query = (grad_query * HEAD_DIM**-0.5).astype(BF)
        grad_q[at : at + block, :] = low_query
        query_sum = query_sum + col_sum(low_query.astype(F32))
    grad_k[...] = key_sum[first:end, :].astype(BF)
    low_value = value_sum[first:end, :].astype(BF)
    grad_v[...] = low_value
    sums[...] = stack_rows([query_sum, col_sum(low_value.astype(F32)), head_sum], width)
    if first:
        key_out[...] = key_sum[:first, :]
        value_out[...] = value_sum[:first, :]


def entry_kernel(place, grad_q, grad_k, grad_v, wq, wk, wv, tok, send0, send1, keep, sums):
    step = pl.program_id(0)
    part = dot_nt(grad_q[...], wq[...]) + dot_nt(grad_k[...], wk[...]) + dot_nt(grad_v[...], wv[...])
    normed, _ = normalize(tok[...].astype(F32))
    fresh = stack_rows([col_sum(part * normed), col_sum(part)], part.shape[1])

    @pl.when(step == 0)
    def _():
        sums[...] = fresh
        cut = send0.shape[1]
        send0[...] = part[:, :cut]
        send1[...] = part[:, cut:]

    @pl.when(step != 0)
    def _():
        sums[...] += fresh
        keep[...] = part


def chip_kernel(keep, got0, got1, out):
    cut = got0.shape[1]
    out[:, :cut] = keep[:, :cut] + got0[...]
    out[:, cut:] = keep[:, cut:] + got1[...]


def token_kernel(place, mine, far, tok, grad_stream, gain, *refs):
    out, wide = refs[-2:]
    normed, factor = normalize(tok[...].astype(F32))
    grad = grad_stream[...] + norm_back((mine[...] + far[...]) * gain[...], normed, factor)
    out[...] = grad
    wide[...] = grad


def output_kernel(place, mine, far, stream, bias, seg, *refs):
    out, wide, sums = refs[-3:]
    ffn = (mine[...] + far[...]) + bias[...]
    result = stream[...] + ffn
    low = result.astype(BF)
    out[...] = low
    wide[...] = low.astype(F32)
    (which,) = rows_to_columns([seg[...].astype(F32)])
    valid = (which >= 0).astype(F32)
    sums[...] = stack_rows([col_sum(valid * ffn * ffn), col_sum(valid * result * result)], ffn.shape[1])


def put_kernel(place, value, full, out):
    out[...] = value[...].astype(out.dtype)


def line_kernel(kind, chunks, half, place, *refs):
    items, out = refs[:-1], refs[-1]
    for c in range(chunks):
        if kind == "chunks":
            out[2 * c * half : 2 * (c + 1) * half, :] = items[c][...]
        else:
            for part in range(2):
                at = pl.ds(pl.multiple_of((2 * c + place[part]) * half, half), half)
                out[at, :] = items[2 * c + part][...].astype(BF)


def weight_kernel(plan, chunks, half, blocks, place, *refs):
    step = pl.program_id(0)
    refs = list(refs)
    count = {"all": 1, "halves": 2 * chunks, "chunks": chunks}
    sources = [[(kind, [refs.pop(0) for _ in range(count[kind])]) for kind in product] for product in plan]
    send, keep = refs[:2]
    holds = refs[2:]
    depth = send.shape[0]
    operands, fills = [], []
    for product in sources:
        row = []
        for kind, items in product:
            if kind == "all":
                row.append(items[0])
            else:
                hold = holds.pop(0)
                fills.append((kind, items, hold))
                row.append(hold)
        operands.append(row)

    @pl.when(step == 0)
    def _():
        for kind, items, hold in fills:
            line_kernel(kind, chunks, half, place, *items, hold)

    def fill(target):
        offset = 0
        for row in operands:
            left = row[0]
            columns = jnp.concatenate(
                [
                    left[:, pl.ds(pl.multiple_of(blocks[step * depth + j] * LANES, LANES), LANES)]
                    for j in range(depth)
                ],
                axis=1,
            )
            for right in row[1:]:
                total = dot_tn(columns, right[...])
                width = total.shape[1]
                target[:, :, offset : offset + width] = total.reshape(depth, LANES, width)
                offset += width

    @pl.when(step == 0)
    def _():
        fill(send)

    @pl.when(step != 0)
    def _():
        fill(keep)


def pair_kernel(keep, got, *outs):
    for j, out in enumerate(outs):
        out[...] = keep[j] + got[j]


def whole(array):
    shape = array.shape
    return (array, shape, lambda *_: (0,) * len(shape))


def swap(value, axis, size, bit):
    return lax.ppermute(value, axis, [(i, i ^ bit) for i in range(size)])


class Order:
    def __init__(self):
        self.last = None

    def after(self, value):
        if self.last is None:
            return value
        return lax.optimization_barrier((value, self.last))[0]

    def keep(self, value):
        self.last = value
        return value

    def call(self, kernel, grid, ins, outs, prefetch=(), scratch=(), aliases=None, vmem=32 << 20, name=None):
        arrays = [item[0] for item in ins]
        specs = [
            pl.BlockSpec(memory_space=pl.ANY) if block is None else pl.BlockSpec(block, place)
            for _, block, place in ins
        ]
        body_of = kernel
        if self.last is not None:
            at = len(prefetch) + len(arrays)
            arrays.append(self.last)
            specs.append(pl.BlockSpec(memory_space=pl.ANY))

            def body_of(*refs):
                return kernel(*refs[:at], *refs[at + 1 :])

        results = pl.pallas_call(
            body_of,
            grid_spec=pltpu.PrefetchScalarGridSpec(
                num_scalar_prefetch=len(prefetch),
                grid=grid,
                in_specs=specs,
                out_specs=[pl.BlockSpec(block, place) for _, _, block, place in outs],
                scratch_shapes=list(scratch),
            ),
            out_shape=[jax.ShapeDtypeStruct(shape, kind) for shape, kind, _, _ in outs],
            input_output_aliases=aliases or {},
            compiler_params=pltpu.CompilerParams(
                dimension_semantics=("arbitrary",) * len(grid), vmem_limit_bytes=vmem
            ),
            cost_estimate=pl.CostEstimate(flops=1000, bytes_accessed=1000, transcendentals=0),
            name=name,
        )(*prefetch, *arrays)
        self.last = min(results, key=lambda r: r.size)
        return results


def body(
    dp, tp, tokens, segments, w_query, w_key, w_value, w_out, w_fc1, w_fc2, ln1_gain, ln1_bias, post_gain, post_bias,
    ln2_gain, ln2_bias, mid_gain, mid_bias, query_bias, value_bias, out_bias, fc1_bias, fc2_bias, head_scale, cotangent,
):
    rows, width = tokens.shape
    hw = w_query.shape[1]
    units = w_fc1.shape[1]
    heads = hw // HEAD_DIM
    size = rows // CHUNKS
    half = size // 2
    block = min(256, size)
    line = Order()
    call = line.call
    row = lambda v: v.reshape(1, -1)
    seg = segments.reshape(1, rows)
    ln1_g, ln1_b, post_g, post_b = row(ln1_gain), row(ln1_bias), row(post_gain), row(post_bias)
    ln2_g, ln2_b, mid_g, mid_b = row(ln2_gain), row(ln2_bias), row(mid_gain), row(mid_bias)
    q_b, v_b, out_b, fc1_b, fc2_b = row(query_bias), row(value_bias), row(out_bias), row(fc1_bias), row(fc2_bias)
    scale = row(jnp.repeat(head_scale, HEAD_DIM))
    core = lax.axis_index("tensor") & 1
    place = (core + jnp.arange(2, dtype=jnp.int32)) & 1
    dp_side = lax.axis_index("dp") & 1
    side = dp_side.astype(jnp.int32).reshape(1)
    chunks = list(range(CHUNKS))
    order = chunks[::-1]

    half_rows = width // 2
    part = lax.dynamic_slice_in_dim(w_out, dp_side * half_rows, half_rows, 0).astype(F32)
    far_half = swap(part, "tensor", tp, 2)
    wide = swap(jnp.concatenate([w_out, w_fc1, w_fc2], 1).astype(F32), "tensor", tp, 1)
    pad = jnp.zeros((5, units), F32)
    near = swap(jnp.concatenate([fc1_b, mid_g, mid_b, pad], 0), "tensor", tp, 1)

    step = min(256, rows)
    entry, query, keys, values = call(
        qkv_kernel,
        (rows // step,),
        [(tokens, (step, width), lambda i: (i, 0))]
        + [whole(a) for a in (ln1_g, ln1_b, w_query, w_key, w_value, q_b, v_b)],
        [((rows, width), BF, (step, width), lambda i: (i, 0))]
        + [((rows, hw), BF, (step, hw), lambda i: (i, 0))] * 3,
        name="qkv",
    )

    at0 = lambda c: (lambda *_: (c, 0))
    at1 = lambda c: (lambda *_: (0, c))
    fix = lambda shape, kind: (shape, kind, shape, lambda *_: (0,) * len(shape))
    own = lambda a, c: (a, (half, a.shape[1]), lambda i, p, c=c: (2 * c + p[0], 0))
    own_seg = lambda c: (seg, (1, half), lambda i, p, c=c: (0, 2 * c + p[0]))

    attended, low_ctx, ctx, logsum = {}, {}, {}, {}
    for c in order:
        end = (c + 1) * size
        attended[c], low_ctx[c], mine, theirs, logsum[c] = call(
            functools.partial(attend_kernel, c * size, block),
            (1,),
            [
                (query, (size, hw), at0(c)),
                (keys, (end, hw), at0(0)),
                (values, (end, hw), at0(0)),
                (seg, (1, size), at1(c)),
                (seg, (1, end), at1(0)),
                whole(scale),
            ],
            [fix((size, hw), F32), fix((size, hw), BF), fix((half, hw), F32), fix((half, hw), F32), fix((8, size), F32)],
            prefetch=(place,),
            scratch=[pltpu.VMEM((size, hw), F32)],
            name="attend",
        )
        ctx[c] = (mine, swap(theirs, "tensor", tp, 1))
    far_ctx = {}
    for c in order:
        mine, got = ctx[c]
        ctx[c] = line.keep(jnp.concatenate([line.after(mine), got], 1))
        far_ctx[c] = swap(ctx[c], "tensor", tp, 2)
    far_rest = swap(line.after(far_half), "dp", dp, 1)

    step = min(256, width)
    wo_chip, fc1_near, fc2_near = call(
        pack_kernel,
        (width // step,),
        [(a, (step, a.shape[1]), lambda i: (i, 0)) for a in (wide, w_out)],
        [((width, n), BF, (step, n), lambda i: (i, 0)) for n in (2 * hw, units, units)],
        name="pack",
    )
    diag_half = swap(far_half, "tensor", tp, 1)
    diag_rest = swap(far_rest, "tensor", tp, 1)
    (grad_mid,) = call(
        upstream_kernel,
        (CHUNKS,),
        [(cotangent, (half, width), lambda i, p: (2 * i + p[0], 0)), whole(w_fc2), whole(fc2_near)],
        [((CHUNKS * half, 2 * units), F32, (half, 2 * units), lambda i, p: (i, 0))],
        prefetch=(place,),
        name="upstream",
    )
    (wo_far,) = call(
        far_kernel,
        (1,),
        [whole(a) for a in (far_half, far_rest, diag_half, diag_rest)],
        [fix((width, 2 * hw), BF)],
        prefetch=(side,),
        name="far",
    )

    mixed, stream, inner, hidden, stats, far_stats, fsums, near_inner = {}, {}, {}, {}, {}, {}, {}, {}
    for c in order:
        mixed[c], stream[c], inner[c], share, hidden[c], stats[c], fsums[c] = call(
            forward_kernel,
            (1,),
            [own_seg(c)]
            + [whole(a) for a in (ctx[c], far_ctx[c], wo_chip, wo_far, out_b)]
            + [own(tokens, c)]
            + [whole(a) for a in (post_g, post_b, ln2_g, ln2_b, w_fc1, fc1_near, fc1_b, mid_g, near)]
            + [own(cotangent, c), (grad_mid, (half, 2 * units), at0(c))],
            [fix((half, width), F32)] * 2
            + [fix((half, width), BF), fix((half, width), F32), fix((half, 2 * units), F32)]
            + [fix((8, half), F32), fix((8, width), F32)],
            prefetch=(place,),
            name="forward",
        )
        far_stats[c] = swap(stats[c], "tensor", tp, 2)
        near_inner[c] = swap(share, "tensor", tp, 1)

    middle, grad_hid, ffn, back, far_back, gsums, nsums = {}, {}, {}, {}, {}, {}, {}
    near_mid, near_hid = {}, {}
    for c in order:
        mid, hid, share_m, share_h, ffn[c], back[c], gsums[c], nsums[c] = call(
            functools.partial(middle_kernel, units * tp),
            (1,),
            [whole(hidden[c]), (grad_mid, (half, 2 * units), at0(c))]
            + [whole(a) for a in (stats[c], far_stats[c], mid_g, mid_b, near)]
            + [whole(a) for a in (w_fc1, fc1_near, w_fc2, fc2_near)],
            [fix((half, units), BF)] * 2
            + [fix((half, units), F32)] * 2
            + [fix((half, width), F32), fix((half + PAD, width), F32)]
            + [fix((8, units), F32)] * 2,
            name="middle",
        )
        middle[c], grad_hid[c] = mid, hid
        far_back[c] = swap(back[c], "tensor", tp, 2)
        near_mid[c], near_hid[c] = swap(share_m, "tensor", tp, 1), swap(share_h, "tensor", tp, 1)

    near_blocks = width // dp == LANES and dp % 2 == 0
    if near_blocks:
        depth = dp // 2
        me = lax.axis_index("dp")
        slot = jnp.arange(dp, dtype=jnp.int32)
        at_ring = (me // 2 + 1 + slot % depth) % depth
        blocks = (2 * at_ring + ((me + 1 + slot // depth) & 1)).astype(jnp.int32)

    def weight(plan, items, columns, name):
        arrays = [item for group in items for operand in group for item in operand]
        kinds = [kind for product in plan for kind in product]
        holds = [
            pltpu.VMEM((rows, operand[0][1][1]), BF)
            for kind, operand in zip(kinds, [o for g in items for o in g])
            if kind != "all"
        ]
        if not near_blocks:
            results = []
            for product, group in zip(plan, items):
                full = []
                for kind, operand in zip(product, group):
                    if kind == "all":
                        full.append(operand[0][0])
                        continue
                    n = operand[0][1][1]
                    (lined,) = call(
                        functools.partial(line_kernel, kind, CHUNKS, half),
                        (1,),
                        operand,
                        [fix((rows, n), BF)],
                        prefetch=(place,),
                        name=name,
                    )
                    full.append(lined)
                results += [
                    lax.psum_scatter(dot_tn(full[0], right), "dp", scatter_dimension=0, tiled=True)
                    for right in full[1:]
                ]
            return lambda: results
        send, keep = call(
            functools.partial(weight_kernel, plan, CHUNKS, half),
            (2,),
            arrays,
            [fix((depth, LANES, columns), F32)] * 2,
            prefetch=(blocks, place),
            scratch=holds,
            name=name,
        )
        got = swap(send, "dp", dp, 1)

        def reduce_pair():
            lanes = min(256, columns)
            firsts = call(
                pair_kernel,
                (columns // lanes,),
                [(a, (depth - 1, LANES, lanes), lambda i: (0, 0, i)) for a in (keep, got)],
                [((LANES, columns), F32, (LANES, lanes), lambda i: (0, i))] * (depth - 1),
                name="pair",
            )
            return [
                lax.ppermute(first, "dp", [(i, (i + 2 * (j + 1)) % dp) for i in range(dp)])
                for j, first in enumerate(firsts)
            ]

        def finish(parts):
            total = line.after(keep)[depth - 1] + got[depth - 1]
            for part in parts:
                total = total + part
            line.keep(total)
            cuts, offset = [], 0
            for group in items:
                for operand in group[1:]:
                    cuts.append(total[:, offset : offset + operand[0][1][1]])
                    offset += operand[0][1][1]
            return cuts

        return reduce_pair, finish

    halves = lambda mine, wide_near: [item for c in chunks for item in (whole(mine[c]), wide_near[c])]
    fc2_sum = weight(
        [("all", "halves")],
        [[[whole(cotangent)], halves(middle, {c: whole(near_mid[c]) for c in chunks})]],
        units,
        "weight_fc2",
    )
    fc1_sum = weight(
        [("halves", "halves")],
        [
            [
                halves(inner, {c: whole(near_inner[c]) for c in chunks}),
                halves(grad_hid, {c: whole(near_hid[c]) for c in chunks}),
            ]
        ],
        units,
        "weight_fc1",
    )

    grad_stream, grad_mix, near_mix, grad_q, grad_k, grad_v, chip, far_chip = {}, {}, {}, {}, {}, {}, {}, {}
    hsums, qsums, esums, far_ffn = {}, {}, {}, {}
    carry = None
    fc2_parts = fc1_parts = None
    for c in order:
        end = (c + 1) * size
        last = c == CHUNKS - 1
        by_half = lambda a: (a, (half, a.shape[1]), lambda i, p: (p[1 - i], 0))
        grad_stream[c], grad_mix[c], wide_mix, ctx_own, ctx_near, hsums[c] = call(
            stream_kernel,
            (1,),
            [whole(a) for a in (back[c], far_back[c], mixed[c], stream[c])]
            + [own(cotangent, c), whole(ln2_g), whole(post_g), whole(wo_chip)],
            [fix((half, width), F32), fix((half, width), BF), fix((half, width), F32)]
            + [fix((half, hw), F32)] * 2
            + [fix((8, width), F32)],
            prefetch=(place,),
            name="stream",
        )
        ctx_near = swap(ctx_near, "tensor", tp, 1)
        near_mix[c] = swap(wide_mix, "tensor", tp, 1)
        results = call(
            functools.partial(attend_back_kernel, c * size, block, last),
            (1,),
            [
                (query, (size, hw), at0(c)),
                (keys, (end, hw), at0(0)),
                (values, (end, hw), at0(0)),
                (seg, (1, size), at1(c)),
                (seg, (1, end), at1(0)),
            ]
            + [whole(a) for a in (ctx_own, ctx_near, attended[c], scale, logsum[c])]
            + ([] if last else [whole(a) for a in carry]),
            [fix((size, hw), BF)] * 3 + [fix((8, hw), F32)] + ([fix((c * size, hw), F32)] * 2 if c else []),
            prefetch=(place,),
            scratch=[pltpu.VMEM((end, hw), F32)] * 2
            + [pltpu.VMEM((end, heads * block), BF)] * 2
            + [pltpu.VMEM((size, hw), BF)],
            name="attend_back",
        )
        grad_q[c], grad_k[c], grad_v[c], qsums[c] = results[:4]
        carry = results[4:]
        if c == order[-1] and near_blocks:
            fc2_parts = fc2_sum[0]()
        send0, send1, keep, esums[c] = call(
            entry_kernel,
            (2,),
            [by_half(a) for a in (grad_q[c], grad_k[c], grad_v[c])]
            + [whole(a) for a in (w_query, w_key, w_value)]
            + [(tokens, (half, width), lambda i, p, c=c: (2 * c + p[1 - i], 0))],
            [fix((half, width // 2), F32)] * 2 + [fix((half, width), F32), fix((8, width), F32)],
            prefetch=(place,),
            name="entry",
        )
        got = [swap(send, "tensor", tp, 1) for send in (send0, send1)]
        if c == order[-1]:
            for d in order:
                far_ffn[d] = swap(line.after(ffn[d]), "tensor", tp, 2)
        (chip[c],) = call(
            chip_kernel,
            (1,),
            [whole(a) for a in (keep, *got)],
            [fix((half, width), F32)],
            name="chip",
        )
        far_chip[c] = swap(chip[c], "tensor", tp, 2)

    own_out = lambda kind, c: ((rows, width), kind, (half, width), lambda i, p, c=c: (2 * c + p[0], 0))
    grown = {"tokens": None, "output": None}

    def grow(which, ins, outs, kernel):
        aliases = None
        if grown[which] is not None:
            aliases = {1 + len(ins): 0}
            ins = ins + [(grown[which], None, None)]
        results = call(kernel, (1,), ins, outs, prefetch=(place,), aliases=aliases, name=which)
        grown[which] = results[0]
        return results[1:]

    def put(which, kind, value, c):
        grow(which, [whole(value)], [((rows, width), kind, (half, width), lambda i, p: (2 * c + p[1], 0))], put_kernel)

    def token(c):
        ins = [(a, (half, width), at0(0)) for a in (chip[c], far_chip[c])]
        ins += [own(tokens, c), whole(grad_stream[c]), whole(ln1_g)]
        (value,) = grow("tokens", ins, [own_out(F32, c), fix((half, width), F32)], token_kernel)
        return swap(value, "tensor", tp, 1)

    def result(c):
        ins = [whole(ffn[c]), whole(far_ffn[c]), whole(stream[c]), whole(fc2_b), own_seg(c)]
        value, osums[c] = grow(
            "output", ins, [own_out(BF, c), fix((half, width), F32), fix((8, width), F32)], output_kernel
        )
        return swap(value, "tensor", tp, 1)

    osums, wide_tok, wide_out = {}, {}, {}
    for c in order[:-1]:
        wide_tok[c] = token(c)
    attn_sum = weight(
        [("halves", "chunks"), ("all", "chunks", "chunks", "chunks")],
        [
            [
                halves(grad_mix, {c: whole(near_mix[c]) for c in chunks}),
                [whole(low_ctx[c]) for c in chunks],
            ],
            [[whole(entry)]] + [[whole(g[c]) for c in chunks] for g in (grad_q, grad_k, grad_v)],
        ],
        4 * hw,
        "weight_attn",
    )
    for c in order[:-1]:
        wide_out[c] = result(c)
        put("tokens", F32, wide_tok[c], c)
    if near_blocks:
        fc1_parts = fc1_sum[0]()
        (grad_w_fc2,) = fc2_sum[1](fc2_parts)
    last = order[-1]
    wide_out[last] = result(last)
    for c in order[:-1]:
        put("output", BF, wide_out[c], c)

    add = lambda parts: functools.reduce(lambda a, b: a + b, [parts[c] for c in chunks])
    fs, gs, ns, hs, qs, es, os = (add(p) for p in (fsums, gsums, nsums, hsums, qsums, esums, osums))
    own_part = jnp.concatenate([hs[:5], fs[:3], os[:2], es[:2], gs[:3]], 0)
    near_part = jnp.concatenate([hs[:5], fs[:3], os[:2], es[:2], ns[:3]], 0)
    packed = own_part + swap(near_part, "tensor", tp, 1)
    far = swap(packed[10:12], "tensor", tp, 2)
    tail = jnp.concatenate([qs[0], qs[1], qs[2], qs[2]]).reshape(1, -1)[:, :width]
    packed = jnp.concatenate([packed[:10], packed[10:12] + far, packed[12:], tail], 0)
    if dp & (dp - 1) == 0:
        bit = 1
        while bit < dp:
            packed = packed + swap(packed, "dp", dp, bit)
            bit *= 2
    else:
        packed = lax.psum(packed, "dp")
    line.keep(packed)
    put("output", BF, wide_out[last], last)
    wide_tok[last] = token(last)
    if near_blocks:
        (grad_w_fc1,) = fc1_sum[1](fc1_parts)
    put("tokens", F32, wide_tok[last], last)
    if near_blocks:
        attn_parts = attn_sum[0]()
        grad_w_out, grad_w_query, grad_w_key, grad_w_value = attn_sum[1](attn_parts)
    else:
        (grad_w_fc2,), (grad_w_fc1,) = fc2_sum(), fc1_sum()
        grad_w_out, grad_w_query, grad_w_key, grad_w_value = attn_sum()
    grad_tokens, output = grown["tokens"], grown["output"]

    last_row = packed[15]
    counted = packed[7, 0]
    squares = jnp.stack([jnp.sum(packed[5]), jnp.sum(packed[8]), jnp.sum(packed[9])])
    rms = jnp.sqrt(squares / (counted * width))
    grad_head = jnp.sum(last_row[2 * hw : 3 * hw].reshape(heads, HEAD_DIM), axis=1)
    return (
        output,
        grad_tokens,
        grad_w_query,
        grad_w_key,
        grad_w_value,
        grad_w_out,
        grad_w_fc1,
        grad_w_fc2,
        packed[10],
        packed[11],
        packed[2],
        packed[3],
        packed[0],
        packed[1],
        packed[12],
        packed[13],
        last_row[:hw],
        last_row[hw : 2 * hw],
        packed[4],
        packed[14],
        packed[6],
        grad_head,
        rms,
    )


def solution(mesh):
    cut = P(None, "tensor")
    part = P("tensor")
    rows = P("dp", None)
    both = P("dp", "tensor")
    return jax.shard_map(
        functools.partial(body, mesh.shape["dp"], mesh.shape["tensor"]),
        mesh=mesh,
        in_specs=(rows, rows) + (cut,) * 6 + (P(),) * 6 + (part,) * 4 + (P(), part, P(), part, rows),
        out_specs=(rows, rows) + (both,) * 6 + (P(),) * 6 + (part,) * 4 + (P(), part, P(), part, P()),
        check_vma=False,
    )
```

```python
import functools

import jax
import jax.numpy as jnp
from jax import lax
from jax.experimental import pallas as pl
from jax.experimental.pallas import tpu as pltpu
from jax.sharding import PartitionSpec as P

HEAD_DIM = 64
EPSILON = 1e-05
EXCLUDED = -1e30
LANES = 128
CHUNKS = 2
PAD = 16
BF = jnp.bfloat16
F32 = jnp.float32


def dot_nn(a, b):
    return lax.dot_general(a, b, (((1,), (0,)), ((), ())), preferred_element_type=F32)


def dot_nt(a, b):
    return lax.dot_general(a, b, (((1,), (1,)), ((), ())), preferred_element_type=F32)


def dot_tn(a, b):
    return lax.dot_general(a, b, (((0,), (0,)), ((), ())), preferred_element_type=F32)


def normalize(v):
    mean = jnp.mean(v, axis=-1, keepdims=True)
    centred = v - mean
    factor = lax.rsqrt(jnp.mean(centred * centred, axis=-1, keepdims=True) + EPSILON)
    return centred * factor, factor


def norm_back(scaled, normed, factor):
    return factor * (
        scaled
        - jnp.mean(scaled, axis=-1, keepdims=True)
        - normed * jnp.mean(scaled * normed, axis=-1, keepdims=True)
    )


def col_sum(v):
    return jnp.sum(v, axis=0, keepdims=True)


def tanh_inner(v):
    return 0.7978845608028654 * (v + 0.044715 * (v * v * v))


def columns_to_rows(columns):
    n = columns[0].shape[0]
    lane = lax.broadcasted_iota(jnp.int32, (n, LANES), 1)
    tile = jnp.zeros((n, LANES), F32)
    for index, column in enumerate(columns):
        tile = jnp.where(lane == index, column, tile)
    return jnp.transpose(tile)[:8]


def rows_to_columns(rows):
    n = rows[0].shape[1]
    sub = lax.broadcasted_iota(jnp.int32, (LANES, n), 0)
    tile = jnp.zeros((LANES, n), F32)
    for index, row in enumerate(rows):
        tile = jnp.where(sub == index, row, tile)
    tile = jnp.transpose(tile)
    return [tile[:, index : index + 1] for index in range(len(rows))]


def stack_rows(rows, width):
    sub = lax.broadcasted_iota(jnp.int32, (8, width), 0)
    tile = jnp.zeros((8, width), F32)
    for index, row in enumerate(rows):
        tile = jnp.where(sub == index, row, tile)
    return tile


def head_masks(width, kind):
    lane = lax.broadcasted_iota(jnp.int32, (1, width), 1) // HEAD_DIM
    return [(lane == head).astype(F32).astype(kind) for head in range(width // HEAD_DIM)]


def qkv_kernel(tok, gain, bias, wq, wk, wv, qb, vb, entry, q, k, v):
    normed, _ = normalize(tok[...].astype(F32))
    low = (normed * gain[...] + bias[...]).astype(BF)
    entry[...] = low
    q[...] = ((dot_nn(low, wq[...]) + qb[...]) * HEAD_DIM**-0.5).astype(BF)
    k[...] = dot_nn(low, wk[...]).astype(BF)
    v[...] = (dot_nn(low, wv[...]) + vb[...]).astype(BF)


def attend_kernel(first, block, place, q, k, v, segq, segk, scale, attended, low, mine, theirs, logsum, hold):
    rows, width = q.shape
    half = rows // 2
    masks = head_masks(width, BF)
    for at in range(0, rows, block):
        length = first + at + block
        query = q[at : at + block, :]
        keys = k[:length, :]
        (seg,) = rows_to_columns([segq[:, at : at + block].astype(F32)])
        place_q = first + at + lax.broadcasted_iota(jnp.int32, (block, length), 0)
        place_k = lax.broadcasted_iota(jnp.int32, (block, length), 1)
        allowed = (seg == segk[:, :length].astype(F32)) & (place_k <= place_q)
        shift = jnp.where(allowed, 0.0, EXCLUDED)
        total = jnp.zeros((block, width), F32)
        sums = []
        for mask in masks:
            scores = dot_nt(query * mask, keys) + shift
            top = jnp.max(scores, axis=-1, keepdims=True)
            expo = jnp.exp(scores - top)
            norm = jnp.sum(expo, axis=-1, keepdims=True)
            weights = (expo * (1.0 / norm)).astype(BF)
            total = total + dot_nn(weights, v[:length, :] * mask)
            sums.append(top + jnp.log(norm))
        attended[at : at + block, :] = total
        context = (total * scale[...]).astype(BF)
        low[at : at + block, :] = context
        hold[at : at + block, :] = context.astype(F32)
        logsum[:, at : at + block] = columns_to_rows(sums)
    mine[...] = hold[pl.ds(pl.multiple_of(place[0] * half, half), half), :]
    theirs[...] = hold[pl.ds(pl.multiple_of(place[1] * half, half), half), :]


def pack_kernel(wide, near_out, out_pair, fc1, fc2):
    width, units = near_out.shape[1], fc1.shape[1]
    out_pair[:, :width] = near_out[...]
    out_pair[:, width:] = wide[:, :width].astype(BF)
    fc1[...] = wide[:, width : width + units].astype(BF)
    fc2[...] = wide[:, width + units :].astype(BF)


def far_kernel(side, far_half, far_rest, diag_half, diag_rest, out):
    rows, width = far_half.shape
    here = pl.ds(pl.multiple_of(side[0] * rows, rows), rows)
    there = pl.ds(pl.multiple_of((1 - side[0]) * rows, rows), rows)
    out[here, :width] = far_half[...].astype(BF)
    out[there, :width] = far_rest[...].astype(BF)
    out[here, width:] = diag_half[...].astype(BF)
    out[there, width:] = diag_rest[...].astype(BF)


def upstream_kernel(place, cot, own, near, out):
    units = own.shape[1]
    out[:, :units] = dot_nn(cot[...], own[...])
    out[:, units:] = dot_nn(cot[...], near[...])


def forward_kernel(
    place, seg, ctx_chip, ctx_far, wo_chip, wo_far, out_bias, tok, post_gain, post_bias, ln2_gain, ln2_bias,
    fc1_own, fc1_near, fc1_bias, mid_gain, near, cot, grad_middle,
    mixed, stream, inner, share, hidden, stats, sums,
):
    units = fc1_own.shape[1]
    mix = (
        dot_nt(ctx_chip[...].astype(BF), wo_chip[...]) + dot_nt(ctx_far[...].astype(BF), wo_far[...])
    ) + out_bias[...]
    mixed[...] = mix
    normed, _ = normalize(mix)
    branch = normed * post_gain[...] + post_bias[...]
    resid = tok[...].astype(F32) + branch
    stream[...] = resid
    normed2, _ = normalize(resid)
    low = (normed2 * ln2_gain[...] + ln2_bias[...]).astype(BF)
    inner[...] = low
    share[...] = low.astype(F32)
    actives, scaleds = [], []
    for part, (weight, bias, gain) in enumerate(
        ((fc1_own, fc1_bias[...], mid_gain[...]), (fc1_near, near[0:1, :], near[1:2, :]))
    ):
        hid = dot_nn(low, weight[...]) + bias
        hidden[:, part * units : (part + 1) * units] = hid
        actives.append(0.5 * hid * (1.0 + jnp.tanh(tanh_inner(hid))))
        scaleds.append(grad_middle[:, part * units : (part + 1) * units] * gain)

    def both(left, right):
        return jnp.sum(left, axis=-1, keepdims=True) + jnp.sum(right, axis=-1, keepdims=True)

    mean = both(*actives) / (2 * units)
    centred = [active - mean for active in actives]
    stats[...] = columns_to_rows(
        [
            mean,
            both(*[c * c for c in centred]),
            both(*scaleds),
            both(*[s * c for s, c in zip(scaleds, centred)]),
        ]
    )
    (which,) = rows_to_columns([seg[...].astype(F32)])
    valid = (which >= 0).astype(F32)
    sums[...] = stack_rows(
        [
            col_sum(valid * branch * branch),
            col_sum(cot[...].astype(F32)),
            col_sum(valid * jnp.ones_like(branch)),
        ],
        branch.shape[1],
    )


def middle_kernel(
    total, hidden, grad_middle, st0, st1, mid_gain, mid_bias, near,
    fc1_own, fc1_near, fc2_own, fc2_near,
    middle, grad_hidden, share, ffn, back, sums_own, sums_near,
):
    units = fc1_own.shape[1]
    n = 2 * units
    mean = (st0[0:1, :] + st1[0:1, :]) * 0.5
    apart = [s[0:1, :] - mean for s in (st0, st1)]
    spread = (st0[1:2, :] + n * (apart[0] * apart[0])) + (st1[1:2, :] + n * (apart[1] * apart[1]))
    factor = lax.rsqrt(spread / total + EPSILON)
    plain = (st0[2:3, :] + st1[2:3, :]) / total
    along = (st0[3:4, :] + apart[0] * st0[2:3, :]) + (st1[3:4, :] + apart[1] * st1[2:3, :])
    mean, factor, plain, along = rows_to_columns([mean, factor, plain, factor * along / total])
    parts = (
        (mid_gain[...], mid_bias[...], fc1_own, fc2_own, sums_own),
        (near[1:2, :], near[2:3, :], fc1_near, fc2_near, sums_near),
    )
    ffn_parts, back_parts = [], []
    for part, (gain, bias, fc1, fc2, sums) in enumerate(parts):
        hid = hidden[:, part * units : (part + 1) * units]
        bend = jnp.tanh(tanh_inner(hid))
        active = 0.5 * hid * (1.0 + bend)
        slope = 0.5 * (1.0 + bend) + 0.5 * hid * (1.0 - bend * bend) * (
            0.7978845608028654 * (1.0 + 3 * 0.044715 * (hid * hid))
        )
        normed = (active - mean) * factor
        mid = (normed * gain + bias).astype(BF)
        grad = grad_middle[:, part * units : (part + 1) * units]
        low = (factor * (grad * gain - plain - normed * along) * slope).astype(BF)
        if part == 0:
            middle[...] = mid
            grad_hidden[...] = low
        else:
            share[:, :units] = mid.astype(F32)
            share[:, units:] = low.astype(F32)
        sums[...] = stack_rows([col_sum(grad * normed), col_sum(grad), col_sum(low.astype(F32))], units)
        ffn_parts.append(dot_nt(mid, fc2[...]))
        back_parts.append(dot_nt(low, fc1[...]))
    ffn[...] = ffn_parts[0] + ffn_parts[1]
    back[: hidden.shape[0], :] = back_parts[0] + back_parts[1]
    back[hidden.shape[0] :, :] = jnp.zeros((PAD, back.shape[1]), F32)


def stream_kernel(
    place, mine, far, mixed, stream, cot, ln2_gain, post_gain, w_out,
    grad_stream, grad_mixed, wide, context_own, context_near, sums,
):
    grad = mine[: stream.shape[0], :] + far[: stream.shape[0], :]
    normed2, factor2 = normalize(stream[...])
    back = cot[...].astype(F32) + norm_back(grad * ln2_gain[...], normed2, factor2)
    grad_stream[...] = back
    normedp, factorp = normalize(mixed[...])
    low = norm_back(back * post_gain[...], normedp, factorp).astype(BF)
    grad_mixed[...] = low
    wide[...] = low.astype(F32)
    context = dot_nn(low, w_out[...])
    width = context_own.shape[1]
    context_own[...] = context[:, :width]
    context_near[...] = context[:, width:]
    sums[...] = stack_rows(
        [
            col_sum(grad * normed2),
            col_sum(grad),
            col_sum(back * normedp),
            col_sum(back),
            col_sum(low.astype(F32)),
        ],
        back.shape[1],
    )


def attend_back_kernel(first, block, last, place, *refs):
    q, k, v, segq, segk, context_own, context_near, attended, scale, logsum = refs[:10]
    rest = list(refs[10:])
    if not last:
        key_in, value_in = rest[:2]
        rest = rest[2:]
    grad_q, grad_k, grad_v, sums = rest[:4]
    rest = rest[4:]
    if first:
        key_out, value_out = rest[:2]
        rest = rest[2:]
    key_sum, value_sum, low_probs, low_scores, grads = rest
    rows, width = q.shape
    half = rows // 2
    end = first + rows
    masks = head_masks(width, BF)
    wide_masks = head_masks(width, F32)
    if last:
        key_sum[...] = jnp.zeros_like(key_sum)
        value_sum[...] = jnp.zeros_like(value_sum)
    else:
        key_sum[...] = key_in[...]
        value_sum[...] = value_in[...]
    head_sum = jnp.zeros((1, width), F32)
    for part, source in enumerate((context_own, context_near)):
        at = pl.ds(pl.multiple_of(place[part] * half, half), half)
        grad_context = source[...]
        head_sum = head_sum + col_sum(grad_context * attended[at, :])
        grads[at, :] = (grad_context * scale[...]).astype(BF)
    (seg,) = rows_to_columns([segk[:, :end].astype(F32)])
    query_sum = jnp.zeros((1, width), F32)
    for at in range(0, rows, block):
        length = first + at + block
        query = q[at : at + block, :]
        grad = grads[at : at + block, :]
        product = grad.astype(F32) * attended[at : at + block, :]
        delta = columns_to_rows([jnp.sum(product * mask, axis=-1, keepdims=True) for mask in wide_masks])
        place_k = lax.broadcasted_iota(jnp.int32, (length, block), 0)
        place_q = first + at + lax.broadcasted_iota(jnp.int32, (length, block), 1)
        allowed = (seg[:length] == segq[:, at : at + block].astype(F32)) & (place_k <= place_q)
        shift = jnp.where(allowed, 0.0, EXCLUDED)
        queries = [query * mask for mask in masks]
        grad_parts = [grad * mask for mask in masks]
        grad_query = jnp.zeros((block, width), F32)
        for head, mask in enumerate(masks):
            scores = dot_nt(k[:length, :], queries[head]) + shift
            probs = jnp.exp(scores - logsum[head : head + 1, at : at + block])
            low_probs[:length, head * block : (head + 1) * block] = probs.astype(BF)
            grad_probs = dot_nt(v[:length, :], grad_parts[head])
            low = (probs * (grad_probs - delta[head : head + 1, :])).astype(BF)
            low_scores[:length, head * block : (head + 1) * block] = low
            grad_query = grad_query + dot_tn(low, k[:length, :] * mask)
        value_sum[:length, :] += dot_nn(low_probs[:length, :], jnp.concatenate(grad_parts, axis=0))
        key_sum[:length, :] += dot_nn(low_scores[:length, :], jnp.concatenate(queries, axis=0))
        low_query = (grad_query * HEAD_DIM**-0.5).astype(BF)
        grad_q[at : at + block, :] = low_query
        query_sum = query_sum + col_sum(low_query.astype(F32))
    grad_k[...] = key_sum[first:end, :].astype(BF)
    low_value = value_sum[first:end, :].astype(BF)
    grad_v[...] = low_value
    sums[...] = stack_rows([query_sum, col_sum(low_value.astype(F32)), head_sum], width)
    if first:
        key_out[...] = key_sum[:first, :]
        value_out[...] = value_sum[:first, :]


def entry_kernel(place, grad_q, grad_k, grad_v, wq, wk, wv, tok, send, keep, sums):
    step = pl.program_id(0)
    part = dot_nt(grad_q[...], wq[...]) + dot_nt(grad_k[...], wk[...]) + dot_nt(grad_v[...], wv[...])
    normed, _ = normalize(tok[...].astype(F32))
    fresh = stack_rows([col_sum(part * normed), col_sum(part)], part.shape[1])

    @pl.when(step == 0)
    def _():
        sums[...] = fresh
        send[...] = part

    @pl.when(step != 0)
    def _():
        sums[...] += fresh
        keep[...] = part


def chip_kernel(keep, got, out):
    out[...] = keep[...] + got[...]


def token_kernel(place, mine, far, tok, grad_stream, gain, *refs):
    out, wide = refs[-2:]
    normed, factor = normalize(tok[...].astype(F32))
    grad = grad_stream[...] + norm_back((mine[...] + far[...]) * gain[...], normed, factor)
    out[...] = grad
    wide[...] = grad


def output_kernel(place, mine, far, stream, bias, seg, *refs):
    out, wide, sums = refs[-3:]
    ffn = (mine[...] + far[...]) + bias[...]
    result = stream[...] + ffn
    low = result.astype(BF)
    out[...] = low
    wide[...] = low.astype(F32)
    (which,) = rows_to_columns([seg[...].astype(F32)])
    valid = (which >= 0).astype(F32)
    sums[...] = stack_rows([col_sum(valid * ffn * ffn), col_sum(valid * result * result)], ffn.shape[1])


def put_kernel(place, value, full, out):
    out[...] = value[...].astype(out.dtype)


def line_kernel(kind, chunks, half, place, *refs):
    items, out = refs[:-1], refs[-1]
    for c in range(chunks):
        if kind == "chunks":
            out[2 * c * half : 2 * (c + 1) * half, :] = items[c][...]
        else:
            for part in range(2):
                at = pl.ds(pl.multiple_of((2 * c + place[part]) * half, half), half)
                out[at, :] = items[2 * c + part][...].astype(BF)


def weight_kernel(plan, chunks, half, blocks, place, *refs):
    step = pl.program_id(0)
    refs = list(refs)
    count = {"all": 1, "halves": 2 * chunks, "chunks": chunks}
    sources = [[(kind, [refs.pop(0) for _ in range(count[kind])]) for kind in product] for product in plan]
    send, keep = refs[:2]
    holds = refs[2:]
    depth = send.shape[0]
    operands, fills = [], []
    for product in sources:
        row = []
        for kind, items in product:
            if kind == "all":
                row.append(items[0])
            else:
                hold = holds.pop(0)
                fills.append((kind, items, hold))
                row.append(hold)
        operands.append(row)

    @pl.when(step == 0)
    def _():
        for kind, items, hold in fills:
            line_kernel(kind, chunks, half, place, *items, hold)

    def fill(target):
        offset = 0
        for row in operands:
            left = row[0]
            columns = jnp.concatenate(
                [
                    left[:, pl.ds(pl.multiple_of(blocks[step * depth + j] * LANES, LANES), LANES)]
                    for j in range(depth)
                ],
                axis=1,
            )
            for right in row[1:]:
                total = dot_tn(columns, right[...])
                width = total.shape[1]
                target[:, :, offset : offset + width] = total.reshape(depth, LANES, width)
                offset += width

    @pl.when(step == 0)
    def _():
        fill(send)

    @pl.when(step != 0)
    def _():
        fill(keep)


def first_kernel(keep, got, out):
    out[...] = keep[...] + got[...]


def second_kernel(keep, got, near, out):
    out[...] = (keep[0] + got[0]) + near[0]


def third_kernel(keep, got, near, far, *outs):
    at = 0
    for out in outs:
        cut = slice(at, at + out.shape[1])
        out[...] = ((keep[0, :, cut] + got[0, :, cut]) + near[0, :, cut]) + far[:, cut]
        at += out.shape[1]


def whole(array):
    shape = array.shape
    return (array, shape, lambda *_: (0,) * len(shape))


def swap(value, axis, size, bit):
    return lax.ppermute(value, axis, [(i, i ^ bit) for i in range(size)])


class Order:
    def __init__(self):
        self.last = None

    def after(self, value):
        if self.last is None:
            return value
        return lax.optimization_barrier((value, self.last))[0]

    def keep(self, value):
        self.last = value
        return value

    def wait(self, values):
        tied = lax.optimization_barrier((tuple(values), self.last))
        self.last = tied[1]
        return list(tied[0])

    def call(self, kernel, grid, ins, outs, prefetch=(), scratch=(), aliases=None, vmem=32 << 20, name=None):
        arrays = [item[0] for item in ins]
        specs = [
            pl.BlockSpec(memory_space=pl.ANY) if block is None else pl.BlockSpec(block, place)
            for _, block, place in ins
        ]
        body_of = kernel
        if self.last is not None:
            at = len(prefetch) + len(arrays)
            arrays.append(self.last)
            specs.append(pl.BlockSpec(memory_space=pl.ANY))

            def body_of(*refs):
                return kernel(*refs[:at], *refs[at + 1 :])

        results = pl.pallas_call(
            body_of,
            grid_spec=pltpu.PrefetchScalarGridSpec(
                num_scalar_prefetch=len(prefetch),
                grid=grid,
                in_specs=specs,
                out_specs=[pl.BlockSpec(block, place) for _, _, block, place in outs],
                scratch_shapes=list(scratch),
            ),
            out_shape=[jax.ShapeDtypeStruct(shape, kind) for shape, kind, _, _ in outs],
            input_output_aliases=aliases or {},
            compiler_params=pltpu.CompilerParams(
                dimension_semantics=("arbitrary",) * len(grid), vmem_limit_bytes=vmem
            ),
            cost_estimate=pl.CostEstimate(flops=1000, bytes_accessed=1000, transcendentals=0),
            name=name,
        )(*prefetch, *arrays)
        self.last = min(results, key=lambda r: r.size)
        return results


def body(
    dp, tp, tokens, segments, w_query, w_key, w_value, w_out, w_fc1, w_fc2, ln1_gain, ln1_bias, post_gain, post_bias,
    ln2_gain, ln2_bias, mid_gain, mid_bias, query_bias, value_bias, out_bias, fc1_bias, fc2_bias, head_scale, cotangent,
):
    rows, width = tokens.shape
    hw = w_query.shape[1]
    units = w_fc1.shape[1]
    heads = hw // HEAD_DIM
    size = rows // CHUNKS
    half = size // 2
    block = min(256, size)
    line = Order()
    call = line.call
    row = lambda v: v.reshape(1, -1)
    seg = segments.reshape(1, rows)
    ln1_g, ln1_b, post_g, post_b = row(ln1_gain), row(ln1_bias), row(post_gain), row(post_bias)
    ln2_g, ln2_b, mid_g, mid_b = row(ln2_gain), row(ln2_bias), row(mid_gain), row(mid_bias)
    q_b, v_b, out_b, fc1_b, fc2_b = row(query_bias), row(value_bias), row(out_bias), row(fc1_bias), row(fc2_bias)
    scale = row(jnp.repeat(head_scale, HEAD_DIM))
    core = lax.axis_index("tensor") & 1
    place = (core + jnp.arange(2, dtype=jnp.int32)) & 1
    dp_side = lax.axis_index("dp") & 1
    side = dp_side.astype(jnp.int32).reshape(1)
    chunks = list(range(CHUNKS))
    order = chunks[::-1]

    half_rows = width // 2
    part = lax.dynamic_slice_in_dim(w_out, dp_side * half_rows, half_rows, 0).astype(F32)
    far_half = swap(part, "tensor", tp, 2)
    wide = swap(jnp.concatenate([w_out, w_fc1, w_fc2], 1).astype(F32), "tensor", tp, 1)
    pad = jnp.zeros((5, units), F32)
    near = swap(jnp.concatenate([fc1_b, mid_g, mid_b, pad], 0), "tensor", tp, 1)

    step = min(256, rows)
    entry, query, keys, values = call(
        qkv_kernel,
        (rows // step,),
        [(tokens, (step, width), lambda i: (i, 0))]
        + [whole(a) for a in (ln1_g, ln1_b, w_query, w_key, w_value, q_b, v_b)],
        [((rows, width), BF, (step, width), lambda i: (i, 0))]
        + [((rows, hw), BF, (step, hw), lambda i: (i, 0))] * 3,
        name="qkv",
    )

    at0 = lambda c: (lambda *_: (c, 0))
    at1 = lambda c: (lambda *_: (0, c))
    fix = lambda shape, kind: (shape, kind, shape, lambda *_: (0,) * len(shape))
    own = lambda a, c: (a, (half, a.shape[1]), lambda i, p, c=c: (2 * c + p[0], 0))
    own_seg = lambda c: (seg, (1, half), lambda i, p, c=c: (0, 2 * c + p[0]))

    (far_half,) = line.wait([far_half])
    far_rest = swap(far_half, "dp", dp, 1)
    attended, low_ctx, ctx, logsum = {}, {}, {}, {}
    for c in order:
        end = (c + 1) * size
        attended[c], low_ctx[c], mine, theirs, logsum[c] = call(
            functools.partial(attend_kernel, c * size, block),
            (1,),
            [
                (query, (size, hw), at0(c)),
                (keys, (end, hw), at0(0)),
                (values, (end, hw), at0(0)),
                (seg, (1, size), at1(c)),
                (seg, (1, end), at1(0)),
                whole(scale),
            ],
            [fix((size, hw), F32), fix((size, hw), BF), fix((half, hw), F32), fix((half, hw), F32), fix((8, size), F32)],
            prefetch=(place,),
            scratch=[pltpu.VMEM((size, hw), F32)],
            name="attend",
        )
        ctx[c] = (mine, swap(theirs, "tensor", tp, 1))
    far_ctx = {}
    for c in order:
        mine, got = ctx[c]
        ctx[c] = line.keep(jnp.concatenate([line.after(mine), got], 1))
        far_ctx[c] = swap(ctx[c], "tensor", tp, 2)

    step = min(256, width)
    wo_chip, fc1_near, fc2_near = call(
        pack_kernel,
        (width // step,),
        [(a, (step, a.shape[1]), lambda i: (i, 0)) for a in (wide, w_out)],
        [((width, n), BF, (step, n), lambda i: (i, 0)) for n in (2 * hw, units, units)],
        name="pack",
    )
    diag_half = swap(far_half, "tensor", tp, 1)
    diag_rest = swap(far_rest, "tensor", tp, 1)
    (grad_mid,) = call(
        upstream_kernel,
        (CHUNKS,),
        [(cotangent, (half, width), lambda i, p: (2 * i + p[0], 0)), whole(w_fc2), whole(fc2_near)],
        [((CHUNKS * half, 2 * units), F32, (half, 2 * units), lambda i, p: (i, 0))],
        prefetch=(place,),
        name="upstream",
    )
    (wo_far,) = call(
        far_kernel,
        (1,),
        [whole(a) for a in (far_half, far_rest, diag_half, diag_rest)],
        [fix((width, 2 * hw), BF)],
        prefetch=(side,),
        name="far",
    )

    mixed, stream, inner, hidden, stats, far_stats, fsums, near_inner = {}, {}, {}, {}, {}, {}, {}, {}
    for c in order:
        mixed[c], stream[c], inner[c], share, hidden[c], stats[c], fsums[c] = call(
            forward_kernel,
            (1,),
            [own_seg(c)]
            + [whole(a) for a in (ctx[c], far_ctx[c], wo_chip, wo_far, out_b)]
            + [own(tokens, c)]
            + [whole(a) for a in (post_g, post_b, ln2_g, ln2_b, w_fc1, fc1_near, fc1_b, mid_g, near)]
            + [own(cotangent, c), (grad_mid, (half, 2 * units), at0(c))],
            [fix((half, width), F32)] * 2
            + [fix((half, width), BF), fix((half, width), F32), fix((half, 2 * units), F32)]
            + [fix((8, half), F32), fix((8, width), F32)],
            prefetch=(place,),
            name="forward",
        )
        far_stats[c] = swap(stats[c], "tensor", tp, 2)
        near_inner[c] = swap(share, "tensor", tp, 1)

    middle, grad_hid, ffn, back, far_back, gsums, nsums = {}, {}, {}, {}, {}, {}, {}
    near_mid, near_hid = {}, {}
    for c in order:
        mid, hid, share, ffn[c], back[c], gsums[c], nsums[c] = call(
            functools.partial(middle_kernel, units * tp),
            (1,),
            [whole(hidden[c]), (grad_mid, (half, 2 * units), at0(c))]
            + [whole(a) for a in (stats[c], far_stats[c], mid_g, mid_b, near)]
            + [whole(a) for a in (w_fc1, fc1_near, w_fc2, fc2_near)],
            [fix((half, units), BF)] * 2
            + [fix((half, 2 * units), F32)]
            + [fix((half, width), F32), fix((half + PAD, width), F32)]
            + [fix((8, units), F32)] * 2,
            name="middle",
        )
        middle[c], grad_hid[c] = mid, hid
        far_back[c] = swap(back[c], "tensor", tp, 2)
        near_both = swap(share, "tensor", tp, 1)
        near_mid[c] = (near_both, (half, units), lambda *_: (0, 0))
        near_hid[c] = (near_both, (half, units), lambda *_: (0, 1))

    near_blocks = width // dp == LANES and dp == 8
    if near_blocks:
        depth = dp // 2
        me = lax.axis_index("dp")
        slot = jnp.arange(dp, dtype=jnp.int32)
        ring = me // 2
        at_ring = jnp.stack([depth - 1 - (ring ^ 1), ring ^ 1, depth - 1 - ring, ring] * 2)
        blocks = (2 * at_ring + ((me + 1 + slot // depth) & 1)).astype(jnp.int32)

    def weight(plan, items, columns, name):
        arrays = [item for group in items for operand in group for item in operand]
        kinds = [kind for product in plan for kind in product]
        holds = [
            pltpu.VMEM((rows, operand[0][1][1]), BF)
            for kind, operand in zip(kinds, [o for g in items for o in g])
            if kind != "all"
        ]
        if not near_blocks:
            results = []
            for product, group in zip(plan, items):
                full = []
                for kind, operand in zip(product, group):
                    if kind == "all":
                        full.append(operand[0][0])
                        continue
                    n = operand[0][1][1]
                    (lined,) = call(
                        functools.partial(line_kernel, kind, CHUNKS, half),
                        (1,),
                        operand,
                        [fix((rows, n), BF)],
                        prefetch=(place,),
                        name=name,
                    )
                    full.append(lined)
                results += [
                    lax.psum_scatter(dot_tn(full[0], right), "dp", scatter_dimension=0, tiled=True)
                    for right in full[1:]
                ]
            return lambda: results
        send, keep = call(
            functools.partial(weight_kernel, plan, CHUNKS, half),
            (2,),
            arrays,
            [fix((depth, LANES, columns), F32)] * 2,
            prefetch=(blocks, place),
            scratch=holds,
            name=name,
        )
        got = swap(send, "dp", dp, 1)

        lanes = min(1024, columns)
        by_lanes = lambda array, count, first: (array, (count, LANES, lanes), lambda i: (first, 0, i))

        def first():
            (send,) = call(
                first_kernel,
                (columns // lanes,),
                [by_lanes(a, 2, 0) for a in (keep, got)],
                [((2, LANES, columns), F32, (2, LANES, lanes), lambda i: (0, 0, i))],
                name="first",
            )
            return swap(send, "dp", dp, 2)

        def second(near):
            (send,) = call(
                second_kernel,
                (columns // lanes,),
                [by_lanes(a, 1, 2) for a in (keep, got)] + [by_lanes(near, 1, 0)],
                [((LANES, columns), F32, (LANES, lanes), lambda i: (0, i))],
                name="second",
            )
            return lax.ppermute(send, "dp", [(i, dp - 2 - i + 2 * (i & 1)) for i in range(dp)])

        def third(near, far):
            return call(
                third_kernel,
                (1,),
                [(a, (1, LANES, columns), lambda *_, f=f: (f, 0, 0)) for a, f in ((keep, 3), (got, 3), (near, 1))]
                + [whole(far)],
                [fix((LANES, operand[0][1][1]), F32) for group in items for operand in group[1:]],
                name="third",
            )

        return first, second, third

    halves = lambda mine, wide_near: [item for c in chunks for item in (whole(mine[c]), wide_near[c])]
    fc2_sum = weight(
        [("all", "halves")],
        [[[whole(cotangent)], halves(middle, near_mid)]],
        units,
        "weight_fc2",
    )
    fc1_sum = weight(
        [("halves", "halves")],
        [
            [
                halves(inner, {c: whole(near_inner[c]) for c in chunks}),
                halves(grad_hid, near_hid),
            ]
        ],
        units,
        "weight_fc1",
    )

    own_out = lambda kind, c: ((rows, width), kind, (half, width), lambda i, p, c=c: (2 * c + p[0], 0))
    grown = {"tokens": None, "output": None}

    def grow(which, ins, outs, kernel):
        aliases = None
        if grown[which] is not None:
            aliases = {1 + len(ins): 0}
            ins = ins + [(grown[which], None, None)]
        results = call(kernel, (1,), ins, outs, prefetch=(place,), aliases=aliases, name=which)
        grown[which] = results[0]
        return results[1:]

    def put(which, kind, value, c):
        grow(which, [whole(value)], [((rows, width), kind, (half, width), lambda i, p: (2 * c + p[1], 0))], put_kernel)

    def token(c):
        ins = [(a, (half, width), at0(0)) for a in (chip[c], far_chip[c])]
        ins += [own(tokens, c), whole(grad_stream[c]), whole(ln1_g)]
        (value,) = grow("tokens", ins, [own_out(F32, c), fix((half, width), F32)], token_kernel)
        return swap(value, "tensor", tp, 1)

    def result(c):
        ins = [whole(ffn[c]), whole(far_ffn[c]), whole(stream[c]), whole(fc2_b), own_seg(c)]
        value, osums[c] = grow(
            "output", ins, [own_out(BF, c), fix((half, width), F32), fix((8, width), F32)], output_kernel
        )
        return swap(value, "tensor", tp, 1)

    grad_stream, grad_mix, near_mix, grad_q, grad_k, grad_v, chip, far_chip = {}, {}, {}, {}, {}, {}, {}, {}
    hsums, qsums, esums, far_ffn = {}, {}, {}, {}
    osums, wide_tok, wide_out = {}, {}, {}
    carry = None
    fc2_part = fc1_part = attn_part = None
    for c in order:
        end = (c + 1) * size
        last = c == CHUNKS - 1
        by_half = lambda a: (a, (half, a.shape[1]), lambda i, p: (p[1 - i], 0))
        grad_stream[c], grad_mix[c], wide_mix, ctx_own, ctx_near, hsums[c] = call(
            stream_kernel,
            (1,),
            [whole(a) for a in (back[c], far_back[c], mixed[c], stream[c])]
            + [own(cotangent, c), whole(ln2_g), whole(post_g), whole(wo_chip)],
            [fix((half, width), F32), fix((half, width), BF), fix((half, width), F32)]
            + [fix((half, hw), F32)] * 2
            + [fix((8, width), F32)],
            prefetch=(place,),
            name="stream",
        )
        ctx_near = swap(ctx_near, "tensor", tp, 1)
        near_mix[c] = swap(wide_mix, "tensor", tp, 1)
        results = call(
            functools.partial(attend_back_kernel, c * size, block, last),
            (1,),
            [
                (query, (size, hw), at0(c)),
                (keys, (end, hw), at0(0)),
                (values, (end, hw), at0(0)),
                (seg, (1, size), at1(c)),
                (seg, (1, end), at1(0)),
            ]
            + [whole(a) for a in (ctx_own, ctx_near, attended[c], scale, logsum[c])]
            + ([] if last else [whole(a) for a in carry]),
            [fix((size, hw), BF)] * 3 + [fix((8, hw), F32)] + ([fix((c * size, hw), F32)] * 2 if c else []),
            prefetch=(place,),
            scratch=[pltpu.VMEM((end, hw), F32)] * 2
            + [pltpu.VMEM((end, heads * block), BF)] * 2
            + [pltpu.VMEM((size, hw), BF)],
            name="attend_back",
        )
        grad_q[c], grad_k[c], grad_v[c], qsums[c] = results[:4]
        carry = results[4:]
        if c == order[-1] and near_blocks:
            fc2_part = fc2_sum[0]()
        send, keep, esums[c] = call(
            entry_kernel,
            (2,),
            [by_half(a) for a in (grad_q[c], grad_k[c], grad_v[c])]
            + [whole(a) for a in (w_query, w_key, w_value)]
            + [(tokens, (half, width), lambda i, p, c=c: (2 * c + p[1 - i], 0))],
            [fix((half, width), F32)] * 2 + [fix((8, width), F32)],
            prefetch=(place,),
            name="entry",
        )
        got = swap(send, "tensor", tp, 1)
        if c == order[-1]:
            for d in order[:-1]:
                far_ffn[d] = swap(ffn[d], "tensor", tp, 2)
                wide_out[d] = result(d)
            far_ffn[c] = swap(line.after(ffn[c]), "tensor", tp, 2)
        (chip[c],) = call(
            chip_kernel,
            (1,),
            [whole(a) for a in (keep, got)],
            [fix((half, width), F32)],
            name="chip",
        )
        far_chip[c] = swap(chip[c], "tensor", tp, 2)

    attn_sum = weight(
        [("halves", "chunks"), ("all", "chunks", "chunks", "chunks")],
        [
            [
                halves(grad_mix, {c: whole(near_mix[c]) for c in chunks}),
                [whole(low_ctx[c]) for c in chunks],
            ],
            [[whole(entry)]] + [[whole(g[c]) for c in chunks] for g in (grad_q, grad_k, grad_v)],
        ],
        4 * hw,
        "weight_attn",
    )
    for c in order[:-1]:
        wide_tok[c] = token(c)
    last = order[-1]
    if near_blocks:
        fc2_last = fc2_sum[1](fc2_part)
        fc1_part = fc1_sum[0]()
        (grad_w_fc2,) = fc2_sum[2](fc2_part, fc2_last)
    wide_out[last] = result(last)
    if near_blocks:
        fc1_last = fc1_sum[1](fc1_part)

    add = lambda parts: functools.reduce(lambda a, b: a + b, [parts[c] for c in chunks])
    fs, gs, ns, hs, qs, es, os = (add(p) for p in (fsums, gsums, nsums, hsums, qsums, esums, osums))
    own_part = jnp.concatenate([hs[:5], fs[:3], os[:2], es[:2], gs[:3]], 0)
    near_part = jnp.concatenate([hs[:5], fs[:3], os[:2], es[:2], ns[:3]], 0)
    packed = own_part + swap(near_part, "tensor", tp, 1)
    far = swap(packed[10:12], "tensor", tp, 2)
    tail = jnp.concatenate([qs[0], qs[1], qs[2], qs[2]]).reshape(1, -1)[:, :width]
    packed = jnp.concatenate([packed[:10], packed[10:12] + far, packed[12:], tail], 0)
    wide_tok[last] = token(last)
    line.keep(packed)

    def exchange(value, bits):
        for bit in bits:
            value = value + swap(value, "dp", dp, bit)
        return value

    power = dp & (dp - 1) == 0
    bits = [1 << n for n in range(dp.bit_length() - 1)] if power else []
    if near_blocks:
        attn_part = attn_sum[0]()
    packed = exchange(line.after(packed), bits[:1])
    wides = line.wait([wide[c] for wide in (wide_tok, wide_out) for c in order])
    for index, c in enumerate(order):
        put("tokens", F32, wides[index], c)
        put("output", BF, wides[len(order) + index], c)
    if near_blocks:
        (grad_w_fc1,) = fc1_sum[2](fc1_part, fc1_last)
        attn_last = attn_sum[1](attn_part)
    packed = exchange(line.after(packed), bits[1:]) if power else lax.psum(packed, "dp")
    if near_blocks:
        grad_w_out, grad_w_query, grad_w_key, grad_w_value = attn_sum[2](attn_part, attn_last)
    else:
        (grad_w_fc2,), (grad_w_fc1,) = fc2_sum(), fc1_sum()
        grad_w_out, grad_w_query, grad_w_key, grad_w_value = attn_sum()
    grad_tokens, output = grown["tokens"], grown["output"]

    last_row = packed[15]
    counted = packed[7, 0]
    squares = jnp.stack([jnp.sum(packed[5]), jnp.sum(packed[8]), jnp.sum(packed[9])])
    rms = jnp.sqrt(squares / (counted * width))
    grad_head = jnp.sum(last_row[2 * hw : 3 * hw].reshape(heads, HEAD_DIM), axis=1)
    return (
        output,
        grad_tokens,
        grad_w_query,
        grad_w_key,
        grad_w_value,
        grad_w_out,
        grad_w_fc1,
        grad_w_fc2,
        packed[10],
        packed[11],
        packed[2],
        packed[3],
        packed[0],
        packed[1],
        packed[12],
        packed[13],
        last_row[:hw],
        last_row[hw : 2 * hw],
        packed[4],
        packed[14],
        packed[6],
        grad_head,
        rms,
    )


def solution(mesh):
    cut = P(None, "tensor")
    part = P("tensor")
    rows = P("dp", None)
    both = P("dp", "tensor")
    return jax.shard_map(
        functools.partial(body, mesh.shape["dp"], mesh.shape["tensor"]),
        mesh=mesh,
        in_specs=(rows, rows) + (cut,) * 6 + (P(),) * 6 + (part,) * 4 + (P(), part, P(), part, rows),
        out_specs=(rows, rows) + (both,) * 6 + (P(),) * 6 + (part,) * 4 + (P(), part, P(), part, P()),
        check_vma=False,
    )
```

```python
import functools

import jax
import jax.numpy as jnp
from jax import lax
from jax.experimental import pallas as pl
from jax.experimental.pallas import tpu as pltpu
from jax.sharding import PartitionSpec as P

HEAD_DIM = 64
EPSILON = 1e-05
EXCLUDED = -1e30
LANES = 128
CHUNKS = 2
PAD = 16
BF = jnp.bfloat16
F32 = jnp.float32


def dot_nn(a, b):
    return lax.dot_general(a, b, (((1,), (0,)), ((), ())), preferred_element_type=F32)


def dot_nt(a, b):
    return lax.dot_general(a, b, (((1,), (1,)), ((), ())), preferred_element_type=F32)


def dot_tn(a, b):
    return lax.dot_general(a, b, (((0,), (0,)), ((), ())), preferred_element_type=F32)


def normalize(v):
    mean = jnp.mean(v, axis=-1, keepdims=True)
    centred = v - mean
    factor = lax.rsqrt(jnp.mean(centred * centred, axis=-1, keepdims=True) + EPSILON)
    return centred * factor, factor


def norm_back(scaled, normed, factor):
    return factor * (
        scaled
        - jnp.mean(scaled, axis=-1, keepdims=True)
        - normed * jnp.mean(scaled * normed, axis=-1, keepdims=True)
    )


def col_sum(v):
    return jnp.sum(v, axis=0, keepdims=True)


def tanh_inner(v):
    return 0.7978845608028654 * (v + 0.044715 * (v * v * v))


def columns_to_rows(columns):
    n = columns[0].shape[0]
    lane = lax.broadcasted_iota(jnp.int32, (n, LANES), 1)
    tile = jnp.zeros((n, LANES), F32)
    for index, column in enumerate(columns):
        tile = jnp.where(lane == index, column, tile)
    return jnp.transpose(tile)[:8]


def rows_to_columns(rows):
    n = rows[0].shape[1]
    sub = lax.broadcasted_iota(jnp.int32, (LANES, n), 0)
    tile = jnp.zeros((LANES, n), F32)
    for index, row in enumerate(rows):
        tile = jnp.where(sub == index, row, tile)
    tile = jnp.transpose(tile)
    return [tile[:, index : index + 1] for index in range(len(rows))]


def stack_rows(rows, width):
    sub = lax.broadcasted_iota(jnp.int32, (8, width), 0)
    tile = jnp.zeros((8, width), F32)
    for index, row in enumerate(rows):
        tile = jnp.where(sub == index, row, tile)
    return tile


def head_masks(width, kind):
    lane = lax.broadcasted_iota(jnp.int32, (1, width), 1) // HEAD_DIM
    return [(lane == head).astype(F32).astype(kind) for head in range(width // HEAD_DIM)]


def qkv_kernel(tok, gain, bias, wq, wk, wv, qb, vb, entry, q, k, v):
    normed, _ = normalize(tok[...].astype(F32))
    low = (normed * gain[...] + bias[...]).astype(BF)
    entry[...] = low
    q[...] = ((dot_nn(low, wq[...]) + qb[...]) * HEAD_DIM**-0.5).astype(BF)
    k[...] = dot_nn(low, wk[...]).astype(BF)
    v[...] = (dot_nn(low, wv[...]) + vb[...]).astype(BF)


def attend_kernel(first, block, place, q, k, v, segq, segk, scale, attended, low, mine, theirs, logsum, hold):
    rows, width = q.shape
    half = rows // 2
    masks = head_masks(width, BF)
    for at in range(0, rows, block):
        length = first + at + block
        query = q[at : at + block, :]
        keys = k[:length, :]
        (seg,) = rows_to_columns([segq[:, at : at + block].astype(F32)])
        place_q = first + at + lax.broadcasted_iota(jnp.int32, (block, length), 0)
        place_k = lax.broadcasted_iota(jnp.int32, (block, length), 1)
        allowed = (seg == segk[:, :length].astype(F32)) & (place_k <= place_q)
        shift = jnp.where(allowed, 0.0, EXCLUDED)
        total = jnp.zeros((block, width), F32)
        sums = []
        for mask in masks:
            scores = dot_nt(query * mask, keys) + shift
            top = jnp.max(scores, axis=-1, keepdims=True)
            expo = jnp.exp(scores - top)
            norm = jnp.sum(expo, axis=-1, keepdims=True)
            weights = (expo * (1.0 / norm)).astype(BF)
            total = total + dot_nn(weights, v[:length, :] * mask)
            sums.append(top + jnp.log(norm))
        attended[at : at + block, :] = total
        context = (total * scale[...]).astype(BF)
        low[at : at + block, :] = context
        hold[at : at + block, :] = context.astype(F32)
        logsum[:, at : at + block] = columns_to_rows(sums)
    mine[...] = hold[pl.ds(pl.multiple_of(place[0] * half, half), half), :]
    theirs[...] = hold[pl.ds(pl.multiple_of(place[1] * half, half), half), :]


def pack_kernel(wide, near_out, out_pair, fc1, fc2):
    width, units = near_out.shape[1], fc1.shape[1]
    out_pair[:, :width] = near_out[...]
    out_pair[:, width:] = wide[:, :width].astype(BF)
    fc1[...] = wide[:, width : width + units].astype(BF)
    fc2[...] = wide[:, width + units :].astype(BF)


def far_kernel(side, far_half, far_rest, diag_half, diag_rest, out):
    rows, width = far_half.shape
    here = pl.ds(pl.multiple_of(side[0] * rows, rows), rows)
    there = pl.ds(pl.multiple_of((1 - side[0]) * rows, rows), rows)
    out[here, :width] = far_half[...].astype(BF)
    out[there, :width] = far_rest[...].astype(BF)
    out[here, width:] = diag_half[...].astype(BF)
    out[there, width:] = diag_rest[...].astype(BF)


def upstream_kernel(place, cot, own, near, out):
    units = own.shape[1]
    out[:, :units] = dot_nn(cot[...], own[...])
    out[:, units:] = dot_nn(cot[...], near[...])


def forward_kernel(
    place, seg, ctx_chip, ctx_far, wo_chip, wo_far, out_bias, tok, post_gain, post_bias, ln2_gain, ln2_bias,
    fc1_own, fc1_near, fc1_bias, mid_gain, near, cot, grad_middle,
    mixed, stream, inner, share, hidden, stats, sums,
):
    units = fc1_own.shape[1]
    mix = (
        dot_nt(ctx_chip[...].astype(BF), wo_chip[...]) + dot_nt(ctx_far[...].astype(BF), wo_far[...])
    ) + out_bias[...]
    mixed[...] = mix
    normed, _ = normalize(mix)
    branch = normed * post_gain[...] + post_bias[...]
    resid = tok[...].astype(F32) + branch
    stream[...] = resid
    normed2, _ = normalize(resid)
    low = (normed2 * ln2_gain[...] + ln2_bias[...]).astype(BF)
    inner[...] = low
    share[...] = low.astype(F32)
    actives, scaleds = [], []
    for part, (weight, bias, gain) in enumerate(
        ((fc1_own, fc1_bias[...], mid_gain[...]), (fc1_near, near[0:1, :], near[1:2, :]))
    ):
        hid = dot_nn(low, weight[...]) + bias
        hidden[:, part * units : (part + 1) * units] = hid
        actives.append(0.5 * hid * (1.0 + jnp.tanh(tanh_inner(hid))))
        scaleds.append(grad_middle[:, part * units : (part + 1) * units] * gain)

    def both(left, right):
        return jnp.sum(left, axis=-1, keepdims=True) + jnp.sum(right, axis=-1, keepdims=True)

    mean = both(*actives) / (2 * units)
    centred = [active - mean for active in actives]
    stats[...] = columns_to_rows(
        [
            mean,
            both(*[c * c for c in centred]),
            both(*scaleds),
            both(*[s * c for s, c in zip(scaleds, centred)]),
        ]
    )
    (which,) = rows_to_columns([seg[...].astype(F32)])
    valid = (which >= 0).astype(F32)
    sums[...] = stack_rows(
        [
            col_sum(valid * branch * branch),
            col_sum(cot[...].astype(F32)),
            col_sum(valid * jnp.ones_like(branch)),
        ],
        branch.shape[1],
    )


def middle_kernel(
    total, hidden, grad_middle, st0, st1, mid_gain, mid_bias, near,
    fc1_own, fc1_near, fc2_own, fc2_near,
    middle, grad_hidden, share, ffn, back, sums_own, sums_near,
):
    units = fc1_own.shape[1]
    n = 2 * units
    mean = (st0[0:1, :] + st1[0:1, :]) * 0.5
    apart = [s[0:1, :] - mean for s in (st0, st1)]
    spread = (st0[1:2, :] + n * (apart[0] * apart[0])) + (st1[1:2, :] + n * (apart[1] * apart[1]))
    factor = lax.rsqrt(spread / total + EPSILON)
    plain = (st0[2:3, :] + st1[2:3, :]) / total
    along = (st0[3:4, :] + apart[0] * st0[2:3, :]) + (st1[3:4, :] + apart[1] * st1[2:3, :])
    mean, factor, plain, along = rows_to_columns([mean, factor, plain, factor * along / total])
    parts = (
        (mid_gain[...], mid_bias[...], fc1_own, fc2_own, sums_own),
        (near[1:2, :], near[2:3, :], fc1_near, fc2_near, sums_near),
    )
    ffn_parts, back_parts = [], []
    for part, (gain, bias, fc1, fc2, sums) in enumerate(parts):
        hid = hidden[:, part * units : (part + 1) * units]
        bend = jnp.tanh(tanh_inner(hid))
        active = 0.5 * hid * (1.0 + bend)
        slope = 0.5 * (1.0 + bend) + 0.5 * hid * (1.0 - bend * bend) * (
            0.7978845608028654 * (1.0 + 3 * 0.044715 * (hid * hid))
        )
        normed = (active - mean) * factor
        mid = (normed * gain + bias).astype(BF)
        grad = grad_middle[:, part * units : (part + 1) * units]
        low = (factor * (grad * gain - plain - normed * along) * slope).astype(BF)
        if part == 0:
            middle[...] = mid
            grad_hidden[...] = low
        else:
            share[:, :units] = mid.astype(F32)
            share[:, units:] = low.astype(F32)
        sums[...] = stack_rows([col_sum(grad * normed), col_sum(grad), col_sum(low.astype(F32))], units)
        ffn_parts.append(dot_nt(mid, fc2[...]))
        back_parts.append(dot_nt(low, fc1[...]))
    ffn[...] = ffn_parts[0] + ffn_parts[1]
    back[: hidden.shape[0], :] = back_parts[0] + back_parts[1]
    back[hidden.shape[0] :, :] = jnp.zeros((PAD, back.shape[1]), F32)


def stream_kernel(
    place, mine, far, mixed, stream, cot, ln2_gain, post_gain, w_out,
    grad_stream, grad_mixed, wide, context_own, context_near, sums,
):
    grad = mine[: stream.shape[0], :] + far[: stream.shape[0], :]
    normed2, factor2 = normalize(stream[...])
    back = cot[...].astype(F32) + norm_back(grad * ln2_gain[...], normed2, factor2)
    grad_stream[...] = back
    normedp, factorp = normalize(mixed[...])
    low = norm_back(back * post_gain[...], normedp, factorp).astype(BF)
    grad_mixed[...] = low
    wide[...] = low.astype(F32)
    context = dot_nn(low, w_out[...])
    width = context_own.shape[1]
    context_own[...] = context[:, :width]
    context_near[...] = context[:, width:]
    sums[...] = stack_rows(
        [
            col_sum(grad * normed2),
            col_sum(grad),
            col_sum(back * normedp),
            col_sum(back),
            col_sum(low.astype(F32)),
        ],
        back.shape[1],
    )


def attend_back_kernel(first, block, last, place, *refs):
    q, k, v, segq, segk, context_own, context_near, attended, scale, logsum = refs[:10]
    rest = list(refs[10:])
    if not last:
        key_in, value_in = rest[:2]
        rest = rest[2:]
    grad_q, grad_k, grad_v, sums = rest[:4]
    rest = rest[4:]
    if first:
        key_out, value_out = rest[:2]
        rest = rest[2:]
    key_sum, value_sum, low_probs, low_scores, grads = rest
    rows, width = q.shape
    half = rows // 2
    end = first + rows
    masks = head_masks(width, BF)
    wide_masks = head_masks(width, F32)
    if last:
        key_sum[...] = jnp.zeros_like(key_sum)
        value_sum[...] = jnp.zeros_like(value_sum)
    else:
        key_sum[...] = key_in[...]
        value_sum[...] = value_in[...]
    head_sum = jnp.zeros((1, width), F32)
    for part, source in enumerate((context_own, context_near)):
        at = pl.ds(pl.multiple_of(place[part] * half, half), half)
        grad_context = source[...]
        head_sum = head_sum + col_sum(grad_context * attended[at, :])
        grads[at, :] = (grad_context * scale[...]).astype(BF)
    (seg,) = rows_to_columns([segk[:, :end].astype(F32)])
    query_sum = jnp.zeros((1, width), F32)
    for at in range(0, rows, block):
        length = first + at + block
        query = q[at : at + block, :]
        grad = grads[at : at + block, :]
        product = grad.astype(F32) * attended[at : at + block, :]
        delta = columns_to_rows([jnp.sum(product * mask, axis=-1, keepdims=True) for mask in wide_masks])
        place_k = lax.broadcasted_iota(jnp.int32, (length, block), 0)
        place_q = first + at + lax.broadcasted_iota(jnp.int32, (length, block), 1)
        allowed = (seg[:length] == segq[:, at : at + block].astype(F32)) & (place_k <= place_q)
        shift = jnp.where(allowed, 0.0, EXCLUDED)
        queries = [query * mask for mask in masks]
        grad_parts = [grad * mask for mask in masks]
        grad_query = jnp.zeros((block, width), F32)
        for head, mask in enumerate(masks):
            scores = dot_nt(k[:length, :], queries[head]) + shift
            probs = jnp.exp(scores - logsum[head : head + 1, at : at + block])
            low_probs[:length, head * block : (head + 1) * block] = probs.astype(BF)
            grad_probs = dot_nt(v[:length, :], grad_parts[head])
            low = (probs * (grad_probs - delta[head : head + 1, :])).astype(BF)
            low_scores[:length, head * block : (head + 1) * block] = low
            grad_query = grad_query + dot_tn(low, k[:length, :] * mask)
        value_sum[:length, :] += dot_nn(low_probs[:length, :], jnp.concatenate(grad_parts, axis=0))
        key_sum[:length, :] += dot_nn(low_scores[:length, :], jnp.concatenate(queries, axis=0))
        low_query = (grad_query * HEAD_DIM**-0.5).astype(BF)
        grad_q[at : at + block, :] = low_query
        query_sum = query_sum + col_sum(low_query.astype(F32))
    grad_k[...] = key_sum[first:end, :].astype(BF)
    low_value = value_sum[first:end, :].astype(BF)
    grad_v[...] = low_value
    sums[...] = stack_rows([query_sum, col_sum(low_value.astype(F32)), head_sum], width)
    if first:
        key_out[...] = key_sum[:first, :]
        value_out[...] = value_sum[:first, :]


def entry_kernel(place, grad_q, grad_k, grad_v, wq, wk, wv, tok, *refs):
    sends, (keep, sums) = refs[:-2], refs[-2:]
    step = pl.program_id(0)
    part = dot_nt(grad_q[...], wq[...]) + dot_nt(grad_k[...], wk[...]) + dot_nt(grad_v[...], wv[...])
    normed, _ = normalize(tok[...].astype(F32))
    fresh = stack_rows([col_sum(part * normed), col_sum(part)], part.shape[1])

    @pl.when(step == 0)
    def _():
        sums[...] = fresh
        cut = sends[0].shape[1]
        for j, send in enumerate(sends):
            send[...] = part[:, j * cut : (j + 1) * cut]

    @pl.when(step != 0)
    def _():
        sums[...] += fresh
        keep[...] = part


def chip_kernel(keep, *refs):
    gots, out = refs[:-1], refs[-1]
    cut = gots[0].shape[1]
    for j, got in enumerate(gots):
        out[:, j * cut : (j + 1) * cut] = keep[:, j * cut : (j + 1) * cut] + got[...]


def token_kernel(place, mine, far, tok, grad_stream, gain, *refs):
    out, wide = refs[-2:]
    normed, factor = normalize(tok[...].astype(F32))
    grad = grad_stream[...] + norm_back((mine[...] + far[...]) * gain[...], normed, factor)
    out[...] = grad
    wide[...] = grad


def output_kernel(place, mine, far, stream, bias, seg, *refs):
    out, wide, sums = refs[-3:]
    ffn = (mine[...] + far[...]) + bias[...]
    result = stream[...] + ffn
    low = result.astype(BF)
    out[...] = low
    wide[...] = low.astype(F32)
    (which,) = rows_to_columns([seg[...].astype(F32)])
    valid = (which >= 0).astype(F32)
    sums[...] = stack_rows([col_sum(valid * ffn * ffn), col_sum(valid * result * result)], ffn.shape[1])


def put_kernel(place, value, full, out):
    out[...] = value[...].astype(out.dtype)


def line_kernel(kind, chunks, half, place, *refs):
    items, out = refs[:-1], refs[-1]
    for c in range(chunks):
        if kind == "chunks":
            out[2 * c * half : 2 * (c + 1) * half, :] = items[c][...]
        else:
            for part in range(2):
                at = pl.ds(pl.multiple_of((2 * c + place[part]) * half, half), half)
                out[at, :] = items[2 * c + part][...].astype(BF)


def weight_kernel(plan, chunks, half, blocks, place, *refs):
    step = pl.program_id(0)
    refs = list(refs)
    count = {"all": 1, "halves": 2 * chunks, "chunks": chunks}
    sources = [[(kind, [refs.pop(0) for _ in range(count[kind])]) for kind in product] for product in plan]
    send, keep = refs[:2]
    holds = refs[2:]
    depth = send.shape[0]
    operands, fills = [], []
    for product in sources:
        row = []
        for kind, items in product:
            if kind == "all":
                row.append(items[0])
            else:
                hold = holds.pop(0)
                fills.append((kind, items, hold))
                row.append(hold)
        operands.append(row)

    @pl.when(step == 0)
    def _():
        for kind, items, hold in fills:
            line_kernel(kind, chunks, half, place, *items, hold)

    def fill(target):
        offset = 0
        for row in operands:
            left = row[0]
            columns = jnp.concatenate(
                [
                    left[:, pl.ds(pl.multiple_of(blocks[step * depth + j] * LANES, LANES), LANES)]
                    for j in range(depth)
                ],
                axis=1,
            )
            for right in row[1:]:
                total = dot_tn(columns, right[...])
                width = total.shape[1]
                target[:, :, offset : offset + width] = total.reshape(depth, LANES, width)
                offset += width

    @pl.when(step == 0)
    def _():
        fill(send)

    @pl.when(step != 0)
    def _():
        fill(keep)


def first_kernel(keep, got, out):
    out[...] = keep[...] + got[...]


def second_kernel(keep, got, near, out):
    out[...] = (keep[0] + got[0]) + near[0]


def third_kernel(keep, got, near, far, *outs):
    at = 0
    for out in outs:
        cut = slice(at, at + out.shape[1])
        out[...] = ((keep[0, :, cut] + got[0, :, cut]) + near[0, :, cut]) + far[:, cut]
        at += out.shape[1]


def whole(array):
    shape = array.shape
    return (array, shape, lambda *_: (0,) * len(shape))


def swap(value, axis, size, bit):
    return lax.ppermute(value, axis, [(i, i ^ bit) for i in range(size)])


class Order:
    def __init__(self):
        self.last = None

    def after(self, value):
        if self.last is None:
            return value
        return lax.optimization_barrier((value, self.last))[0]

    def keep(self, value):
        self.last = value
        return value

    def wait(self, values):
        tied = lax.optimization_barrier((tuple(values), self.last))
        self.last = tied[1]
        return list(tied[0])

    def call(self, kernel, grid, ins, outs, prefetch=(), scratch=(), aliases=None, vmem=16 << 20, name=None):
        arrays = [item[0] for item in ins]
        specs = [
            pl.BlockSpec(memory_space=pl.ANY) if block is None else pl.BlockSpec(block, place)
            for _, block, place in ins
        ]
        body_of = kernel
        if self.last is not None:
            at = len(prefetch) + len(arrays)
            arrays.append(self.last)
            specs.append(pl.BlockSpec(memory_space=pl.ANY))

            def body_of(*refs):
                return kernel(*refs[:at], *refs[at + 1 :])

        results = pl.pallas_call(
            body_of,
            grid_spec=pltpu.PrefetchScalarGridSpec(
                num_scalar_prefetch=len(prefetch),
                grid=grid,
                in_specs=specs,
                out_specs=[pl.BlockSpec(block, place) for _, _, block, place in outs],
                scratch_shapes=list(scratch),
            ),
            out_shape=[jax.ShapeDtypeStruct(shape, kind) for shape, kind, _, _ in outs],
            input_output_aliases=aliases or {},
            compiler_params=pltpu.CompilerParams(
                dimension_semantics=("arbitrary",) * len(grid), vmem_limit_bytes=vmem
            ),
            cost_estimate=pl.CostEstimate(flops=1000, bytes_accessed=1000, transcendentals=0),
            name=name,
        )(*prefetch, *arrays)
        self.last = min(results, key=lambda r: r.size)
        return results


def body(
    dp, tp, tokens, segments, w_query, w_key, w_value, w_out, w_fc1, w_fc2, ln1_gain, ln1_bias, post_gain, post_bias,
    ln2_gain, ln2_bias, mid_gain, mid_bias, query_bias, value_bias, out_bias, fc1_bias, fc2_bias, head_scale, cotangent,
):
    rows, width = tokens.shape
    hw = w_query.shape[1]
    units = w_fc1.shape[1]
    heads = hw // HEAD_DIM
    size = rows // CHUNKS
    half = size // 2
    block = min(256, size)
    line = Order()
    call = line.call
    row = lambda v: v.reshape(1, -1)
    seg = segments.reshape(1, rows)
    ln1_g, ln1_b, post_g, post_b = row(ln1_gain), row(ln1_bias), row(post_gain), row(post_bias)
    ln2_g, ln2_b, mid_g, mid_b = row(ln2_gain), row(ln2_bias), row(mid_gain), row(mid_bias)
    q_b, v_b, out_b, fc1_b, fc2_b = row(query_bias), row(value_bias), row(out_bias), row(fc1_bias), row(fc2_bias)
    scale = row(jnp.repeat(head_scale, HEAD_DIM))
    core = lax.axis_index("tensor") & 1
    place = (core + jnp.arange(2, dtype=jnp.int32)) & 1
    dp_side = lax.axis_index("dp") & 1
    side = dp_side.astype(jnp.int32).reshape(1)
    chunks = list(range(CHUNKS))
    order = chunks[::-1]

    half_rows = width // 2
    part = lax.dynamic_slice_in_dim(w_out, dp_side * half_rows, half_rows, 0).astype(F32)
    far_half = swap(part, "tensor", tp, 2)
    wide = swap(jnp.concatenate([w_out, w_fc1, w_fc2], 1).astype(F32), "tensor", tp, 1)
    pad = jnp.zeros((5, units), F32)
    near = swap(jnp.concatenate([fc1_b, mid_g, mid_b, pad], 0), "tensor", tp, 1)

    step = min(256, rows)
    entry, query, keys, values = call(
        qkv_kernel,
        (rows // step,),
        [(tokens, (step, width), lambda i: (i, 0))]
        + [whole(a) for a in (ln1_g, ln1_b, w_query, w_key, w_value, q_b, v_b)],
        [((rows, width), BF, (step, width), lambda i: (i, 0))]
        + [((rows, hw), BF, (step, hw), lambda i: (i, 0))] * 3,
        name="qkv",
    )

    at0 = lambda c: (lambda *_: (c, 0))
    at1 = lambda c: (lambda *_: (0, c))
    fix = lambda shape, kind: (shape, kind, shape, lambda *_: (0,) * len(shape))
    own = lambda a, c: (a, (half, a.shape[1]), lambda i, p, c=c: (2 * c + p[0], 0))
    own_seg = lambda c: (seg, (1, half), lambda i, p, c=c: (0, 2 * c + p[0]))

    (far_half,) = line.wait([far_half])
    far_rest = swap(far_half, "dp", dp, 1)
    attended, low_ctx, ctx, logsum = {}, {}, {}, {}
    for c in order:
        end = (c + 1) * size
        attended[c], low_ctx[c], mine, theirs, logsum[c] = call(
            functools.partial(attend_kernel, c * size, block),
            (1,),
            [
                (query, (size, hw), at0(c)),
                (keys, (end, hw), at0(0)),
                (values, (end, hw), at0(0)),
                (seg, (1, size), at1(c)),
                (seg, (1, end), at1(0)),
                whole(scale),
            ],
            [fix((size, hw), F32), fix((size, hw), BF), fix((half, hw), F32), fix((half, hw), F32), fix((8, size), F32)],
            prefetch=(place,),
            scratch=[pltpu.VMEM((size, hw), F32)],
            name="attend",
        )
        ctx[c] = (mine, swap(theirs, "tensor", tp, 1))
    far_ctx = {}
    for c in order:
        mine, got = ctx[c]
        ctx[c] = line.keep(jnp.concatenate([line.after(mine), got], 1))
        far_ctx[c] = swap(ctx[c], "tensor", tp, 2)

    step = min(256, width)
    wo_chip, fc1_near, fc2_near = call(
        pack_kernel,
        (width // step,),
        [(a, (step, a.shape[1]), lambda i: (i, 0)) for a in (wide, w_out)],
        [((width, n), BF, (step, n), lambda i: (i, 0)) for n in (2 * hw, units, units)],
        name="pack",
    )
    diag_half = swap(far_half, "tensor", tp, 1)
    diag_rest = swap(far_rest, "tensor", tp, 1)
    (grad_mid,) = call(
        upstream_kernel,
        (CHUNKS,),
        [(cotangent, (half, width), lambda i, p: (2 * i + p[0], 0)), whole(w_fc2), whole(fc2_near)],
        [((CHUNKS * half, 2 * units), F32, (half, 2 * units), lambda i, p: (i, 0))],
        prefetch=(place,),
        name="upstream",
    )
    (wo_far,) = call(
        far_kernel,
        (1,),
        [whole(a) for a in (far_half, far_rest, diag_half, diag_rest)],
        [fix((width, 2 * hw), BF)],
        prefetch=(side,),
        name="far",
    )

    mixed, stream, inner, hidden, stats, far_stats, fsums, near_inner = {}, {}, {}, {}, {}, {}, {}, {}
    for c in order:
        mixed[c], stream[c], inner[c], share, hidden[c], stats[c], fsums[c] = call(
            forward_kernel,
            (1,),
            [own_seg(c)]
            + [whole(a) for a in (ctx[c], far_ctx[c], wo_chip, wo_far, out_b)]
            + [own(tokens, c)]
            + [whole(a) for a in (post_g, post_b, ln2_g, ln2_b, w_fc1, fc1_near, fc1_b, mid_g, near)]
            + [own(cotangent, c), (grad_mid, (half, 2 * units), at0(c))],
            [fix((half, width), F32)] * 2
            + [fix((half, width), BF), fix((half, width), F32), fix((half, 2 * units), F32)]
            + [fix((8, half), F32), fix((8, width), F32)],
            prefetch=(place,),
            name="forward",
        )
        far_stats[c] = swap(stats[c], "tensor", tp, 2)
        near_inner[c] = swap(share, "tensor", tp, 1)

    middle, grad_hid, ffn, back, far_back, gsums, nsums = {}, {}, {}, {}, {}, {}, {}
    near_mid, near_hid = {}, {}
    for c in order:
        mid, hid, share, ffn[c], back[c], gsums[c], nsums[c] = call(
            functools.partial(middle_kernel, units * tp),
            (1,),
            [whole(hidden[c]), (grad_mid, (half, 2 * units), at0(c))]
            + [whole(a) for a in (stats[c], far_stats[c], mid_g, mid_b, near)]
            + [whole(a) for a in (w_fc1, fc1_near, w_fc2, fc2_near)],
            [fix((half, units), BF)] * 2
            + [fix((half, 2 * units), F32)]
            + [fix((half, width), F32), fix((half + PAD, width), F32)]
            + [fix((8, units), F32)] * 2,
            name="middle",
        )
        middle[c], grad_hid[c] = mid, hid
        far_back[c] = swap(back[c], "tensor", tp, 2)
        near_both = swap(share, "tensor", tp, 1)
        near_mid[c] = (near_both, (half, units), lambda *_: (0, 0))
        near_hid[c] = (near_both, (half, units), lambda *_: (0, 1))

    near_blocks = width // dp == LANES and dp == 8
    if near_blocks:
        depth = dp // 2
        me = lax.axis_index("dp")
        slot = jnp.arange(dp, dtype=jnp.int32)
        ring = me // 2
        at_ring = jnp.stack([depth - 1 - (ring ^ 1), ring ^ 1, depth - 1 - ring, ring] * 2)
        opposite = [(i, dp - 2 - i + 2 * (i & 1)) for i in range(dp)]
        blocks = (2 * at_ring + ((me + 1 + slot // depth) & 1)).astype(jnp.int32)

    def weight(plan, items, columns, name):
        arrays = [item for group in items for operand in group for item in operand]
        kinds = [kind for product in plan for kind in product]
        holds = [
            pltpu.VMEM((rows, operand[0][1][1]), BF)
            for kind, operand in zip(kinds, [o for g in items for o in g])
            if kind != "all"
        ]
        if not near_blocks:
            results = []
            for product, group in zip(plan, items):
                full = []
                for kind, operand in zip(product, group):
                    if kind == "all":
                        full.append(operand[0][0])
                        continue
                    n = operand[0][1][1]
                    (lined,) = call(
                        functools.partial(line_kernel, kind, CHUNKS, half),
                        (1,),
                        operand,
                        [fix((rows, n), BF)],
                        prefetch=(place,),
                        name=name,
                    )
                    full.append(lined)
                results += [
                    lax.psum_scatter(dot_tn(full[0], right), "dp", scatter_dimension=0, tiled=True)
                    for right in full[1:]
                ]
            return lambda: results
        send, keep = call(
            functools.partial(weight_kernel, plan, CHUNKS, half),
            (2,),
            arrays,
            [fix((depth, LANES, columns), F32)] * 2,
            prefetch=(blocks, place),
            scratch=holds,
            name=name,
        )
        got = swap(send, "dp", dp, 1)

        lanes = min(1024, columns)
        by_lanes = lambda array, count, first: (array, (count, LANES, lanes), lambda i: (first, 0, i))

        def first():
            (send,) = call(
                first_kernel,
                (columns // lanes,),
                [by_lanes(a, 2, 0) for a in (keep, got)],
                [((2, LANES, columns), F32, (2, LANES, lanes), lambda i: (0, 0, i))],
                name="first",
            )
            return swap(send, "dp", dp, 2)

        def second(near):
            (send,) = call(
                second_kernel,
                (columns // lanes,),
                [by_lanes(a, 1, 2) for a in (keep, got)] + [by_lanes(near, 1, 0)],
                [((LANES, columns), F32, (LANES, lanes), lambda i: (0, i))],
                name="second",
            )
            return lax.ppermute(send, "dp", opposite)

        def third(near, far):
            return call(
                third_kernel,
                (1,),
                [(a, (1, LANES, columns), lambda *_, f=f: (f, 0, 0)) for a, f in ((keep, 3), (got, 3), (near, 1))]
                + [whole(far)],
                [fix((LANES, operand[0][1][1]), F32) for group in items for operand in group[1:]],
                name="third",
            )

        return first, second, third

    halves = lambda mine, wide_near: [item for c in chunks for item in (whole(mine[c]), wide_near[c])]
    fc2_sum = weight(
        [("all", "halves")],
        [[[whole(cotangent)], halves(middle, near_mid)]],
        units,
        "weight_fc2",
    )
    fc1_sum = weight(
        [("halves", "halves")],
        [
            [
                halves(inner, {c: whole(near_inner[c]) for c in chunks}),
                halves(grad_hid, near_hid),
            ]
        ],
        units,
        "weight_fc1",
    )

    own_out = lambda kind, c: ((rows, width), kind, (half, width), lambda i, p, c=c: (2 * c + p[0], 0))
    grown = {"tokens": None, "output": None}

    def grow(which, ins, outs, kernel):
        aliases = None
        if grown[which] is not None:
            aliases = {1 + len(ins): 0}
            ins = ins + [(grown[which], None, None)]
        results = call(kernel, (1,), ins, outs, prefetch=(place,), aliases=aliases, name=which)
        grown[which] = results[0]
        return results[1:]

    def put(which, kind, value, c):
        grow(which, [whole(value)], [((rows, width), kind, (half, width), lambda i, p: (2 * c + p[1], 0))], put_kernel)

    def token(c):
        ins = [(a, (half, width), at0(0)) for a in (chip[c], far_chip[c])]
        ins += [own(tokens, c), whole(grad_stream[c]), whole(ln1_g)]
        (value,) = grow("tokens", ins, [own_out(F32, c), fix((half, width), F32)], token_kernel)
        return swap(value, "tensor", tp, 1)

    def result(c):
        ins = [whole(ffn[c]), whole(far_ffn[c]), whole(stream[c]), whole(fc2_b), own_seg(c)]
        value, osums[c] = grow(
            "output", ins, [own_out(BF, c), fix((half, width), F32), fix((8, width), F32)], output_kernel
        )
        return swap(value, "tensor", tp, 1)

    grad_stream, grad_mix, near_mix, grad_q, grad_k, grad_v, chip, far_chip = {}, {}, {}, {}, {}, {}, {}, {}
    hsums, qsums, esums, far_ffn = {}, {}, {}, {}
    osums, wide_tok, wide_out = {}, {}, {}
    carry = None
    fc2_part = fc1_part = attn_part = None
    for c in order:
        end = (c + 1) * size
        last = c == CHUNKS - 1
        by_half = lambda a: (a, (half, a.shape[1]), lambda i, p: (p[1 - i], 0))
        grad_stream[c], grad_mix[c], wide_mix, ctx_own, ctx_near, hsums[c] = call(
            stream_kernel,
            (1,),
            [whole(a) for a in (back[c], far_back[c], mixed[c], stream[c])]
            + [own(cotangent, c), whole(ln2_g), whole(post_g), whole(wo_chip)],
            [fix((half, width), F32), fix((half, width), BF), fix((half, width), F32)]
            + [fix((half, hw), F32)] * 2
            + [fix((8, width), F32)],
            prefetch=(place,),
            name="stream",
        )
        ctx_near = swap(ctx_near, "tensor", tp, 1)
        near_mix[c] = swap(wide_mix, "tensor", tp, 1)
        results = call(
            functools.partial(attend_back_kernel, c * size, block, last),
            (1,),
            [
                (query, (size, hw), at0(c)),
                (keys, (end, hw), at0(0)),
                (values, (end, hw), at0(0)),
                (seg, (1, size), at1(c)),
                (seg, (1, end), at1(0)),
            ]
            + [whole(a) for a in (ctx_own, ctx_near, attended[c], scale, logsum[c])]
            + ([] if last else [whole(a) for a in carry]),
            [fix((size, hw), BF)] * 3 + [fix((8, hw), F32)] + ([fix((c * size, hw), F32)] * 2 if c else []),
            prefetch=(place,),
            scratch=[pltpu.VMEM((end, hw), F32)] * 2
            + [pltpu.VMEM((end, heads * block), BF)] * 2
            + [pltpu.VMEM((size, hw), BF)],
            name="attend_back",
        )
        grad_q[c], grad_k[c], grad_v[c], qsums[c] = results[:4]
        carry = results[4:]
        if c == order[-1] and near_blocks:
            fc2_part = fc2_sum[0]()
        count = 1 if c == order[-1] else 2
        *sends, keep, esums[c] = call(
            entry_kernel,
            (2,),
            [by_half(a) for a in (grad_q[c], grad_k[c], grad_v[c])]
            + [whole(a) for a in (w_query, w_key, w_value)]
            + [(tokens, (half, width), lambda i, p, c=c: (2 * c + p[1 - i], 0))],
            [fix((half, width // count), F32)] * count + [fix((half, width), F32), fix((8, width), F32)],
            prefetch=(place,),
            name="entry",
        )
        gots = [swap(send, "tensor", tp, 1) for send in sends]
        if c == order[-1]:
            for d in order[:-1]:
                far_ffn[d] = swap(ffn[d], "tensor", tp, 2)
                wide_out[d] = result(d)
            far_ffn[c] = swap(line.after(ffn[c]), "tensor", tp, 2)
        (chip[c],) = call(
            chip_kernel,
            (1,),
            [whole(a) for a in (keep, *gots)],
            [fix((half, width), F32)],
            name="chip",
        )
        far_chip[c] = swap(chip[c], "tensor", tp, 2)

    attn_sum = weight(
        [("halves", "chunks"), ("all", "chunks", "chunks", "chunks")],
        [
            [
                halves(grad_mix, {c: whole(near_mix[c]) for c in chunks}),
                [whole(low_ctx[c]) for c in chunks],
            ],
            [[whole(entry)]] + [[whole(g[c]) for c in chunks] for g in (grad_q, grad_k, grad_v)],
        ],
        4 * hw,
        "weight_attn",
    )
    for c in order[:-1]:
        wide_tok[c] = token(c)
    last = order[-1]
    if near_blocks:
        fc2_last = fc2_sum[1](fc2_part)
        fc1_part = fc1_sum[0]()
        (grad_w_fc2,) = fc2_sum[2](fc2_part, fc2_last)
    wide_out[last] = result(last)
    if near_blocks:
        fc1_last = fc1_sum[1](fc1_part)

    add = lambda parts: functools.reduce(lambda a, b: a + b, [parts[c] for c in chunks])
    fs, gs, ns, hs, qs, es, os = (add(p) for p in (fsums, gsums, nsums, hsums, qsums, esums, osums))
    own_part = jnp.concatenate([hs[:5], fs[:3], os[:2], es[:2], gs[:3]], 0)
    near_part = jnp.concatenate([hs[:5], fs[:3], os[:2], es[:2], ns[:3]], 0)
    packed = own_part + swap(near_part, "tensor", tp, 1)
    far = swap(packed[10:12], "tensor", tp, 2)
    tail = jnp.concatenate([qs[0], qs[1], qs[2], qs[2]]).reshape(1, -1)[:, :width]
    packed = jnp.concatenate([packed[:10], packed[10:12] + far, packed[12:], tail], 0)
    wide_tok[last] = token(last)
    line.keep(packed)

    if near_blocks:
        attn_part = attn_sum[0]()
        packed = line.after(packed)
        packed = packed + swap(packed, "dp", dp, 1)
        packed = packed + swap(packed, "dp", dp, 2)
    else:
        packed = lax.psum(packed, "dp")
    wides = line.wait([wide[c] for wide in (wide_tok, wide_out) for c in order])
    for index, c in enumerate(order):
        put("tokens", F32, wides[index], c)
        put("output", BF, wides[len(order) + index], c)
    if near_blocks:
        (grad_w_fc1,) = fc1_sum[2](fc1_part, fc1_last)
        packed = line.keep(line.after(packed))
        attn_last = attn_sum[1](attn_part)
        packed = line.after(packed)
        packed = packed + lax.ppermute(packed, "dp", opposite)
        grad_w_out, grad_w_query, grad_w_key, grad_w_value = attn_sum[2](attn_part, attn_last)
    else:
        (grad_w_fc2,), (grad_w_fc1,) = fc2_sum(), fc1_sum()
        grad_w_out, grad_w_query, grad_w_key, grad_w_value = attn_sum()
    grad_tokens, output = grown["tokens"], grown["output"]

    last_row = packed[15]
    counted = packed[7, 0]
    squares = jnp.stack([jnp.sum(packed[5]), jnp.sum(packed[8]), jnp.sum(packed[9])])
    rms = jnp.sqrt(squares / (counted * width))
    grad_head = jnp.sum(last_row[2 * hw : 3 * hw].reshape(heads, HEAD_DIM), axis=1)
    return (
        output,
        grad_tokens,
        grad_w_query,
        grad_w_key,
        grad_w_value,
        grad_w_out,
        grad_w_fc1,
        grad_w_fc2,
        packed[10],
        packed[11],
        packed[2],
        packed[3],
        packed[0],
        packed[1],
        packed[12],
        packed[13],
        last_row[:hw],
        last_row[hw : 2 * hw],
        packed[4],
        packed[14],
        packed[6],
        grad_head,
        rms,
    )


def solution(mesh):
    cut = P(None, "tensor")
    part = P("tensor")
    rows = P("dp", None)
    both = P("dp", "tensor")
    return jax.shard_map(
        functools.partial(body, mesh.shape["dp"], mesh.shape["tensor"]),
        mesh=mesh,
        in_specs=(rows, rows) + (cut,) * 6 + (P(),) * 6 + (part,) * 4 + (P(), part, P(), part, rows),
        out_specs=(rows, rows) + (both,) * 6 + (P(),) * 6 + (part,) * 4 + (P(), part, P(), part, P()),
        check_vma=False,
    )
```

```python
import functools

import jax
import jax.numpy as jnp
from jax import lax
from jax.experimental import pallas as pl
from jax.experimental.pallas import tpu as pltpu
from jax.sharding import PartitionSpec as P

HEAD_DIM = 64
EPSILON = 1e-05
EXCLUDED = -1e30
LANES = 128
CHUNKS = 2
PAD = 16
BF = jnp.bfloat16
F32 = jnp.float32


def dot_nn(a, b):
    return lax.dot_general(a, b, (((1,), (0,)), ((), ())), preferred_element_type=F32)


def dot_nt(a, b):
    return lax.dot_general(a, b, (((1,), (1,)), ((), ())), preferred_element_type=F32)


def dot_tn(a, b):
    return lax.dot_general(a, b, (((0,), (0,)), ((), ())), preferred_element_type=F32)


def normalize(v):
    mean = jnp.mean(v, axis=-1, keepdims=True)
    centred = v - mean
    factor = lax.rsqrt(jnp.mean(centred * centred, axis=-1, keepdims=True) + EPSILON)
    return centred * factor, factor


def norm_back(scaled, normed, factor):
    return factor * (
        scaled
        - jnp.mean(scaled, axis=-1, keepdims=True)
        - normed * jnp.mean(scaled * normed, axis=-1, keepdims=True)
    )


def col_sum(v):
    return jnp.sum(v, axis=0, keepdims=True)


def tanh_inner(v):
    return 0.7978845608028654 * (v + 0.044715 * (v * v * v))


def columns_to_rows(columns):
    n = columns[0].shape[0]
    lane = lax.broadcasted_iota(jnp.int32, (n, LANES), 1)
    tile = jnp.zeros((n, LANES), F32)
    for index, column in enumerate(columns):
        tile = jnp.where(lane == index, column, tile)
    return jnp.transpose(tile)[:8]


def rows_to_columns(rows):
    n = rows[0].shape[1]
    sub = lax.broadcasted_iota(jnp.int32, (LANES, n), 0)
    tile = jnp.zeros((LANES, n), F32)
    for index, row in enumerate(rows):
        tile = jnp.where(sub == index, row, tile)
    tile = jnp.transpose(tile)
    return [tile[:, index : index + 1] for index in range(len(rows))]


def stack_rows(rows, width):
    sub = lax.broadcasted_iota(jnp.int32, (8, width), 0)
    tile = jnp.zeros((8, width), F32)
    for index, row in enumerate(rows):
        tile = jnp.where(sub == index, row, tile)
    return tile


def head_masks(width, kind):
    lane = lax.broadcasted_iota(jnp.int32, (1, width), 1) // HEAD_DIM
    return [(lane == head).astype(F32).astype(kind) for head in range(width // HEAD_DIM)]


def qkv_kernel(tok, gain, bias, wq, wk, wv, qb, vb, entry, q, k, v):
    normed, _ = normalize(tok[...].astype(F32))
    low = (normed * gain[...] + bias[...]).astype(BF)
    entry[...] = low
    q[...] = ((dot_nn(low, wq[...]) + qb[...]) * HEAD_DIM**-0.5).astype(BF)
    k[...] = dot_nn(low, wk[...]).astype(BF)
    v[...] = (dot_nn(low, wv[...]) + vb[...]).astype(BF)


def attend_kernel(first, block, place, q, k, v, segq, segk, scale, attended, low, mine, theirs, logsum, hold):
    rows, width = q.shape
    half = rows // 2
    masks = head_masks(width, BF)
    for at in range(0, rows, block):
        length = first + at + block
        query = q[at : at + block, :]
        keys = k[:length, :]
        (seg,) = rows_to_columns([segq[:, at : at + block].astype(F32)])
        place_q = first + at + lax.broadcasted_iota(jnp.int32, (block, length), 0)
        place_k = lax.broadcasted_iota(jnp.int32, (block, length), 1)
        allowed = (seg == segk[:, :length].astype(F32)) & (place_k <= place_q)
        shift = jnp.where(allowed, 0.0, EXCLUDED)
        total = jnp.zeros((block, width), F32)
        sums = []
        for mask in masks:
            scores = dot_nt(query * mask, keys) + shift
            top = jnp.max(scores, axis=-1, keepdims=True)
            expo = jnp.exp(scores - top)
            norm = jnp.sum(expo, axis=-1, keepdims=True)
            weights = (expo * (1.0 / norm)).astype(BF)
            total = total + dot_nn(weights, v[:length, :] * mask)
            sums.append(top + jnp.log(norm))
        attended[at : at + block, :] = total
        context = (total * scale[...]).astype(BF)
        low[at : at + block, :] = context
        hold[at : at + block, :] = context.astype(F32)
        logsum[:, at : at + block] = columns_to_rows(sums)
    mine[...] = hold[pl.ds(pl.multiple_of(place[0] * half, half), half), :]
    theirs[...] = hold[pl.ds(pl.multiple_of(place[1] * half, half), half), :]


def pack_kernel(wide, near_out, out_pair, fc1, fc2):
    width, units = near_out.shape[1], fc1.shape[1]
    out_pair[:, :width] = near_out[...]
    out_pair[:, width:] = wide[:, :width].astype(BF)
    fc1[...] = wide[:, width : width + units].astype(BF)
    fc2[...] = wide[:, width + units :].astype(BF)


def far_kernel(side, far_half, far_rest, diag_half, diag_rest, out):
    rows, width = far_half.shape
    here = pl.ds(pl.multiple_of(side[0] * rows, rows), rows)
    there = pl.ds(pl.multiple_of((1 - side[0]) * rows, rows), rows)
    out[here, :width] = far_half[...].astype(BF)
    out[there, :width] = far_rest[...].astype(BF)
    out[here, width:] = diag_half[...].astype(BF)
    out[there, width:] = diag_rest[...].astype(BF)


def upstream_kernel(place, cot, own, near, out):
    units = own.shape[1]
    out[:, :units] = dot_nn(cot[...], own[...])
    out[:, units:] = dot_nn(cot[...], near[...])


def forward_kernel(
    place, seg, ctx_chip, ctx_far, wo_chip, wo_far, out_bias, tok, post_gain, post_bias, ln2_gain, ln2_bias,
    fc1_own, fc1_near, fc1_bias, mid_gain, near, cot, grad_middle,
    mixed, stream, inner, share, hidden, stats, sums,
):
    units = fc1_own.shape[1]
    mix = (
        dot_nt(ctx_chip[...].astype(BF), wo_chip[...]) + dot_nt(ctx_far[...].astype(BF), wo_far[...])
    ) + out_bias[...]
    mixed[...] = mix
    normed, _ = normalize(mix)
    branch = normed * post_gain[...] + post_bias[...]
    resid = tok[...].astype(F32) + branch
    stream[...] = resid
    normed2, _ = normalize(resid)
    low = (normed2 * ln2_gain[...] + ln2_bias[...]).astype(BF)
    inner[...] = low
    share[...] = low.astype(F32)
    actives, scaleds = [], []
    for part, (weight, bias, gain) in enumerate(
        ((fc1_own, fc1_bias[...], mid_gain[...]), (fc1_near, near[0:1, :], near[1:2, :]))
    ):
        hid = dot_nn(low, weight[...]) + bias
        hidden[:, part * units : (part + 1) * units] = hid
        actives.append(0.5 * hid * (1.0 + jnp.tanh(tanh_inner(hid))))
        scaleds.append(grad_middle[:, part * units : (part + 1) * units] * gain)

    def both(left, right):
        return jnp.sum(left, axis=-1, keepdims=True) + jnp.sum(right, axis=-1, keepdims=True)

    mean = both(*actives) / (2 * units)
    centred = [active - mean for active in actives]
    stats[...] = columns_to_rows(
        [
            mean,
            both(*[c * c for c in centred]),
            both(*scaleds),
            both(*[s * c for s, c in zip(scaleds, centred)]),
        ]
    )
    (which,) = rows_to_columns([seg[...].astype(F32)])
    valid = (which >= 0).astype(F32)
    sums[...] = stack_rows(
        [
            col_sum(valid * branch * branch),
            col_sum(cot[...].astype(F32)),
            col_sum(valid * jnp.ones_like(branch)),
        ],
        branch.shape[1],
    )


def middle_kernel(
    total, hidden, grad_middle, st0, st1, mid_gain, mid_bias, near,
    fc1_own, fc1_near, fc2_own, fc2_near,
    middle, grad_hidden, share, ffn, back, sums_own, sums_near,
):
    units = fc1_own.shape[1]
    n = 2 * units
    mean = (st0[0:1, :] + st1[0:1, :]) * 0.5
    apart = [s[0:1, :] - mean for s in (st0, st1)]
    spread = (st0[1:2, :] + n * (apart[0] * apart[0])) + (st1[1:2, :] + n * (apart[1] * apart[1]))
    factor = lax.rsqrt(spread / total + EPSILON)
    plain = (st0[2:3, :] + st1[2:3, :]) / total
    along = (st0[3:4, :] + apart[0] * st0[2:3, :]) + (st1[3:4, :] + apart[1] * st1[2:3, :])
    mean, factor, plain, along = rows_to_columns([mean, factor, plain, factor * along / total])
    parts = (
        (mid_gain[...], mid_bias[...], fc1_own, fc2_own, sums_own),
        (near[1:2, :], near[2:3, :], fc1_near, fc2_near, sums_near),
    )
    ffn_parts, back_parts = [], []
    for part, (gain, bias, fc1, fc2, sums) in enumerate(parts):
        hid = hidden[:, part * units : (part + 1) * units]
        bend = jnp.tanh(tanh_inner(hid))
        active = 0.5 * hid * (1.0 + bend)
        slope = 0.5 * (1.0 + bend) + 0.5 * hid * (1.0 - bend * bend) * (
            0.7978845608028654 * (1.0 + 3 * 0.044715 * (hid * hid))
        )
        normed = (active - mean) * factor
        mid = (normed * gain + bias).astype(BF)
        grad = grad_middle[:, part * units : (part + 1) * units]
        low = (factor * (grad * gain - plain - normed * along) * slope).astype(BF)
        if part == 0:
            middle[...] = mid
            grad_hidden[...] = low
        else:
            share[:, :units] = mid.astype(F32)
            share[:, units:] = low.astype(F32)
        sums[...] = stack_rows([col_sum(grad * normed), col_sum(grad), col_sum(low.astype(F32))], units)
        ffn_parts.append(dot_nt(mid, fc2[...]))
        back_parts.append(dot_nt(low, fc1[...]))
    ffn[...] = ffn_parts[0] + ffn_parts[1]
    back[: hidden.shape[0], :] = back_parts[0] + back_parts[1]
    back[hidden.shape[0] :, :] = jnp.zeros((PAD, back.shape[1]), F32)


def stream_kernel(
    place, mine, far, mixed, stream, cot, ln2_gain, post_gain, w_out,
    grad_stream, grad_mixed, wide, context_own, context_near, sums,
):
    grad = mine[: stream.shape[0], :] + far[: stream.shape[0], :]
    normed2, factor2 = normalize(stream[...])
    back = cot[...].astype(F32) + norm_back(grad * ln2_gain[...], normed2, factor2)
    grad_stream[...] = back
    normedp, factorp = normalize(mixed[...])
    low = norm_back(back * post_gain[...], normedp, factorp).astype(BF)
    grad_mixed[...] = low
    wide[...] = low.astype(F32)
    context = dot_nn(low, w_out[...])
    width = context_own.shape[1]
    context_own[...] = context[:, :width]
    context_near[...] = context[:, width:]
    sums[...] = stack_rows(
        [
            col_sum(grad * normed2),
            col_sum(grad),
            col_sum(back * normedp),
            col_sum(back),
            col_sum(low.astype(F32)),
        ],
        back.shape[1],
    )


def attend_back_kernel(first, block, last, place, *refs):
    q, k, v, segq, segk, context_own, context_near, attended, scale, logsum = refs[:10]
    rest = list(refs[10:])
    if not last:
        key_in, value_in = rest[:2]
        rest = rest[2:]
    grad_q, grad_k, grad_v, sums = rest[:4]
    rest = rest[4:]
    if first:
        key_out, value_out = rest[:2]
        rest = rest[2:]
    key_sum, value_sum, low_probs, low_scores, grads = rest
    rows, width = q.shape
    half = rows // 2
    end = first + rows
    masks = head_masks(width, BF)
    wide_masks = head_masks(width, F32)
    if last:
        key_sum[...] = jnp.zeros_like(key_sum)
        value_sum[...] = jnp.zeros_like(value_sum)
    else:
        key_sum[...] = key_in[...]
        value_sum[...] = value_in[...]
    head_sum = jnp.zeros((1, width), F32)
    for part, source in enumerate((context_own, context_near)):
        at = pl.ds(pl.multiple_of(place[part] * half, half), half)
        grad_context = source[...]
        head_sum = head_sum + col_sum(grad_context * attended[at, :])
        grads[at, :] = (grad_context * scale[...]).astype(BF)
    (seg,) = rows_to_columns([segk[:, :end].astype(F32)])
    query_sum = jnp.zeros((1, width), F32)
    for at in range(0, rows, block):
        length = first + at + block
        query = q[at : at + block, :]
        grad = grads[at : at + block, :]
        product = grad.astype(F32) * attended[at : at + block, :]
        delta = columns_to_rows([jnp.sum(product * mask, axis=-1, keepdims=True) for mask in wide_masks])
        place_k = lax.broadcasted_iota(jnp.int32, (length, block), 0)
        place_q = first + at + lax.broadcasted_iota(jnp.int32, (length, block), 1)
        allowed = (seg[:length] == segq[:, at : at + block].astype(F32)) & (place_k <= place_q)
        shift = jnp.where(allowed, 0.0, EXCLUDED)
        queries = [query * mask for mask in masks]
        grad_parts = [grad * mask for mask in masks]
        grad_query = jnp.zeros((block, width), F32)
        for head, mask in enumerate(masks):
            scores = dot_nt(k[:length, :], queries[head]) + shift
            probs = jnp.exp(scores - logsum[head : head + 1, at : at + block])
            low_probs[:length, head * block : (head + 1) * block] = probs.astype(BF)
            grad_probs = dot_nt(v[:length, :], grad_parts[head])
            low = (probs * (grad_probs - delta[head : head + 1, :])).astype(BF)
            low_scores[:length, head * block : (head + 1) * block] = low
            grad_query = grad_query + dot_tn(low, k[:length, :] * mask)
        value_sum[:length, :] += dot_nn(low_probs[:length, :], jnp.concatenate(grad_parts, axis=0))
        key_sum[:length, :] += dot_nn(low_scores[:length, :], jnp.concatenate(queries, axis=0))
        low_query = (grad_query * HEAD_DIM**-0.5).astype(BF)
        grad_q[at : at + block, :] = low_query
        query_sum = query_sum + col_sum(low_query.astype(F32))
    grad_k[...] = key_sum[first:end, :].astype(BF)
    low_value = value_sum[first:end, :].astype(BF)
    grad_v[...] = low_value
    sums[...] = stack_rows([query_sum, col_sum(low_value.astype(F32)), head_sum], width)
    if first:
        key_out[...] = key_sum[:first, :]
        value_out[...] = value_sum[:first, :]


def entry_kernel(place, grad_q, grad_k, grad_v, wq, wk, wv, tok, *refs):
    sends, (keep, sums) = refs[:-2], refs[-2:]
    step = pl.program_id(0)
    part = dot_nt(grad_q[...], wq[...]) + dot_nt(grad_k[...], wk[...]) + dot_nt(grad_v[...], wv[...])
    normed, _ = normalize(tok[...].astype(F32))
    fresh = stack_rows([col_sum(part * normed), col_sum(part)], part.shape[1])

    @pl.when(step == 0)
    def _():
        sums[...] = fresh
        cut = sends[0].shape[1]
        for j, send in enumerate(sends):
            send[...] = part[:, j * cut : (j + 1) * cut]

    @pl.when(step != 0)
    def _():
        sums[...] += fresh
        keep[...] = part


def chip_kernel(keep, *refs):
    gots, out = refs[:-1], refs[-1]
    cut = gots[0].shape[1]
    for j, got in enumerate(gots):
        out[:, j * cut : (j + 1) * cut] = keep[:, j * cut : (j + 1) * cut] + got[...]


def token_kernel(place, mine, far, tok, grad_stream, gain, *refs):
    out, wide = refs[-2:]
    normed, factor = normalize(tok[...].astype(F32))
    grad = grad_stream[...] + norm_back((mine[...] + far[...]) * gain[...], normed, factor)
    out[...] = grad
    wide[...] = grad


def output_kernel(place, mine, far, stream, bias, seg, *refs):
    out, wide, sums = refs[-3:]
    ffn = (mine[...] + far[...]) + bias[...]
    result = stream[...] + ffn
    low = result.astype(BF)
    out[...] = low
    wide[...] = low.astype(F32)
    (which,) = rows_to_columns([seg[...].astype(F32)])
    valid = (which >= 0).astype(F32)
    sums[...] = stack_rows([col_sum(valid * ffn * ffn), col_sum(valid * result * result)], ffn.shape[1])


def put_kernel(place, value, full, out):
    out[...] = value[...].astype(out.dtype)


def line_kernel(kind, chunks, half, place, *refs):
    items, out = refs[:-1], refs[-1]
    for c in range(chunks):
        if kind == "chunks":
            out[2 * c * half : 2 * (c + 1) * half, :] = items[c][...]
        else:
            for part in range(2):
                at = pl.ds(pl.multiple_of((2 * c + place[part]) * half, half), half)
                out[at, :] = items[2 * c + part][...].astype(BF)


def weight_kernel(plan, chunks, half, blocks, place, *refs):
    step = pl.program_id(0)
    refs = list(refs)
    count = {"all": 1, "halves": 2 * chunks, "chunks": chunks}
    sources = [[(kind, [refs.pop(0) for _ in range(count[kind])]) for kind in product] for product in plan]
    send, keep = refs[:2]
    holds = refs[2:]
    depth = send.shape[0]
    operands, fills = [], []
    for product in sources:
        row = []
        for kind, items in product:
            if kind == "all":
                row.append(items[0])
            else:
                hold = holds.pop(0)
                fills.append((kind, items, hold))
                row.append(hold)
        operands.append(row)

    @pl.when(step == 0)
    def _():
        for kind, items, hold in fills:
            line_kernel(kind, chunks, half, place, *items, hold)

    def fill(target):
        offset = 0
        for row in operands:
            left = row[0]
            columns = jnp.concatenate(
                [
                    left[:, pl.ds(pl.multiple_of(blocks[step * depth + j] * LANES, LANES), LANES)]
                    for j in range(depth)
                ],
                axis=1,
            )
            for right in row[1:]:
                total = dot_tn(columns, right[...])
                width = total.shape[1]
                target[:, :, offset : offset + width] = total.reshape(depth, LANES, width)
                offset += width

    @pl.when(step == 0)
    def _():
        fill(send)

    @pl.when(step != 0)
    def _():
        fill(keep)


def first_kernel(keep, got, out):
    out[...] = keep[...] + got[...]


def second_kernel(keep, got, near, out):
    out[...] = (keep[0] + got[0]) + near[0]


def third_kernel(keep, got, near, far, *outs):
    at = 0
    for out in outs:
        cut = slice(at, at + out.shape[1])
        out[...] = ((keep[0, :, cut] + got[0, :, cut]) + near[0, :, cut]) + far[:, cut]
        at += out.shape[1]


def whole(array):
    shape = array.shape
    return (array, shape, lambda *_: (0,) * len(shape))


def swap(value, axis, size, bit):
    return lax.ppermute(value, axis, [(i, i ^ bit) for i in range(size)])


class Order:
    def __init__(self):
        self.last = None

    def after(self, value):
        if self.last is None:
            return value
        return lax.optimization_barrier((value, self.last))[0]

    def keep(self, value):
        self.last = value
        return value

    def wait(self, values):
        tied = lax.optimization_barrier((tuple(values), self.last))
        self.last = tied[1]
        return list(tied[0])

    def call(self, kernel, grid, ins, outs, prefetch=(), scratch=(), aliases=None, vmem=16 << 20, name=None):
        arrays = [item[0] for item in ins]
        specs = [
            pl.BlockSpec(memory_space=pl.ANY) if block is None else pl.BlockSpec(block, place)
            for _, block, place in ins
        ]
        body_of = kernel
        if self.last is not None:
            at = len(prefetch) + len(arrays)
            arrays.append(self.last)
            specs.append(pl.BlockSpec(memory_space=pl.ANY))

            def body_of(*refs):
                return kernel(*refs[:at], *refs[at + 1 :])

        results = pl.pallas_call(
            body_of,
            grid_spec=pltpu.PrefetchScalarGridSpec(
                num_scalar_prefetch=len(prefetch),
                grid=grid,
                in_specs=specs,
                out_specs=[pl.BlockSpec(block, place) for _, _, block, place in outs],
                scratch_shapes=list(scratch),
            ),
            out_shape=[jax.ShapeDtypeStruct(shape, kind) for shape, kind, _, _ in outs],
            input_output_aliases=aliases or {},
            compiler_params=pltpu.CompilerParams(
                dimension_semantics=("arbitrary",) * len(grid), vmem_limit_bytes=vmem
            ),
            cost_estimate=pl.CostEstimate(flops=1000, bytes_accessed=1000, transcendentals=0),
            name=name,
        )(*prefetch, *arrays)
        self.last = min(results, key=lambda r: r.size)
        return results


def body(
    dp, tp, tokens, segments, w_query, w_key, w_value, w_out, w_fc1, w_fc2, ln1_gain, ln1_bias, post_gain, post_bias,
    ln2_gain, ln2_bias, mid_gain, mid_bias, query_bias, value_bias, out_bias, fc1_bias, fc2_bias, head_scale, cotangent,
):
    rows, width = tokens.shape
    hw = w_query.shape[1]
    units = w_fc1.shape[1]
    heads = hw // HEAD_DIM
    size = rows // CHUNKS
    half = size // 2
    block = min(256, size)
    line = Order()
    call = line.call
    row = lambda v: v.reshape(1, -1)
    seg = segments.reshape(1, rows)
    ln1_g, ln1_b, post_g, post_b = row(ln1_gain), row(ln1_bias), row(post_gain), row(post_bias)
    ln2_g, ln2_b, mid_g, mid_b = row(ln2_gain), row(ln2_bias), row(mid_gain), row(mid_bias)
    q_b, v_b, out_b, fc1_b, fc2_b = row(query_bias), row(value_bias), row(out_bias), row(fc1_bias), row(fc2_bias)
    scale = row(jnp.repeat(head_scale, HEAD_DIM))
    core = lax.axis_index("tensor") & 1
    place = (core + jnp.arange(2, dtype=jnp.int32)) & 1
    dp_side = lax.axis_index("dp") & 1
    side = dp_side.astype(jnp.int32).reshape(1)
    chunks = list(range(CHUNKS))
    order = chunks[::-1]

    half_rows = width // 2
    part = lax.dynamic_slice_in_dim(w_out, dp_side * half_rows, half_rows, 0).astype(F32)
    far_half = swap(part, "tensor", tp, 2)
    wide = swap(jnp.concatenate([w_out, w_fc1, w_fc2], 1).astype(F32), "tensor", tp, 1)
    pad = jnp.zeros((5, units), F32)
    near = swap(jnp.concatenate([fc1_b, mid_g, mid_b, pad], 0), "tensor", tp, 1)

    step = min(256, rows)
    entry, query, keys, values = call(
        qkv_kernel,
        (rows // step,),
        [(tokens, (step, width), lambda i: (i, 0))]
        + [whole(a) for a in (ln1_g, ln1_b, w_query, w_key, w_value, q_b, v_b)],
        [((rows, width), BF, (step, width), lambda i: (i, 0))]
        + [((rows, hw), BF, (step, hw), lambda i: (i, 0))] * 3,
        name="qkv",
    )

    at0 = lambda c: (lambda *_: (c, 0))
    at1 = lambda c: (lambda *_: (0, c))
    fix = lambda shape, kind: (shape, kind, shape, lambda *_: (0,) * len(shape))
    own = lambda a, c: (a, (half, a.shape[1]), lambda i, p, c=c: (2 * c + p[0], 0))
    own_seg = lambda c: (seg, (1, half), lambda i, p, c=c: (0, 2 * c + p[0]))

    (far_half,) = line.wait([far_half])
    far_rest = swap(far_half, "dp", dp, 1)
    attended, low_ctx, ctx, logsum = {}, {}, {}, {}
    for c in order:
        end = (c + 1) * size
        attended[c], low_ctx[c], mine, theirs, logsum[c] = call(
            functools.partial(attend_kernel, c * size, block),
            (1,),
            [
                (query, (size, hw), at0(c)),
                (keys, (end, hw), at0(0)),
                (values, (end, hw), at0(0)),
                (seg, (1, size), at1(c)),
                (seg, (1, end), at1(0)),
                whole(scale),
            ],
            [fix((size, hw), F32), fix((size, hw), BF), fix((half, hw), F32), fix((half, hw), F32), fix((8, size), F32)],
            prefetch=(place,),
            scratch=[pltpu.VMEM((size, hw), F32)],
            name="attend",
        )
        ctx[c] = (mine, swap(theirs, "tensor", tp, 1))
    far_ctx = {}
    for c in order:
        mine, got = ctx[c]
        ctx[c] = line.keep(jnp.concatenate([line.after(mine), got], 1))
        far_ctx[c] = swap(ctx[c], "tensor", tp, 2)

    step = min(256, width)
    wo_chip, fc1_near, fc2_near = call(
        pack_kernel,
        (width // step,),
        [(a, (step, a.shape[1]), lambda i: (i, 0)) for a in (wide, w_out)],
        [((width, n), BF, (step, n), lambda i: (i, 0)) for n in (2 * hw, units, units)],
        name="pack",
    )
    diag_half = swap(far_half, "tensor", tp, 1)
    diag_rest = swap(far_rest, "tensor", tp, 1)
    (grad_mid,) = call(
        upstream_kernel,
        (CHUNKS,),
        [(cotangent, (half, width), lambda i, p: (2 * i + p[0], 0)), whole(w_fc2), whole(fc2_near)],
        [((CHUNKS * half, 2 * units), F32, (half, 2 * units), lambda i, p: (i, 0))],
        prefetch=(place,),
        name="upstream",
    )
    (wo_far,) = call(
        far_kernel,
        (1,),
        [whole(a) for a in (far_half, far_rest, diag_half, diag_rest)],
        [fix((width, 2 * hw), BF)],
        prefetch=(side,),
        name="far",
    )

    mixed, stream, inner, hidden, stats, far_stats, fsums, near_inner = {}, {}, {}, {}, {}, {}, {}, {}
    for c in order:
        mixed[c], stream[c], inner[c], share, hidden[c], stats[c], fsums[c] = call(
            forward_kernel,
            (1,),
            [own_seg(c)]
            + [whole(a) for a in (ctx[c], far_ctx[c], wo_chip, wo_far, out_b)]
            + [own(tokens, c)]
            + [whole(a) for a in (post_g, post_b, ln2_g, ln2_b, w_fc1, fc1_near, fc1_b, mid_g, near)]
            + [own(cotangent, c), (grad_mid, (half, 2 * units), at0(c))],
            [fix((half, width), F32)] * 2
            + [fix((half, width), BF), fix((half, width), F32), fix((half, 2 * units), F32)]
            + [fix((8, half), F32), fix((8, width), F32)],
            prefetch=(place,),
            name="forward",
        )
        far_stats[c] = swap(stats[c], "tensor", tp, 2)
        near_inner[c] = swap(share, "tensor", tp, 1)

    middle, grad_hid, ffn, back, far_back, gsums, nsums = {}, {}, {}, {}, {}, {}, {}
    near_mid, near_hid = {}, {}
    for c in order:
        mid, hid, share, ffn[c], back[c], gsums[c], nsums[c] = call(
            functools.partial(middle_kernel, units * tp),
            (1,),
            [whole(hidden[c]), (grad_mid, (half, 2 * units), at0(c))]
            + [whole(a) for a in (stats[c], far_stats[c], mid_g, mid_b, near)]
            + [whole(a) for a in (w_fc1, fc1_near, w_fc2, fc2_near)],
            [fix((half, units), BF)] * 2
            + [fix((half, 2 * units), F32)]
            + [fix((half, width), F32), fix((half + PAD, width), F32)]
            + [fix((8, units), F32)] * 2,
            name="middle",
        )
        middle[c], grad_hid[c] = mid, hid
        far_back[c] = swap(back[c], "tensor", tp, 2)
        near_both = swap(share, "tensor", tp, 1)
        near_mid[c] = (near_both, (half, units), lambda *_: (0, 0))
        near_hid[c] = (near_both, (half, units), lambda *_: (0, 1))

    near_blocks = width // dp == LANES and dp == 8
    if near_blocks:
        depth = dp // 2
        me = lax.axis_index("dp")
        ring, across = me // 2, me & 1
        lines = [depth - 1 - (ring ^ 1), ring ^ 1, depth - 1 - ring, ring]
        opposite = [(i, dp - 2 - i + 2 * (i & 1)) for i in range(dp)]
        pairs = [[(i, i ^ bit) for i in range(dp)] for bit in (1, 2)]
        orders = {
            "first": ([2 * at + 1 - across for at in lines] + [2 * at + across for at in lines], pairs + [opposite]),
            "last": (
                [2 * at + side for at in lines for side in (1 - across, across)],
                [pairs[1], opposite, pairs[0]],
            ),
        }

    def weight(plan, items, columns, name, columns_at="first"):
        arrays = [item for group in items for operand in group for item in operand]
        kinds = [kind for product in plan for kind in product]
        holds = [
            pltpu.VMEM((rows, operand[0][1][1]), BF)
            for kind, operand in zip(kinds, [o for g in items for o in g])
            if kind != "all"
        ]
        if not near_blocks:
            results = []
            for product, group in zip(plan, items):
                full = []
                for kind, operand in zip(product, group):
                    if kind == "all":
                        full.append(operand[0][0])
                        continue
                    n = operand[0][1][1]
                    (lined,) = call(
                        functools.partial(line_kernel, kind, CHUNKS, half),
                        (1,),
                        operand,
                        [fix((rows, n), BF)],
                        prefetch=(place,),
                        name=name,
                    )
                    full.append(lined)
                results += [
                    lax.psum_scatter(dot_tn(full[0], right), "dp", scatter_dimension=0, tiled=True)
                    for right in full[1:]
                ]
            return lambda: results
        blocks, perms = orders[columns_at]
        blocks = jnp.stack(blocks).astype(jnp.int32)
        send, keep = call(
            functools.partial(weight_kernel, plan, CHUNKS, half),
            (2,),
            arrays,
            [fix((depth, LANES, columns), F32)] * 2,
            prefetch=(blocks, place),
            scratch=holds,
            name=name,
        )
        got = lax.ppermute(send, "dp", perms[0])

        lanes = min(1024, columns)
        by_lanes = lambda array, count, first: (array, (count, LANES, lanes), lambda i: (first, 0, i))

        def first():
            (send,) = call(
                first_kernel,
                (columns // lanes,),
                [by_lanes(a, 2, 0) for a in (keep, got)],
                [((2, LANES, columns), F32, (2, LANES, lanes), lambda i: (0, 0, i))],
                name="first",
            )
            return lax.ppermute(send, "dp", perms[1])

        def second(near):
            (send,) = call(
                second_kernel,
                (columns // lanes,),
                [by_lanes(a, 1, 2) for a in (keep, got)] + [by_lanes(near, 1, 0)],
                [((LANES, columns), F32, (LANES, lanes), lambda i: (0, i))],
                name="second",
            )
            return lax.ppermute(send, "dp", perms[2])

        def third(near, far):
            return call(
                third_kernel,
                (1,),
                [(a, (1, LANES, columns), lambda *_, f=f: (f, 0, 0)) for a, f in ((keep, 3), (got, 3), (near, 1))]
                + [whole(far)],
                [fix((LANES, operand[0][1][1]), F32) for group in items for operand in group[1:]],
                name="third",
            )

        return first, second, third

    halves = lambda mine, wide_near: [item for c in chunks for item in (whole(mine[c]), wide_near[c])]
    fc2_sum = weight(
        [("all", "halves")],
        [[[whole(cotangent)], halves(middle, near_mid)]],
        units,
        "weight_fc2",
        "last",
    )
    fc1_sum = weight(
        [("halves", "halves")],
        [
            [
                halves(inner, {c: whole(near_inner[c]) for c in chunks}),
                halves(grad_hid, near_hid),
            ]
        ],
        units,
        "weight_fc1",
    )

    own_out = lambda kind, c: ((rows, width), kind, (half, width), lambda i, p, c=c: (2 * c + p[0], 0))
    grown = {"tokens": None, "output": None}

    def grow(which, ins, outs, kernel):
        aliases = None
        if grown[which] is not None:
            aliases = {1 + len(ins): 0}
            ins = ins + [(grown[which], None, None)]
        results = call(kernel, (1,), ins, outs, prefetch=(place,), aliases=aliases, name=which)
        grown[which] = results[0]
        return results[1:]

    def put(which, kind, value, c):
        grow(which, [whole(value)], [((rows, width), kind, (half, width), lambda i, p: (2 * c + p[1], 0))], put_kernel)

    def token(c):
        ins = [(a, (half, width), at0(0)) for a in (chip[c], far_chip[c])]
        ins += [own(tokens, c), whole(grad_stream[c]), whole(ln1_g)]
        (value,) = grow("tokens", ins, [own_out(F32, c), fix((half, width), F32)], token_kernel)
        return swap(value, "tensor", tp, 1)

    def result(c):
        ins = [whole(ffn[c]), whole(far_ffn[c]), whole(stream[c]), whole(fc2_b), own_seg(c)]
        value, osums[c] = grow(
            "output", ins, [own_out(BF, c), fix((half, width), F32), fix((8, width), F32)], output_kernel
        )
        return swap(value, "tensor", tp, 1)

    grad_stream, grad_mix, near_mix, grad_q, grad_k, grad_v, chip, far_chip = {}, {}, {}, {}, {}, {}, {}, {}
    hsums, qsums, esums, far_ffn = {}, {}, {}, {}
    osums, wide_tok, wide_out = {}, {}, {}
    carry = None
    fc2_part = fc1_part = attn_part = None
    for c in order:
        end = (c + 1) * size
        last = c == CHUNKS - 1
        by_half = lambda a: (a, (half, a.shape[1]), lambda i, p: (p[1 - i], 0))
        grad_stream[c], grad_mix[c], wide_mix, ctx_own, ctx_near, hsums[c] = call(
            stream_kernel,
            (1,),
            [whole(a) for a in (back[c], far_back[c], mixed[c], stream[c])]
            + [own(cotangent, c), whole(ln2_g), whole(post_g), whole(wo_chip)],
            [fix((half, width), F32), fix((half, width), BF), fix((half, width), F32)]
            + [fix((half, hw), F32)] * 2
            + [fix((8, width), F32)],
            prefetch=(place,),
            name="stream",
        )
        ctx_near = swap(ctx_near, "tensor", tp, 1)
        near_mix[c] = swap(wide_mix, "tensor", tp, 1)
        results = call(
            functools.partial(attend_back_kernel, c * size, block, last),
            (1,),
            [
                (query, (size, hw), at0(c)),
                (keys, (end, hw), at0(0)),
                (values, (end, hw), at0(0)),
                (seg, (1, size), at1(c)),
                (seg, (1, end), at1(0)),
            ]
            + [whole(a) for a in (ctx_own, ctx_near, attended[c], scale, logsum[c])]
            + ([] if last else [whole(a) for a in carry]),
            [fix((size, hw), BF)] * 3 + [fix((8, hw), F32)] + ([fix((c * size, hw), F32)] * 2 if c else []),
            prefetch=(place,),
            scratch=[pltpu.VMEM((end, hw), F32)] * 2
            + [pltpu.VMEM((end, heads * block), BF)] * 2
            + [pltpu.VMEM((size, hw), BF)],
            name="attend_back",
        )
        grad_q[c], grad_k[c], grad_v[c], qsums[c] = results[:4]
        carry = results[4:]
        if c == order[-1] and near_blocks:
            fc2_part = fc2_sum[0]()
        count = 1 if c == order[-1] else 2
        *sends, keep, esums[c] = call(
            entry_kernel,
            (2,),
            [by_half(a) for a in (grad_q[c], grad_k[c], grad_v[c])]
            + [whole(a) for a in (w_query, w_key, w_value)]
            + [(tokens, (half, width), lambda i, p, c=c: (2 * c + p[1 - i], 0))],
            [fix((half, width // count), F32)] * count + [fix((half, width), F32), fix((8, width), F32)],
            prefetch=(place,),
            name="entry",
        )
        gots = [swap(send, "tensor", tp, 1) for send in sends]
        if c == order[-1]:
            for d in order[:-1]:
                far_ffn[d] = swap(line.after(ffn[d]), "tensor", tp, 2)
            far_ffn[c] = swap(line.after(ffn[c]), "tensor", tp, 2)
        (chip[c],) = call(
            chip_kernel,
            (1,),
            [whole(a) for a in (keep, *gots)],
            [fix((half, width), F32)],
            name="chip",
        )
        far_chip[c] = swap(chip[c], "tensor", tp, 2)

    if near_blocks:
        fc1_part = fc1_sum[0]()
    attn_sum = weight(
        [("halves", "chunks"), ("all", "chunks", "chunks", "chunks")],
        [
            [
                halves(grad_mix, {c: whole(near_mix[c]) for c in chunks}),
                [whole(low_ctx[c]) for c in chunks],
            ],
            [[whole(entry)]] + [[whole(g[c]) for c in chunks] for g in (grad_q, grad_k, grad_v)],
        ],
        4 * hw,
        "weight_attn",
    )
    last = order[-1]
    for c in order[:-1]:
        wide_tok[c] = token(c)
    for c in order[:-1]:
        wide_out[c] = result(c)
    if near_blocks:
        fc2_last = fc2_sum[1](fc2_part)
        fc1_last = fc1_sum[1](fc1_part)
        attn_part = attn_sum[0]()

    def puts(some):
        wides = line.wait([wide[c] for wide in (wide_tok, wide_out) for c in some])
        for index, c in enumerate(some):
            put("tokens", F32, wides[index], c)
            put("output", BF, wides[len(some) + index], c)

    if len(order) > 1:
        puts(order[:-1])
    if near_blocks:
        (grad_w_fc1,) = fc1_sum[2](fc1_part, fc1_last)
        attn_last = attn_sum[1](attn_part)
        grad_w_out, grad_w_query, grad_w_key, grad_w_value = attn_sum[2](attn_part, attn_last)
    else:
        (grad_w_fc2,), (grad_w_fc1,) = fc2_sum(), fc1_sum()
        grad_w_out, grad_w_query, grad_w_key, grad_w_value = attn_sum()
    wide_out[last] = result(last)

    add = lambda parts: functools.reduce(lambda a, b: a + b, [parts[c] for c in chunks])
    fs, gs, ns, hs, qs, es, os = (add(p) for p in (fsums, gsums, nsums, hsums, qsums, esums, osums))
    own_part = jnp.concatenate([hs[:5], fs[:3], os[:2], es[:2], gs[:3]], 0)
    near_part = jnp.concatenate([hs[:5], fs[:3], os[:2], es[:2], ns[:3]], 0)
    packed = own_part + swap(near_part, "tensor", tp, 1)
    far = swap(packed[10:12], "tensor", tp, 2)
    tail = jnp.concatenate([qs[0], qs[1], qs[2], qs[2]]).reshape(1, -1)[:, :width]
    packed = jnp.concatenate([packed[:10], packed[10:12] + far, packed[12:], tail], 0)
    wide_tok[last] = token(last)
    if near_blocks:
        for perm in (*pairs, opposite):
            packed = packed + lax.ppermute(packed, "dp", perm)
    else:
        packed = lax.psum(packed, "dp")
    puts(order[-1:])
    if near_blocks:
        (grad_w_fc2,) = fc2_sum[2](fc2_part, fc2_last)
    grad_tokens, output = grown["tokens"], grown["output"]

    last_row = packed[15]
    counted = packed[7, 0]
    squares = jnp.stack([jnp.sum(packed[5]), jnp.sum(packed[8]), jnp.sum(packed[9])])
    rms = jnp.sqrt(squares / (counted * width))
    grad_head = jnp.sum(last_row[2 * hw : 3 * hw].reshape(heads, HEAD_DIM), axis=1)
    return (
        output,
        grad_tokens,
        grad_w_query,
        grad_w_key,
        grad_w_value,
        grad_w_out,
        grad_w_fc1,
        grad_w_fc2,
        packed[10],
        packed[11],
        packed[2],
        packed[3],
        packed[0],
        packed[1],
        packed[12],
        packed[13],
        last_row[:hw],
        last_row[hw : 2 * hw],
        packed[4],
        packed[14],
        packed[6],
        grad_head,
        rms,
    )


def solution(mesh):
    cut = P(None, "tensor")
    part = P("tensor")
    rows = P("dp", None)
    both = P("dp", "tensor")
    return jax.shard_map(
        functools.partial(body, mesh.shape["dp"], mesh.shape["tensor"]),
        mesh=mesh,
        in_specs=(rows, rows) + (cut,) * 6 + (P(),) * 6 + (part,) * 4 + (P(), part, P(), part, rows),
        out_specs=(rows, rows) + (both,) * 6 + (P(),) * 6 + (part,) * 4 + (P(), part, P(), part, P()),
        check_vma=False,
    )
```

```python
import functools

import jax
import jax.numpy as jnp
from jax import lax
from jax.experimental import pallas as pl
from jax.experimental.pallas import tpu as pltpu
from jax.sharding import PartitionSpec as P

HEAD_DIM = 64
EPSILON = 1e-05
EXCLUDED = -1e30
LANES = 128
CHUNKS = 2
PAD = 16
BF = jnp.bfloat16
F32 = jnp.float32


def dot_nn(a, b):
    return lax.dot_general(a, b, (((1,), (0,)), ((), ())), preferred_element_type=F32)


def dot_nt(a, b):
    return lax.dot_general(a, b, (((1,), (1,)), ((), ())), preferred_element_type=F32)


def dot_tn(a, b):
    return lax.dot_general(a, b, (((0,), (0,)), ((), ())), preferred_element_type=F32)


def normalize(v):
    mean = jnp.mean(v, axis=-1, keepdims=True)
    centred = v - mean
    factor = lax.rsqrt(jnp.mean(centred * centred, axis=-1, keepdims=True) + EPSILON)
    return centred * factor, factor


def norm_back(scaled, normed, factor):
    return factor * (
        scaled
        - jnp.mean(scaled, axis=-1, keepdims=True)
        - normed * jnp.mean(scaled * normed, axis=-1, keepdims=True)
    )


def col_sum(v):
    return jnp.sum(v, axis=0, keepdims=True)


def tanh_inner(v):
    return 0.7978845608028654 * (v + 0.044715 * (v * v * v))


def columns_to_rows(columns):
    n = columns[0].shape[0]
    lane = lax.broadcasted_iota(jnp.int32, (n, LANES), 1)
    tile = jnp.zeros((n, LANES), F32)
    for index, column in enumerate(columns):
        tile = jnp.where(lane == index, column, tile)
    return jnp.transpose(tile)[:8]


def rows_to_columns(rows):
    n = rows[0].shape[1]
    sub = lax.broadcasted_iota(jnp.int32, (LANES, n), 0)
    tile = jnp.zeros((LANES, n), F32)
    for index, row in enumerate(rows):
        tile = jnp.where(sub == index, row, tile)
    tile = jnp.transpose(tile)
    return [tile[:, index : index + 1] for index in range(len(rows))]


def stack_rows(rows, width):
    sub = lax.broadcasted_iota(jnp.int32, (8, width), 0)
    tile = jnp.zeros((8, width), F32)
    for index, row in enumerate(rows):
        tile = jnp.where(sub == index, row, tile)
    return tile


def head_masks(width, kind):
    lane = lax.broadcasted_iota(jnp.int32, (1, width), 1) // HEAD_DIM
    return [(lane == head).astype(F32).astype(kind) for head in range(width // HEAD_DIM)]


def qkv_kernel(tok, gain, bias, wq, wk, wv, qb, vb, entry, q, k, v):
    normed, _ = normalize(tok[...].astype(F32))
    low = (normed * gain[...] + bias[...]).astype(BF)
    entry[...] = low
    q[...] = ((dot_nn(low, wq[...]) + qb[...]) * HEAD_DIM**-0.5).astype(BF)
    k[...] = dot_nn(low, wk[...]).astype(BF)
    v[...] = (dot_nn(low, wv[...]) + vb[...]).astype(BF)


def attend_kernel(first, block, place, q, k, v, segq, segk, scale, attended, low, mine, theirs, logsum, hold):
    rows, width = q.shape
    half = rows // 2
    masks = head_masks(width, BF)
    for at in range(0, rows, block):
        length = first + at + block
        query = q[at : at + block, :]
        keys = k[:length, :]
        (seg,) = rows_to_columns([segq[:, at : at + block].astype(F32)])
        place_q = first + at + lax.broadcasted_iota(jnp.int32, (block, length), 0)
        place_k = lax.broadcasted_iota(jnp.int32, (block, length), 1)
        allowed = (seg == segk[:, :length].astype(F32)) & (place_k <= place_q)
        shift = jnp.where(allowed, 0.0, EXCLUDED)
        total = jnp.zeros((block, width), F32)
        sums = []
        for mask in masks:
            scores = dot_nt(query * mask, keys) + shift
            top = jnp.max(scores, axis=-1, keepdims=True)
            expo = jnp.exp(scores - top)
            norm = jnp.sum(expo, axis=-1, keepdims=True)
            weights = (expo * (1.0 / norm)).astype(BF)
            total = total + dot_nn(weights, v[:length, :] * mask)
            sums.append(top + jnp.log(norm))
        attended[at : at + block, :] = total
        context = (total * scale[...]).astype(BF)
        low[at : at + block, :] = context
        hold[at : at + block, :] = context.astype(F32)
        logsum[:, at : at + block] = columns_to_rows(sums)
    mine[...] = hold[pl.ds(pl.multiple_of(place[0] * half, half), half), :]
    theirs[...] = hold[pl.ds(pl.multiple_of(place[1] * half, half), half), :]


def pack_kernel(wide, near_out, out_pair, fc1, fc2):
    width, units = near_out.shape[1], fc1.shape[1]
    out_pair[:, :width] = near_out[...]
    out_pair[:, width:] = wide[:, :width].astype(BF)
    fc1[...] = wide[:, width : width + units].astype(BF)
    fc2[...] = wide[:, width + units :].astype(BF)


def far_kernel(side, far_half, far_rest, diag_half, diag_rest, out):
    rows, width = far_half.shape
    here = pl.ds(pl.multiple_of(side[0] * rows, rows), rows)
    there = pl.ds(pl.multiple_of((1 - side[0]) * rows, rows), rows)
    out[here, :width] = far_half[...].astype(BF)
    out[there, :width] = far_rest[...].astype(BF)
    out[here, width:] = diag_half[...].astype(BF)
    out[there, width:] = diag_rest[...].astype(BF)


def upstream_kernel(place, cot, own, near, out):
    units = own.shape[1]
    out[:, :units] = dot_nn(cot[...], own[...])
    out[:, units:] = dot_nn(cot[...], near[...])


def forward_kernel(
    place, seg, ctx_chip, ctx_far, wo_chip, wo_far, out_bias, tok, post_gain, post_bias, ln2_gain, ln2_bias,
    fc1_own, fc1_near, fc1_bias, mid_gain, near, cot, grad_middle,
    mixed, stream, inner, share, hidden, stats, sums,
):
    units = fc1_own.shape[1]
    mix = (
        dot_nt(ctx_chip[...].astype(BF), wo_chip[...]) + dot_nt(ctx_far[...].astype(BF), wo_far[...])
    ) + out_bias[...]
    mixed[...] = mix
    normed, _ = normalize(mix)
    branch = normed * post_gain[...] + post_bias[...]
    resid = tok[...].astype(F32) + branch
    stream[...] = resid
    normed2, _ = normalize(resid)
    low = (normed2 * ln2_gain[...] + ln2_bias[...]).astype(BF)
    inner[...] = low
    share[...] = low.astype(F32)
    actives, scaleds = [], []
    for part, (weight, bias, gain) in enumerate(
        ((fc1_own, fc1_bias[...], mid_gain[...]), (fc1_near, near[0:1, :], near[1:2, :]))
    ):
        hid = dot_nn(low, weight[...]) + bias
        hidden[:, part * units : (part + 1) * units] = hid
        actives.append(0.5 * hid * (1.0 + jnp.tanh(tanh_inner(hid))))
        scaleds.append(grad_middle[:, part * units : (part + 1) * units] * gain)

    def both(left, right):
        return jnp.sum(left, axis=-1, keepdims=True) + jnp.sum(right, axis=-1, keepdims=True)

    mean = both(*actives) / (2 * units)
    centred = [active - mean for active in actives]
    stats[...] = columns_to_rows(
        [
            mean,
            both(*[c * c for c in centred]),
            both(*scaleds),
            both(*[s * c for s, c in zip(scaleds, centred)]),
        ]
    )
    (which,) = rows_to_columns([seg[...].astype(F32)])
    valid = (which >= 0).astype(F32)
    sums[...] = stack_rows(
        [
            col_sum(valid * branch * branch),
            col_sum(cot[...].astype(F32)),
            col_sum(valid * jnp.ones_like(branch)),
        ],
        branch.shape[1],
    )


def middle_kernel(
    total, hidden, grad_middle, st0, st1, mid_gain, mid_bias, near,
    fc1_own, fc1_near, fc2_own, fc2_near,
    middle, grad_hidden, share, ffn, back, sums_own, sums_near,
):
    units = fc1_own.shape[1]
    n = 2 * units
    mean = (st0[0:1, :] + st1[0:1, :]) * 0.5
    apart = [s[0:1, :] - mean for s in (st0, st1)]
    spread = (st0[1:2, :] + n * (apart[0] * apart[0])) + (st1[1:2, :] + n * (apart[1] * apart[1]))
    factor = lax.rsqrt(spread / total + EPSILON)
    plain = (st0[2:3, :] + st1[2:3, :]) / total
    along = (st0[3:4, :] + apart[0] * st0[2:3, :]) + (st1[3:4, :] + apart[1] * st1[2:3, :])
    mean, factor, plain, along = rows_to_columns([mean, factor, plain, factor * along / total])
    parts = (
        (mid_gain[...], mid_bias[...], fc1_own, fc2_own, sums_own),
        (near[1:2, :], near[2:3, :], fc1_near, fc2_near, sums_near),
    )
    ffn_parts, back_parts = [], []
    for part, (gain, bias, fc1, fc2, sums) in enumerate(parts):
        hid = hidden[:, part * units : (part + 1) * units]
        bend = jnp.tanh(tanh_inner(hid))
        active = 0.5 * hid * (1.0 + bend)
        slope = 0.5 * (1.0 + bend) + 0.5 * hid * (1.0 - bend * bend) * (
            0.7978845608028654 * (1.0 + 3 * 0.044715 * (hid * hid))
        )
        normed = (active - mean) * factor
        mid = (normed * gain + bias).astype(BF)
        grad = grad_middle[:, part * units : (part + 1) * units]
        low = (factor * (grad * gain - plain - normed * along) * slope).astype(BF)
        if part == 0:
            middle[...] = mid
            grad_hidden[...] = low
        else:
            share[:, :units] = mid.astype(F32)
            share[:, units:] = low.astype(F32)
        sums[...] = stack_rows([col_sum(grad * normed), col_sum(grad), col_sum(low.astype(F32))], units)
        ffn_parts.append(dot_nt(mid, fc2[...]))
        back_parts.append(dot_nt(low, fc1[...]))
    ffn[...] = ffn_parts[0] + ffn_parts[1]
    back[: hidden.shape[0], :] = back_parts[0] + back_parts[1]
    back[hidden.shape[0] :, :] = jnp.zeros((PAD, back.shape[1]), F32)


def stream_kernel(
    place, mine, far, mixed, stream, cot, ln2_gain, post_gain, w_out,
    grad_stream, grad_mixed, wide, context_own, context_near, sums,
):
    grad = mine[: stream.shape[0], :] + far[: stream.shape[0], :]
    normed2, factor2 = normalize(stream[...])
    back = cot[...].astype(F32) + norm_back(grad * ln2_gain[...], normed2, factor2)
    grad_stream[...] = back
    normedp, factorp = normalize(mixed[...])
    low = norm_back(back * post_gain[...], normedp, factorp).astype(BF)
    grad_mixed[...] = low
    wide[...] = low.astype(F32)
    context = dot_nn(low, w_out[...])
    width = context_own.shape[1]
    context_own[...] = context[:, :width]
    context_near[...] = context[:, width:]
    sums[...] = stack_rows(
        [
            col_sum(grad * normed2),
            col_sum(grad),
            col_sum(back * normedp),
            col_sum(back),
            col_sum(low.astype(F32)),
        ],
        back.shape[1],
    )


def attend_back_kernel(first, block, last, place, *refs):
    q, k, v, segq, segk, context_own, context_near, attended, scale, logsum = refs[:10]
    rest = list(refs[10:])
    if not last:
        key_in, value_in = rest[:2]
        rest = rest[2:]
    grad_q, grad_k, grad_v, sums = rest[:4]
    rest = rest[4:]
    if first:
        key_out, value_out = rest[:2]
        rest = rest[2:]
    key_sum, value_sum, low_probs, low_scores, grads = rest
    rows, width = q.shape
    half = rows // 2
    end = first + rows
    masks = head_masks(width, BF)
    wide_masks = head_masks(width, F32)
    if last:
        key_sum[...] = jnp.zeros_like(key_sum)
        value_sum[...] = jnp.zeros_like(value_sum)
    else:
        key_sum[...] = key_in[...]
        value_sum[...] = value_in[...]
    head_sum = jnp.zeros((1, width), F32)
    for part, source in enumerate((context_own, context_near)):
        at = pl.ds(pl.multiple_of(place[part] * half, half), half)
        grad_context = source[...]
        head_sum = head_sum + col_sum(grad_context * attended[at, :])
        grads[at, :] = (grad_context * scale[...]).astype(BF)
    (seg,) = rows_to_columns([segk[:, :end].astype(F32)])
    query_sum = jnp.zeros((1, width), F32)
    for at in range(0, rows, block):
        length = first + at + block
        query = q[at : at + block, :]
        grad = grads[at : at + block, :]
        product = grad.astype(F32) * attended[at : at + block, :]
        delta = columns_to_rows([jnp.sum(product * mask, axis=-1, keepdims=True) for mask in wide_masks])
        place_k = lax.broadcasted_iota(jnp.int32, (length, block), 0)
        place_q = first + at + lax.broadcasted_iota(jnp.int32, (length, block), 1)
        allowed = (seg[:length] == segq[:, at : at + block].astype(F32)) & (place_k <= place_q)
        shift = jnp.where(allowed, 0.0, EXCLUDED)
        queries = [query * mask for mask in masks]
        grad_parts = [grad * mask for mask in masks]
        grad_query = jnp.zeros((block, width), F32)
        for head, mask in enumerate(masks):
            scores = dot_nt(k[:length, :], queries[head]) + shift
            probs = jnp.exp(scores - logsum[head : head + 1, at : at + block])
            low_probs[:length, head * block : (head + 1) * block] = probs.astype(BF)
            grad_probs = dot_nt(v[:length, :], grad_parts[head])
            low = (probs * (grad_probs - delta[head : head + 1, :])).astype(BF)
            low_scores[:length, head * block : (head + 1) * block] = low
            grad_query = grad_query + dot_tn(low, k[:length, :] * mask)
        value_sum[:length, :] += dot_nn(low_probs[:length, :], jnp.concatenate(grad_parts, axis=0))
        key_sum[:length, :] += dot_nn(low_scores[:length, :], jnp.concatenate(queries, axis=0))
        low_query = (grad_query * HEAD_DIM**-0.5).astype(BF)
        grad_q[at : at + block, :] = low_query
        query_sum = query_sum + col_sum(low_query.astype(F32))
    grad_k[...] = key_sum[first:end, :].astype(BF)
    low_value = value_sum[first:end, :].astype(BF)
    grad_v[...] = low_value
    sums[...] = stack_rows([query_sum, col_sum(low_value.astype(F32)), head_sum], width)
    if first:
        key_out[...] = key_sum[:first, :]
        value_out[...] = value_sum[:first, :]


def entry_kernel(place, grad_q, grad_k, grad_v, wq, wk, wv, tok, *refs):
    sends, (keep, sums) = refs[:-2], refs[-2:]
    step = pl.program_id(0)
    part = dot_nt(grad_q[...], wq[...]) + dot_nt(grad_k[...], wk[...]) + dot_nt(grad_v[...], wv[...])
    normed, _ = normalize(tok[...].astype(F32))
    fresh = stack_rows([col_sum(part * normed), col_sum(part)], part.shape[1])

    @pl.when(step == 0)
    def _():
        sums[...] = fresh
        cut = sends[0].shape[1]
        for j, send in enumerate(sends):
            send[...] = part[:, j * cut : (j + 1) * cut]

    @pl.when(step != 0)
    def _():
        sums[...] += fresh
        keep[...] = part


def chip_kernel(keep, *refs):
    gots, out = refs[:-1], refs[-1]
    cut = gots[0].shape[1]
    for j, got in enumerate(gots):
        out[:, j * cut : (j + 1) * cut] = keep[:, j * cut : (j + 1) * cut] + got[...]


def token_kernel(place, mine, far, tok, grad_stream, gain, *refs):
    out, wide = refs[-2:]
    normed, factor = normalize(tok[...].astype(F32))
    grad = grad_stream[...] + norm_back((mine[...] + far[...]) * gain[...], normed, factor)
    out[...] = grad
    wide[...] = grad


def output_kernel(place, mine, far, stream, bias, seg, *refs):
    out, wide, sums = refs[-3:]
    ffn = (mine[...] + far[...]) + bias[...]
    result = stream[...] + ffn
    low = result.astype(BF)
    out[...] = low
    wide[...] = low.astype(F32)
    (which,) = rows_to_columns([seg[...].astype(F32)])
    valid = (which >= 0).astype(F32)
    sums[...] = stack_rows([col_sum(valid * ffn * ffn), col_sum(valid * result * result)], ffn.shape[1])


def put_kernel(place, value, full, out):
    out[...] = value[...].astype(out.dtype)


def line_kernel(kind, chunks, half, place, *refs):
    items, out = refs[:-1], refs[-1]
    for c in range(chunks):
        if kind == "chunks":
            out[2 * c * half : 2 * (c + 1) * half, :] = items[c][...]
        else:
            for part in range(2):
                at = pl.ds(pl.multiple_of((2 * c + place[part]) * half, half), half)
                out[at, :] = items[2 * c + part][...].astype(BF)


def weight_kernel(plan, chunks, half, blocks, place, *refs):
    step = pl.program_id(0)
    refs = list(refs)
    count = {"all": 1, "halves": 2 * chunks, "chunks": chunks}
    sources = [[(kind, [refs.pop(0) for _ in range(count[kind])]) for kind in product] for product in plan]
    send, keep = refs[:2]
    holds = refs[2:]
    depth = send.shape[0]
    operands, fills = [], []
    for product in sources:
        row = []
        for kind, items in product:
            if kind == "all":
                row.append(items[0])
            else:
                hold = holds.pop(0)
                fills.append((kind, items, hold))
                row.append(hold)
        operands.append(row)

    @pl.when(step == 0)
    def _():
        for kind, items, hold in fills:
            line_kernel(kind, chunks, half, place, *items, hold)

    def fill(target):
        offset = 0
        for row in operands:
            left = row[0]
            columns = jnp.concatenate(
                [
                    left[:, pl.ds(pl.multiple_of(blocks[step * depth + j] * LANES, LANES), LANES)]
                    for j in range(depth)
                ],
                axis=1,
            )
            for right in row[1:]:
                total = dot_tn(columns, right[...])
                width = total.shape[1]
                target[:, :, offset : offset + width] = total.reshape(depth, LANES, width)
                offset += width

    @pl.when(step == 0)
    def _():
        fill(send)

    @pl.when(step != 0)
    def _():
        fill(keep)


def first_kernel(keep, got, out):
    out[...] = keep[...] + got[...]


def second_kernel(keep, got, near, out):
    out[...] = (keep[0] + got[0]) + near[0]


def third_kernel(keep, got, near, far, *outs):
    at = 0
    for out in outs:
        cut = slice(at, at + out.shape[1])
        out[...] = ((keep[0, :, cut] + got[0, :, cut]) + near[0, :, cut]) + far[:, cut]
        at += out.shape[1]


def whole(array):
    shape = array.shape
    return (array, shape, lambda *_: (0,) * len(shape))


def swap(value, axis, size, bit):
    return lax.ppermute(value, axis, [(i, i ^ bit) for i in range(size)])


class Order:
    def __init__(self):
        self.last = None

    def after(self, value):
        if self.last is None:
            return value
        return lax.optimization_barrier((value, self.last))[0]

    def keep(self, value):
        self.last = value
        return value

    def wait(self, values):
        tied = lax.optimization_barrier((tuple(values), self.last))
        self.last = tied[1]
        return list(tied[0])

    def call(self, kernel, grid, ins, outs, prefetch=(), scratch=(), aliases=None, vmem=16 << 20, name=None):
        arrays = [item[0] for item in ins]
        specs = [
            pl.BlockSpec(memory_space=pl.ANY) if block is None else pl.BlockSpec(block, place)
            for _, block, place in ins
        ]
        body_of = kernel
        if self.last is not None:
            at = len(prefetch) + len(arrays)
            arrays.append(self.last)
            specs.append(pl.BlockSpec(memory_space=pl.ANY))

            def body_of(*refs):
                return kernel(*refs[:at], *refs[at + 1 :])

        results = pl.pallas_call(
            body_of,
            grid_spec=pltpu.PrefetchScalarGridSpec(
                num_scalar_prefetch=len(prefetch),
                grid=grid,
                in_specs=specs,
                out_specs=[pl.BlockSpec(block, place) for _, _, block, place in outs],
                scratch_shapes=list(scratch),
            ),
            out_shape=[jax.ShapeDtypeStruct(shape, kind) for shape, kind, _, _ in outs],
            input_output_aliases=aliases or {},
            compiler_params=pltpu.CompilerParams(
                dimension_semantics=("arbitrary",) * len(grid), vmem_limit_bytes=vmem
            ),
            cost_estimate=pl.CostEstimate(flops=1000, bytes_accessed=1000, transcendentals=0),
            name=name,
        )(*prefetch, *arrays)
        self.last = min(results, key=lambda r: r.size)
        return results


def body(
    dp, tp, tokens, segments, w_query, w_key, w_value, w_out, w_fc1, w_fc2, ln1_gain, ln1_bias, post_gain, post_bias,
    ln2_gain, ln2_bias, mid_gain, mid_bias, query_bias, value_bias, out_bias, fc1_bias, fc2_bias, head_scale, cotangent,
):
    rows, width = tokens.shape
    hw = w_query.shape[1]
    units = w_fc1.shape[1]
    heads = hw // HEAD_DIM
    size = rows // CHUNKS
    half = size // 2
    block = min(256, size)
    line = Order()
    call = line.call
    row = lambda v: v.reshape(1, -1)
    seg = segments.reshape(1, rows)
    ln1_g, ln1_b, post_g, post_b = row(ln1_gain), row(ln1_bias), row(post_gain), row(post_bias)
    ln2_g, ln2_b, mid_g, mid_b = row(ln2_gain), row(ln2_bias), row(mid_gain), row(mid_bias)
    q_b, v_b, out_b, fc1_b, fc2_b = row(query_bias), row(value_bias), row(out_bias), row(fc1_bias), row(fc2_bias)
    scale = row(jnp.repeat(head_scale, HEAD_DIM))
    core = lax.axis_index("tensor") & 1
    place = (core + jnp.arange(2, dtype=jnp.int32)) & 1
    dp_side = lax.axis_index("dp") & 1
    side = dp_side.astype(jnp.int32).reshape(1)
    chunks = list(range(CHUNKS))
    order = chunks[::-1]

    half_rows = width // 2
    part = lax.dynamic_slice_in_dim(w_out, dp_side * half_rows, half_rows, 0).astype(F32)
    far_half = swap(part, "tensor", tp, 2)
    wide = swap(jnp.concatenate([w_out, w_fc1, w_fc2], 1).astype(F32), "tensor", tp, 1)
    pad = jnp.zeros((5, units), F32)
    near = swap(jnp.concatenate([fc1_b, mid_g, mid_b, pad], 0), "tensor", tp, 1)

    step = min(256, rows)
    entry, query, keys, values = call(
        qkv_kernel,
        (rows // step,),
        [(tokens, (step, width), lambda i: (i, 0))]
        + [whole(a) for a in (ln1_g, ln1_b, w_query, w_key, w_value, q_b, v_b)],
        [((rows, width), BF, (step, width), lambda i: (i, 0))]
        + [((rows, hw), BF, (step, hw), lambda i: (i, 0))] * 3,
        name="qkv",
    )

    at0 = lambda c: (lambda *_: (c, 0))
    at1 = lambda c: (lambda *_: (0, c))
    fix = lambda shape, kind: (shape, kind, shape, lambda *_: (0,) * len(shape))
    own = lambda a, c: (a, (half, a.shape[1]), lambda i, p, c=c: (2 * c + p[0], 0))
    own_seg = lambda c: (seg, (1, half), lambda i, p, c=c: (0, 2 * c + p[0]))

    (far_half,) = line.wait([far_half])
    far_rest = swap(far_half, "dp", dp, 1)
    attended, low_ctx, ctx, logsum = {}, {}, {}, {}
    for c in order:
        end = (c + 1) * size
        attended[c], low_ctx[c], mine, theirs, logsum[c] = call(
            functools.partial(attend_kernel, c * size, block),
            (1,),
            [
                (query, (size, hw), at0(c)),
                (keys, (end, hw), at0(0)),
                (values, (end, hw), at0(0)),
                (seg, (1, size), at1(c)),
                (seg, (1, end), at1(0)),
                whole(scale),
            ],
            [fix((size, hw), F32), fix((size, hw), BF), fix((half, hw), F32), fix((half, hw), F32), fix((8, size), F32)],
            prefetch=(place,),
            scratch=[pltpu.VMEM((size, hw), F32)],
            name="attend",
        )
        ctx[c] = (mine, swap(theirs, "tensor", tp, 1))
    far_ctx = {}
    for c in order:
        mine, got = ctx[c]
        ctx[c] = line.keep(jnp.concatenate([line.after(mine), got], 1))
        far_ctx[c] = swap(ctx[c], "tensor", tp, 2)

    step = min(256, width)
    wo_chip, fc1_near, fc2_near = call(
        pack_kernel,
        (width // step,),
        [(a, (step, a.shape[1]), lambda i: (i, 0)) for a in (wide, w_out)],
        [((width, n), BF, (step, n), lambda i: (i, 0)) for n in (2 * hw, units, units)],
        name="pack",
    )
    diag_half = swap(far_half, "tensor", tp, 1)
    diag_rest = swap(far_rest, "tensor", tp, 1)
    (grad_mid,) = call(
        upstream_kernel,
        (CHUNKS,),
        [(cotangent, (half, width), lambda i, p: (2 * i + p[0], 0)), whole(w_fc2), whole(fc2_near)],
        [((CHUNKS * half, 2 * units), F32, (half, 2 * units), lambda i, p: (i, 0))],
        prefetch=(place,),
        name="upstream",
    )
    (wo_far,) = call(
        far_kernel,
        (1,),
        [whole(a) for a in (far_half, far_rest, diag_half, diag_rest)],
        [fix((width, 2 * hw), BF)],
        prefetch=(side,),
        name="far",
    )

    mixed, stream, inner, hidden, stats, far_stats, fsums, near_inner = {}, {}, {}, {}, {}, {}, {}, {}
    for c in order:
        mixed[c], stream[c], inner[c], share, hidden[c], stats[c], fsums[c] = call(
            forward_kernel,
            (1,),
            [own_seg(c)]
            + [whole(a) for a in (ctx[c], far_ctx[c], wo_chip, wo_far, out_b)]
            + [own(tokens, c)]
            + [whole(a) for a in (post_g, post_b, ln2_g, ln2_b, w_fc1, fc1_near, fc1_b, mid_g, near)]
            + [own(cotangent, c), (grad_mid, (half, 2 * units), at0(c))],
            [fix((half, width), F32)] * 2
            + [fix((half, width), BF), fix((half, width), F32), fix((half, 2 * units), F32)]
            + [fix((8, half), F32), fix((8, width), F32)],
            prefetch=(place,),
            name="forward",
        )
        far_stats[c] = swap(stats[c], "tensor", tp, 2)
        near_inner[c] = swap(share, "tensor", tp, 1)

    middle, grad_hid, ffn, back, far_back, gsums, nsums = {}, {}, {}, {}, {}, {}, {}
    near_mid, near_hid = {}, {}
    for c in order:
        mid, hid, share, ffn[c], back[c], gsums[c], nsums[c] = call(
            functools.partial(middle_kernel, units * tp),
            (1,),
            [whole(hidden[c]), (grad_mid, (half, 2 * units), at0(c))]
            + [whole(a) for a in (stats[c], far_stats[c], mid_g, mid_b, near)]
            + [whole(a) for a in (w_fc1, fc1_near, w_fc2, fc2_near)],
            [fix((half, units), BF)] * 2
            + [fix((half, 2 * units), F32)]
            + [fix((half, width), F32), fix((half + PAD, width), F32)]
            + [fix((8, units), F32)] * 2,
            name="middle",
        )
        middle[c], grad_hid[c] = mid, hid
        far_back[c] = swap(back[c], "tensor", tp, 2)
        near_both = swap(share, "tensor", tp, 1)
        near_mid[c] = (near_both, (half, units), lambda *_: (0, 0))
        near_hid[c] = (near_both, (half, units), lambda *_: (0, 1))

    near_blocks = width // dp == LANES and dp == 8
    if near_blocks:
        depth = dp // 2
        me = lax.axis_index("dp")
        ring, across = me // 2, me & 1
        lines = [depth - 1 - (ring ^ 1), ring ^ 1, depth - 1 - ring, ring]
        opposite = [(i, dp - 2 - i + 2 * (i & 1)) for i in range(dp)]
        pairs = [[(i, i ^ bit) for i in range(dp)] for bit in (1, 2)]
        orders = {
            "first": ([2 * at + 1 - across for at in lines] + [2 * at + across for at in lines], pairs + [opposite]),
            "last": (
                [2 * at + side for at in lines for side in (1 - across, across)],
                [pairs[1], opposite, pairs[0]],
            ),
        }

    def weight(plan, items, columns, name, columns_at="first"):
        arrays = [item for group in items for operand in group for item in operand]
        kinds = [kind for product in plan for kind in product]
        holds = [
            pltpu.VMEM((rows, operand[0][1][1]), BF)
            for kind, operand in zip(kinds, [o for g in items for o in g])
            if kind != "all"
        ]
        if not near_blocks:
            results = []
            for product, group in zip(plan, items):
                full = []
                for kind, operand in zip(product, group):
                    if kind == "all":
                        full.append(operand[0][0])
                        continue
                    n = operand[0][1][1]
                    (lined,) = call(
                        functools.partial(line_kernel, kind, CHUNKS, half),
                        (1,),
                        operand,
                        [fix((rows, n), BF)],
                        prefetch=(place,),
                        name=name,
                    )
                    full.append(lined)
                results += [
                    lax.psum_scatter(dot_tn(full[0], right), "dp", scatter_dimension=0, tiled=True)
                    for right in full[1:]
                ]
            return lambda: results
        blocks, perms = orders[columns_at]
        blocks = jnp.stack(blocks).astype(jnp.int32)
        send, keep = call(
            functools.partial(weight_kernel, plan, CHUNKS, half),
            (2,),
            arrays,
            [fix((depth, LANES, columns), F32)] * 2,
            prefetch=(blocks, place),
            scratch=holds,
            name=name,
        )
        got = lax.ppermute(send, "dp", perms[0])

        lanes = min(1024, columns)
        by_lanes = lambda array, count, first: (array, (count, LANES, lanes), lambda i: (first, 0, i))

        def first():
            (send,) = call(
                first_kernel,
                (columns // lanes,),
                [by_lanes(a, 2, 0) for a in (keep, got)],
                [((2, LANES, columns), F32, (2, LANES, lanes), lambda i: (0, 0, i))],
                name="first",
            )
            return lax.ppermute(send, "dp", perms[1])

        def second(near):
            (send,) = call(
                second_kernel,
                (columns // lanes,),
                [by_lanes(a, 1, 2) for a in (keep, got)] + [by_lanes(near, 1, 0)],
                [((LANES, columns), F32, (LANES, lanes), lambda i: (0, i))],
                name="second",
            )
            return lax.ppermute(send, "dp", perms[2])

        def third(near, far):
            return call(
                third_kernel,
                (1,),
                [(a, (1, LANES, columns), lambda *_, f=f: (f, 0, 0)) for a, f in ((keep, 3), (got, 3), (near, 1))]
                + [whole(far)],
                [fix((LANES, operand[0][1][1]), F32) for group in items for operand in group[1:]],
                name="third",
            )

        return first, second, third

    halves = lambda mine, wide_near: [item for c in chunks for item in (whole(mine[c]), wide_near[c])]
    fc2_sum = weight(
        [("all", "halves")],
        [[[whole(cotangent)], halves(middle, near_mid)]],
        units,
        "weight_fc2",
        "last",
    )
    fc1_sum = weight(
        [("halves", "halves")],
        [
            [
                halves(inner, {c: whole(near_inner[c]) for c in chunks}),
                halves(grad_hid, near_hid),
            ]
        ],
        units,
        "weight_fc1",
    )

    own_out = lambda kind, c: ((rows, width), kind, (half, width), lambda i, p, c=c: (2 * c + p[0], 0))
    grown = {"tokens": None, "output": None}

    def grow(which, ins, outs, kernel):
        aliases = None
        if grown[which] is not None:
            aliases = {1 + len(ins): 0}
            ins = ins + [(grown[which], None, None)]
        results = call(kernel, (1,), ins, outs, prefetch=(place,), aliases=aliases, name=which)
        grown[which] = results[0]
        return results[1:]

    def put(which, kind, value, c):
        grow(which, [whole(value)], [((rows, width), kind, (half, width), lambda i, p: (2 * c + p[1], 0))], put_kernel)

    def token(c):
        ins = [(a, (half, width), at0(0)) for a in (chip[c], far_chip[c])]
        ins += [own(tokens, c), whole(grad_stream[c]), whole(ln1_g)]
        (value,) = grow("tokens", ins, [own_out(F32, c), fix((half, width), F32)], token_kernel)
        return swap(value, "tensor", tp, 1)

    def result(c):
        ins = [whole(ffn[c]), whole(far_ffn[c]), whole(stream[c]), whole(fc2_b), own_seg(c)]
        value, osums[c] = grow(
            "output", ins, [own_out(BF, c), fix((half, width), F32), fix((8, width), F32)], output_kernel
        )
        return swap(value, "tensor", tp, 1)

    grad_stream, grad_mix, near_mix, grad_q, grad_k, grad_v, chip, far_chip = {}, {}, {}, {}, {}, {}, {}, {}
    hsums, qsums, esums, far_ffn = {}, {}, {}, {}
    osums, wide_tok, wide_out = {}, {}, {}
    carry = None
    fc2_part = fc1_part = attn_part = None
    for c in order:
        end = (c + 1) * size
        last = c == CHUNKS - 1
        by_half = lambda a: (a, (half, a.shape[1]), lambda i, p: (p[1 - i], 0))
        grad_stream[c], grad_mix[c], wide_mix, ctx_own, ctx_near, hsums[c] = call(
            stream_kernel,
            (1,),
            [whole(a) for a in (back[c], far_back[c], mixed[c], stream[c])]
            + [own(cotangent, c), whole(ln2_g), whole(post_g), whole(wo_chip)],
            [fix((half, width), F32), fix((half, width), BF), fix((half, width), F32)]
            + [fix((half, hw), F32)] * 2
            + [fix((8, width), F32)],
            prefetch=(place,),
            name="stream",
        )
        ctx_near = swap(ctx_near, "tensor", tp, 1)
        near_mix[c] = swap(wide_mix, "tensor", tp, 1)
        results = call(
            functools.partial(attend_back_kernel, c * size, block, last),
            (1,),
            [
                (query, (size, hw), at0(c)),
                (keys, (end, hw), at0(0)),
                (values, (end, hw), at0(0)),
                (seg, (1, size), at1(c)),
                (seg, (1, end), at1(0)),
            ]
            + [whole(a) for a in (ctx_own, ctx_near, attended[c], scale, logsum[c])]
            + ([] if last else [whole(a) for a in carry]),
            [fix((size, hw), BF)] * 3 + [fix((8, hw), F32)] + ([fix((c * size, hw), F32)] * 2 if c else []),
            prefetch=(place,),
            scratch=[pltpu.VMEM((end, hw), F32)] * 2
            + [pltpu.VMEM((end, heads * block), BF)] * 2
            + [pltpu.VMEM((size, hw), BF)],
            name="attend_back",
        )
        grad_q[c], grad_k[c], grad_v[c], qsums[c] = results[:4]
        carry = results[4:]
        if c == order[-1] and near_blocks:
            fc2_part = fc2_sum[0]()
        count = 1 if c == order[-1] else 2
        *sends, keep, esums[c] = call(
            entry_kernel,
            (2,),
            [by_half(a) for a in (grad_q[c], grad_k[c], grad_v[c])]
            + [whole(a) for a in (w_query, w_key, w_value)]
            + [(tokens, (half, width), lambda i, p, c=c: (2 * c + p[1 - i], 0))],
            [fix((half, width // count), F32)] * count + [fix((half, width), F32), fix((8, width), F32)],
            prefetch=(place,),
            name="entry",
        )
        gots = [swap(send, "tensor", tp, 1) for send in sends]
        if c == order[-1]:
            for d in order[:-1]:
                far_ffn[d] = swap(ffn[d], "tensor", tp, 2)
                wide_out[d] = result(d)
            far_ffn[c] = swap(line.after(ffn[c]), "tensor", tp, 2)
        (chip[c],) = call(
            chip_kernel,
            (1,),
            [whole(a) for a in (keep, *gots)],
            [fix((half, width), F32)],
            name="chip",
        )
        far_chip[c] = swap(chip[c], "tensor", tp, 2)

    attn_sum = weight(
        [("halves", "chunks"), ("all", "chunks", "chunks", "chunks")],
        [
            [
                halves(grad_mix, {c: whole(near_mix[c]) for c in chunks}),
                [whole(low_ctx[c]) for c in chunks],
            ],
            [[whole(entry)]] + [[whole(g[c]) for c in chunks] for g in (grad_q, grad_k, grad_v)],
        ],
        4 * hw,
        "weight_attn",
    )
    last = order[-1]
    if near_blocks:
        fc1_part = fc1_sum[0]()
    for c in order[:-1]:
        wide_tok[c] = token(c)
    if near_blocks:
        fc2_last = fc2_sum[1](fc2_part)
    wide_out[last] = result(last)
    if near_blocks:
        fc1_last = fc1_sum[1](fc1_part)

    add = lambda parts: functools.reduce(lambda a, b: a + b, [parts[c] for c in chunks])
    fs, gs, ns, hs, qs, es, os = (add(p) for p in (fsums, gsums, nsums, hsums, qsums, esums, osums))
    own_part = jnp.concatenate([hs[:5], fs[:3], os[:2], es[:2], gs[:3]], 0)
    near_part = jnp.concatenate([hs[:5], fs[:3], os[:2], es[:2], ns[:3]], 0)
    packed = own_part + swap(near_part, "tensor", tp, 1)
    far = swap(packed[10:12], "tensor", tp, 2)
    tail = jnp.concatenate([qs[0], qs[1], qs[2], qs[2]]).reshape(1, -1)[:, :width]
    packed = jnp.concatenate([packed[:10], packed[10:12] + far, packed[12:], tail], 0)
    wide_tok[last] = token(last)
    if near_blocks:
        (grad_w_fc1,) = fc1_sum[2](fc1_part, fc1_last)
        attn_part = attn_sum[0]()
        packed = line.after(packed)
        packed = packed + swap(packed, "dp", dp, 1)
        packed = packed + swap(packed, "dp", dp, 2)
    else:
        packed = lax.psum(packed, "dp")
    wides = line.wait([wide[c] for wide in (wide_tok, wide_out) for c in order])
    for index, c in enumerate(order):
        put("tokens", F32, wides[index], c)
        put("output", BF, wides[len(order) + index], c)
    if near_blocks:
        packed = line.keep(line.after(packed))
        attn_last = attn_sum[1](attn_part)
        packed = line.after(packed)
        packed = packed + lax.ppermute(packed, "dp", opposite)
        (grad_w_fc2,) = fc2_sum[2](fc2_part, fc2_last)
        grad_w_out, grad_w_query, grad_w_key, grad_w_value = attn_sum[2](attn_part, attn_last)
    else:
        (grad_w_fc2,), (grad_w_fc1,) = fc2_sum(), fc1_sum()
        grad_w_out, grad_w_query, grad_w_key, grad_w_value = attn_sum()
    grad_tokens, output = grown["tokens"], grown["output"]

    last_row = packed[15]
    counted = packed[7, 0]
    squares = jnp.stack([jnp.sum(packed[5]), jnp.sum(packed[8]), jnp.sum(packed[9])])
    rms = jnp.sqrt(squares / (counted * width))
    grad_head = jnp.sum(last_row[2 * hw : 3 * hw].reshape(heads, HEAD_DIM), axis=1)
    return (
        output,
        grad_tokens,
        grad_w_query,
        grad_w_key,
        grad_w_value,
        grad_w_out,
        grad_w_fc1,
        grad_w_fc2,
        packed[10],
        packed[11],
        packed[2],
        packed[3],
        packed[0],
        packed[1],
        packed[12],
        packed[13],
        last_row[:hw],
        last_row[hw : 2 * hw],
        packed[4],
        packed[14],
        packed[6],
        grad_head,
        rms,
    )


def solution(mesh):
    cut = P(None, "tensor")
    part = P("tensor")
    rows = P("dp", None)
    both = P("dp", "tensor")
    return jax.shard_map(
        functools.partial(body, mesh.shape["dp"], mesh.shape["tensor"]),
        mesh=mesh,
        in_specs=(rows, rows) + (cut,) * 6 + (P(),) * 6 + (part,) * 4 + (P(), part, P(), part, rows),
        out_specs=(rows, rows) + (both,) * 6 + (P(),) * 6 + (part,) * 4 + (P(), part, P(), part, P()),
        check_vma=False,
    )
```

```python
import functools

import jax
import jax.numpy as jnp
from jax import lax
from jax.experimental import pallas as pl
from jax.experimental.pallas import tpu as pltpu
from jax.sharding import PartitionSpec as P

HEAD_DIM = 64
EPSILON = 1e-05
EXCLUDED = -1e30
LANES = 128
CHUNKS = 2
PAD = 16
BF = jnp.bfloat16
F32 = jnp.float32


def dot_nn(a, b):
    return lax.dot_general(a, b, (((1,), (0,)), ((), ())), preferred_element_type=F32)


def dot_nt(a, b):
    return lax.dot_general(a, b, (((1,), (1,)), ((), ())), preferred_element_type=F32)


def dot_tn(a, b):
    return lax.dot_general(a, b, (((0,), (0,)), ((), ())), preferred_element_type=F32)


def normalize(v):
    mean = jnp.mean(v, axis=-1, keepdims=True)
    centred = v - mean
    factor = lax.rsqrt(jnp.mean(centred * centred, axis=-1, keepdims=True) + EPSILON)
    return centred * factor, factor


def norm_back(scaled, normed, factor):
    return factor * (
        scaled
        - jnp.mean(scaled, axis=-1, keepdims=True)
        - normed * jnp.mean(scaled * normed, axis=-1, keepdims=True)
    )


def col_sum(v):
    return jnp.sum(v, axis=0, keepdims=True)


def tanh_inner(v):
    return 0.7978845608028654 * (v + 0.044715 * (v * v * v))


def columns_to_rows(columns):
    n = columns[0].shape[0]
    lane = lax.broadcasted_iota(jnp.int32, (n, LANES), 1)
    tile = jnp.zeros((n, LANES), F32)
    for index, column in enumerate(columns):
        tile = jnp.where(lane == index, column, tile)
    return jnp.transpose(tile)[:8]


def rows_to_columns(rows):
    n = rows[0].shape[1]
    sub = lax.broadcasted_iota(jnp.int32, (LANES, n), 0)
    tile = jnp.zeros((LANES, n), F32)
    for index, row in enumerate(rows):
        tile = jnp.where(sub == index, row, tile)
    tile = jnp.transpose(tile)
    return [tile[:, index : index + 1] for index in range(len(rows))]


def stack_rows(rows, width):
    sub = lax.broadcasted_iota(jnp.int32, (8, width), 0)
    tile = jnp.zeros((8, width), F32)
    for index, row in enumerate(rows):
        tile = jnp.where(sub == index, row, tile)
    return tile


def head_masks(width, kind):
    lane = lax.broadcasted_iota(jnp.int32, (1, width), 1) // HEAD_DIM
    return [(lane == head).astype(F32).astype(kind) for head in range(width // HEAD_DIM)]


def qkv_kernel(tok, gain, bias, wq, wk, wv, qb, vb, entry, q, k, v):
    normed, _ = normalize(tok[...].astype(F32))
    low = (normed * gain[...] + bias[...]).astype(BF)
    entry[...] = low
    q[...] = ((dot_nn(low, wq[...]) + qb[...]) * HEAD_DIM**-0.5).astype(BF)
    k[...] = dot_nn(low, wk[...]).astype(BF)
    v[...] = (dot_nn(low, wv[...]) + vb[...]).astype(BF)


def attend_kernel(first, block, place, q, k, v, segq, segk, scale, attended, low, mine, theirs, logsum, hold):
    rows, width = q.shape
    half = rows // 2
    masks = head_masks(width, BF)
    for at in range(0, rows, block):
        length = first + at + block
        query = q[at : at + block, :]
        keys = k[:length, :]
        (seg,) = rows_to_columns([segq[:, at : at + block].astype(F32)])
        place_q = first + at + lax.broadcasted_iota(jnp.int32, (block, length), 0)
        place_k = lax.broadcasted_iota(jnp.int32, (block, length), 1)
        allowed = (seg == segk[:, :length].astype(F32)) & (place_k <= place_q)
        shift = jnp.where(allowed, 0.0, EXCLUDED)
        total = jnp.zeros((block, width), F32)
        sums = []
        for mask in masks:
            scores = dot_nt(query * mask, keys) + shift
            top = jnp.max(scores, axis=-1, keepdims=True)
            expo = jnp.exp(scores - top)
            norm = jnp.sum(expo, axis=-1, keepdims=True)
            weights = (expo * (1.0 / norm)).astype(BF)
            total = total + dot_nn(weights, v[:length, :] * mask)
            sums.append(top + jnp.log(norm))
        attended[at : at + block, :] = total
        context = (total * scale[...]).astype(BF)
        low[at : at + block, :] = context
        hold[at : at + block, :] = context.astype(F32)
        logsum[:, at : at + block] = columns_to_rows(sums)
    mine[...] = hold[pl.ds(pl.multiple_of(place[0] * half, half), half), :]
    theirs[...] = hold[pl.ds(pl.multiple_of(place[1] * half, half), half), :]


def pack_kernel(wide, near_out, out_pair, fc1, fc2):
    width, units = near_out.shape[1], fc1.shape[1]
    out_pair[:, :width] = near_out[...]
    out_pair[:, width:] = wide[:, :width].astype(BF)
    fc1[...] = wide[:, width : width + units].astype(BF)
    fc2[...] = wide[:, width + units :].astype(BF)


def far_kernel(side, far_half, far_rest, diag_half, diag_rest, out):
    rows, width = far_half.shape
    here = pl.ds(pl.multiple_of(side[0] * rows, rows), rows)
    there = pl.ds(pl.multiple_of((1 - side[0]) * rows, rows), rows)
    out[here, :width] = far_half[...].astype(BF)
    out[there, :width] = far_rest[...].astype(BF)
    out[here, width:] = diag_half[...].astype(BF)
    out[there, width:] = diag_rest[...].astype(BF)


def upstream_kernel(place, cot, own, near, out):
    units = own.shape[1]
    out[:, :units] = dot_nn(cot[...], own[...])
    out[:, units:] = dot_nn(cot[...], near[...])


def forward_kernel(
    place, seg, ctx_chip, ctx_far, wo_chip, wo_far, out_bias, tok, post_gain, post_bias, ln2_gain, ln2_bias,
    fc1_own, fc1_near, fc1_bias, mid_gain, near, cot, grad_middle,
    mixed, stream, inner, share, hidden, stats, sums,
):
    units = fc1_own.shape[1]
    mix = (
        dot_nt(ctx_chip[...].astype(BF), wo_chip[...]) + dot_nt(ctx_far[...].astype(BF), wo_far[...])
    ) + out_bias[...]
    mixed[...] = mix
    normed, _ = normalize(mix)
    branch = normed * post_gain[...] + post_bias[...]
    resid = tok[...].astype(F32) + branch
    stream[...] = resid
    normed2, _ = normalize(resid)
    low = (normed2 * ln2_gain[...] + ln2_bias[...]).astype(BF)
    inner[...] = low
    share[...] = low.astype(F32)
    actives, scaleds = [], []
    for part, (weight, bias, gain) in enumerate(
        ((fc1_own, fc1_bias[...], mid_gain[...]), (fc1_near, near[0:1, :], near[1:2, :]))
    ):
        hid = dot_nn(low, weight[...]) + bias
        hidden[:, part * units : (part + 1) * units] = hid
        actives.append(0.5 * hid * (1.0 + jnp.tanh(tanh_inner(hid))))
        scaleds.append(grad_middle[:, part * units : (part + 1) * units] * gain)

    def both(left, right):
        return jnp.sum(left, axis=-1, keepdims=True) + jnp.sum(right, axis=-1, keepdims=True)

    mean = both(*actives) / (2 * units)
    centred = [active - mean for active in actives]
    stats[...] = columns_to_rows(
        [
            mean,
            both(*[c * c for c in centred]),
            both(*scaleds),
            both(*[s * c for s, c in zip(scaleds, centred)]),
        ]
    )
    (which,) = rows_to_columns([seg[...].astype(F32)])
    valid = (which >= 0).astype(F32)
    sums[...] = stack_rows(
        [
            col_sum(valid * branch * branch),
            col_sum(cot[...].astype(F32)),
            col_sum(valid * jnp.ones_like(branch)),
        ],
        branch.shape[1],
    )


def middle_kernel(
    total, hidden, grad_middle, st0, st1, mid_gain, mid_bias, near,
    fc1_own, fc1_near, fc2_own, fc2_near,
    middle, grad_hidden, share, ffn, back, sums_own, sums_near,
):
    units = fc1_own.shape[1]
    n = 2 * units
    mean = (st0[0:1, :] + st1[0:1, :]) * 0.5
    apart = [s[0:1, :] - mean for s in (st0, st1)]
    spread = (st0[1:2, :] + n * (apart[0] * apart[0])) + (st1[1:2, :] + n * (apart[1] * apart[1]))
    factor = lax.rsqrt(spread / total + EPSILON)
    plain = (st0[2:3, :] + st1[2:3, :]) / total
    along = (st0[3:4, :] + apart[0] * st0[2:3, :]) + (st1[3:4, :] + apart[1] * st1[2:3, :])
    mean, factor, plain, along = rows_to_columns([mean, factor, plain, factor * along / total])
    parts = (
        (mid_gain[...], mid_bias[...], fc1_own, fc2_own, sums_own),
        (near[1:2, :], near[2:3, :], fc1_near, fc2_near, sums_near),
    )
    ffn_parts, back_parts = [], []
    for part, (gain, bias, fc1, fc2, sums) in enumerate(parts):
        hid = hidden[:, part * units : (part + 1) * units]
        bend = jnp.tanh(tanh_inner(hid))
        active = 0.5 * hid * (1.0 + bend)
        slope = 0.5 * (1.0 + bend) + 0.5 * hid * (1.0 - bend * bend) * (
            0.7978845608028654 * (1.0 + 3 * 0.044715 * (hid * hid))
        )
        normed = (active - mean) * factor
        mid = (normed * gain + bias).astype(BF)
        grad = grad_middle[:, part * units : (part + 1) * units]
        low = (factor * (grad * gain - plain - normed * along) * slope).astype(BF)
        if part == 0:
            middle[...] = mid
            grad_hidden[...] = low
        else:
            share[:, :units] = mid.astype(F32)
            share[:, units:] = low.astype(F32)
        sums[...] = stack_rows([col_sum(grad * normed), col_sum(grad), col_sum(low.astype(F32))], units)
        ffn_parts.append(dot_nt(mid, fc2[...]))
        back_parts.append(dot_nt(low, fc1[...]))
    ffn[...] = ffn_parts[0] + ffn_parts[1]
    back[: hidden.shape[0], :] = back_parts[0] + back_parts[1]
    back[hidden.shape[0] :, :] = jnp.zeros((PAD, back.shape[1]), F32)


def stream_kernel(
    place, mine, far, mixed, stream, cot, ln2_gain, post_gain, w_out,
    grad_stream, grad_mixed, wide, context_own, context_near, sums,
):
    grad = mine[: stream.shape[0], :] + far[: stream.shape[0], :]
    normed2, factor2 = normalize(stream[...])
    back = cot[...].astype(F32) + norm_back(grad * ln2_gain[...], normed2, factor2)
    grad_stream[...] = back
    normedp, factorp = normalize(mixed[...])
    low = norm_back(back * post_gain[...], normedp, factorp).astype(BF)
    grad_mixed[...] = low
    wide[...] = low.astype(F32)
    context = dot_nn(low, w_out[...])
    width = context_own.shape[1]
    context_own[...] = context[:, :width]
    context_near[...] = context[:, width:]
    sums[...] = stack_rows(
        [
            col_sum(grad * normed2),
            col_sum(grad),
            col_sum(back * normedp),
            col_sum(back),
            col_sum(low.astype(F32)),
        ],
        back.shape[1],
    )


def attend_back_kernel(first, block, last, place, *refs):
    q, k, v, segq, segk, context_own, context_near, attended, scale, logsum = refs[:10]
    rest = list(refs[10:])
    if not last:
        key_in, value_in = rest[:2]
        rest = rest[2:]
    grad_q, grad_k, grad_v, sums = rest[:4]
    rest = rest[4:]
    if first:
        key_out, value_out = rest[:2]
        rest = rest[2:]
    key_sum, value_sum, low_probs, low_scores, grads = rest
    rows, width = q.shape
    half = rows // 2
    end = first + rows
    masks = head_masks(width, BF)
    wide_masks = head_masks(width, F32)
    if last:
        key_sum[...] = jnp.zeros_like(key_sum)
        value_sum[...] = jnp.zeros_like(value_sum)
    else:
        key_sum[...] = key_in[...]
        value_sum[...] = value_in[...]
    head_sum = jnp.zeros((1, width), F32)
    for part, source in enumerate((context_own, context_near)):
        at = pl.ds(pl.multiple_of(place[part] * half, half), half)
        grad_context = source[...]
        head_sum = head_sum + col_sum(grad_context * attended[at, :])
        grads[at, :] = (grad_context * scale[...]).astype(BF)
    (seg,) = rows_to_columns([segk[:, :end].astype(F32)])
    query_sum = jnp.zeros((1, width), F32)
    for at in range(0, rows, block):
        length = first + at + block
        query = q[at : at + block, :]
        grad = grads[at : at + block, :]
        product = grad.astype(F32) * attended[at : at + block, :]
        delta = columns_to_rows([jnp.sum(product * mask, axis=-1, keepdims=True) for mask in wide_masks])
        place_k = lax.broadcasted_iota(jnp.int32, (length, block), 0)
        place_q = first + at + lax.broadcasted_iota(jnp.int32, (length, block), 1)
        allowed = (seg[:length] == segq[:, at : at + block].astype(F32)) & (place_k <= place_q)
        shift = jnp.where(allowed, 0.0, EXCLUDED)
        queries = [query * mask for mask in masks]
        grad_parts = [grad * mask for mask in masks]
        grad_query = jnp.zeros((block, width), F32)
        for head, mask in enumerate(masks):
            scores = dot_nt(k[:length, :], queries[head]) + shift
            probs = jnp.exp(scores - logsum[head : head + 1, at : at + block])
            low_probs[:length, head * block : (head + 1) * block] = probs.astype(BF)
            grad_probs = dot_nt(v[:length, :], grad_parts[head])
            low = (probs * (grad_probs - delta[head : head + 1, :])).astype(BF)
            low_scores[:length, head * block : (head + 1) * block] = low
            grad_query = grad_query + dot_tn(low, k[:length, :] * mask)
        value_sum[:length, :] += dot_nn(low_probs[:length, :], jnp.concatenate(grad_parts, axis=0))
        key_sum[:length, :] += dot_nn(low_scores[:length, :], jnp.concatenate(queries, axis=0))
        low_query = (grad_query * HEAD_DIM**-0.5).astype(BF)
        grad_q[at : at + block, :] = low_query
        query_sum = query_sum + col_sum(low_query.astype(F32))
    grad_k[...] = key_sum[first:end, :].astype(BF)
    low_value = value_sum[first:end, :].astype(BF)
    grad_v[...] = low_value
    sums[...] = stack_rows([query_sum, col_sum(low_value.astype(F32)), head_sum], width)
    if first:
        key_out[...] = key_sum[:first, :]
        value_out[...] = value_sum[:first, :]


def entry_kernel(place, grad_q, grad_k, grad_v, wq, wk, wv, tok, *refs):
    sends, (keep, sums) = refs[:-2], refs[-2:]
    step = pl.program_id(0)
    part = dot_nt(grad_q[...], wq[...]) + dot_nt(grad_k[...], wk[...]) + dot_nt(grad_v[...], wv[...])
    normed, _ = normalize(tok[...].astype(F32))
    fresh = stack_rows([col_sum(part * normed), col_sum(part)], part.shape[1])

    @pl.when(step == 0)
    def _():
        sums[...] = fresh
        cut = sends[0].shape[1]
        for j, send in enumerate(sends):
            send[...] = part[:, j * cut : (j + 1) * cut]

    @pl.when(step != 0)
    def _():
        sums[...] += fresh
        keep[...] = part


def chip_kernel(keep, *refs):
    gots, out = refs[:-1], refs[-1]
    cut = gots[0].shape[1]
    for j, got in enumerate(gots):
        out[:, j * cut : (j + 1) * cut] = keep[:, j * cut : (j + 1) * cut] + got[...]


def token_kernel(place, mine, far, tok, grad_stream, gain, *refs):
    out, wide = refs[-2:]
    normed, factor = normalize(tok[...].astype(F32))
    grad = grad_stream[...] + norm_back((mine[...] + far[...]) * gain[...], normed, factor)
    out[...] = grad
    wide[...] = grad


def output_kernel(place, mine, far, stream, bias, seg, *refs):
    out, wide, sums = refs[-3:]
    ffn = (mine[...] + far[...]) + bias[...]
    result = stream[...] + ffn
    low = result.astype(BF)
    out[...] = low
    wide[...] = low.astype(F32)
    (which,) = rows_to_columns([seg[...].astype(F32)])
    valid = (which >= 0).astype(F32)
    sums[...] = stack_rows([col_sum(valid * ffn * ffn), col_sum(valid * result * result)], ffn.shape[1])


def put_kernel(place, value, full, out):
    out[...] = value[...].astype(out.dtype)


def line_kernel(kind, chunks, half, place, *refs):
    items, out = refs[:-1], refs[-1]
    for c in range(chunks):
        if kind == "chunks":
            out[2 * c * half : 2 * (c + 1) * half, :] = items[c][...]
        else:
            for part in range(2):
                at = pl.ds(pl.multiple_of((2 * c + place[part]) * half, half), half)
                out[at, :] = items[2 * c + part][...].astype(BF)


def weight_kernel(plan, chunks, half, blocks, place, *refs):
    step = pl.program_id(0)
    refs = list(refs)
    count = {"all": 1, "halves": 2 * chunks, "chunks": chunks}
    sources = [[(kind, [refs.pop(0) for _ in range(count[kind])]) for kind in product] for product in plan]
    send, keep = refs[:2]
    holds = refs[2:]
    depth = send.shape[0]
    operands, fills = [], []
    for product in sources:
        row = []
        for kind, items in product:
            if kind == "all":
                row.append(items[0])
            else:
                hold = holds.pop(0)
                fills.append((kind, items, hold))
                row.append(hold)
        operands.append(row)

    @pl.when(step == 0)
    def _():
        for kind, items, hold in fills:
            line_kernel(kind, chunks, half, place, *items, hold)

    def fill(target):
        offset = 0
        for row in operands:
            left = row[0]
            columns = jnp.concatenate(
                [
                    left[:, pl.ds(pl.multiple_of(blocks[step * depth + j] * LANES, LANES), LANES)]
                    for j in range(depth)
                ],
                axis=1,
            )
            for right in row[1:]:
                total = dot_tn(columns, right[...])
                width = total.shape[1]
                target[:, :, offset : offset + width] = total.reshape(depth, LANES, width)
                offset += width

    @pl.when(step == 0)
    def _():
        fill(send)

    @pl.when(step != 0)
    def _():
        fill(keep)


def first_kernel(keep, got, out):
    out[...] = keep[...] + got[...]


def second_kernel(keep, got, near, out):
    out[...] = (keep[0] + got[0]) + near[0]


def third_kernel(keep, got, near, far, *outs):
    at = 0
    for out in outs:
        cut = slice(at, at + out.shape[1])
        out[...] = ((keep[0, :, cut] + got[0, :, cut]) + near[0, :, cut]) + far[:, cut]
        at += out.shape[1]


def whole(array):
    shape = array.shape
    return (array, shape, lambda *_: (0,) * len(shape))


def swap(value, axis, size, bit):
    return lax.ppermute(value, axis, [(i, i ^ bit) for i in range(size)])


class Order:
    def __init__(self):
        self.last = None

    def after(self, value):
        if self.last is None:
            return value
        return lax.optimization_barrier((value, self.last))[0]

    def keep(self, value):
        self.last = value
        return value

    def wait(self, values):
        tied = lax.optimization_barrier((tuple(values), self.last))
        self.last = tied[1]
        return list(tied[0])

    def call(self, kernel, grid, ins, outs, prefetch=(), scratch=(), aliases=None, vmem=16 << 20, name=None):
        arrays = [item[0] for item in ins]
        specs = [
            pl.BlockSpec(memory_space=pl.ANY) if block is None else pl.BlockSpec(block, place)
            for _, block, place in ins
        ]
        body_of = kernel
        if self.last is not None:
            at = len(prefetch) + len(arrays)
            arrays.append(self.last)
            specs.append(pl.BlockSpec(memory_space=pl.ANY))

            def body_of(*refs):
                return kernel(*refs[:at], *refs[at + 1 :])

        results = pl.pallas_call(
            body_of,
            grid_spec=pltpu.PrefetchScalarGridSpec(
                num_scalar_prefetch=len(prefetch),
                grid=grid,
                in_specs=specs,
                out_specs=[pl.BlockSpec(block, place) for _, _, block, place in outs],
                scratch_shapes=list(scratch),
            ),
            out_shape=[jax.ShapeDtypeStruct(shape, kind) for shape, kind, _, _ in outs],
            input_output_aliases=aliases or {},
            compiler_params=pltpu.CompilerParams(
                dimension_semantics=("arbitrary",) * len(grid), vmem_limit_bytes=vmem
            ),
            cost_estimate=pl.CostEstimate(flops=1000, bytes_accessed=1000, transcendentals=0),
            name=name,
        )(*prefetch, *arrays)
        self.last = min(results, key=lambda r: r.size)
        return results


def body(
    dp, tp, tokens, segments, w_query, w_key, w_value, w_out, w_fc1, w_fc2, ln1_gain, ln1_bias, post_gain, post_bias,
    ln2_gain, ln2_bias, mid_gain, mid_bias, query_bias, value_bias, out_bias, fc1_bias, fc2_bias, head_scale, cotangent,
):
    rows, width = tokens.shape
    hw = w_query.shape[1]
    units = w_fc1.shape[1]
    heads = hw // HEAD_DIM
    size = rows // CHUNKS
    half = size // 2
    block = min(256, size)
    line = Order()
    call = line.call
    row = lambda v: v.reshape(1, -1)
    seg = segments.reshape(1, rows)
    ln1_g, ln1_b, post_g, post_b = row(ln1_gain), row(ln1_bias), row(post_gain), row(post_bias)
    ln2_g, ln2_b, mid_g, mid_b = row(ln2_gain), row(ln2_bias), row(mid_gain), row(mid_bias)
    q_b, v_b, out_b, fc1_b, fc2_b = row(query_bias), row(value_bias), row(out_bias), row(fc1_bias), row(fc2_bias)
    scale = row(jnp.repeat(head_scale, HEAD_DIM))
    core = lax.axis_index("tensor") & 1
    place = (core + jnp.arange(2, dtype=jnp.int32)) & 1
    dp_side = lax.axis_index("dp") & 1
    side = dp_side.astype(jnp.int32).reshape(1)
    chunks = list(range(CHUNKS))
    order = chunks[::-1]

    half_rows = width // 2
    part = lax.dynamic_slice_in_dim(w_out, dp_side * half_rows, half_rows, 0).astype(F32)
    far_half = swap(part, "tensor", tp, 2)
    wide = swap(jnp.concatenate([w_out, w_fc1, w_fc2], 1).astype(F32), "tensor", tp, 1)
    pad = jnp.zeros((5, units), F32)
    near = swap(jnp.concatenate([fc1_b, mid_g, mid_b, pad], 0), "tensor", tp, 1)

    step = min(256, rows)
    entry, query, keys, values = call(
        qkv_kernel,
        (rows // step,),
        [(tokens, (step, width), lambda i: (i, 0))]
        + [whole(a) for a in (ln1_g, ln1_b, w_query, w_key, w_value, q_b, v_b)],
        [((rows, width), BF, (step, width), lambda i: (i, 0))]
        + [((rows, hw), BF, (step, hw), lambda i: (i, 0))] * 3,
        name="qkv",
    )

    at0 = lambda c: (lambda *_: (c, 0))
    at1 = lambda c: (lambda *_: (0, c))
    fix = lambda shape, kind: (shape, kind, shape, lambda *_: (0,) * len(shape))
    own = lambda a, c: (a, (half, a.shape[1]), lambda i, p, c=c: (2 * c + p[0], 0))
    own_seg = lambda c: (seg, (1, half), lambda i, p, c=c: (0, 2 * c + p[0]))

    attended, low_ctx, ctx, logsum = {}, {}, {}, {}
    for c in order:
        end = (c + 1) * size
        attended[c], low_ctx[c], mine, theirs, logsum[c] = call(
            functools.partial(attend_kernel, c * size, block),
            (1,),
            [
                (query, (size, hw), at0(c)),
                (keys, (end, hw), at0(0)),
                (values, (end, hw), at0(0)),
                (seg, (1, size), at1(c)),
                (seg, (1, end), at1(0)),
                whole(scale),
            ],
            [fix((size, hw), F32), fix((size, hw), BF), fix((half, hw), F32), fix((half, hw), F32), fix((8, size), F32)],
            prefetch=(place,),
            scratch=[pltpu.VMEM((size, hw), F32)],
            name="attend",
        )
        ctx[c] = (mine, swap(theirs, "tensor", tp, 1))
        if c == order[0]:
            (far_half,) = line.wait([far_half])
            far_rest = swap(far_half, "dp", dp, 1)
    far_ctx = {}
    for c in order:
        mine, got = ctx[c]
        ctx[c] = line.keep(jnp.concatenate([line.after(mine), got], 1))
        far_ctx[c] = swap(ctx[c], "tensor", tp, 2)

    step = min(256, width)
    wo_chip, fc1_near, fc2_near = call(
        pack_kernel,
        (width // step,),
        [(a, (step, a.shape[1]), lambda i: (i, 0)) for a in (wide, w_out)],
        [((width, n), BF, (step, n), lambda i: (i, 0)) for n in (2 * hw, units, units)],
        name="pack",
    )
    (far_rest,) = line.wait([far_rest])
    diag_half = swap(far_half, "tensor", tp, 1)
    diag_rest = swap(far_rest, "tensor", tp, 1)
    (grad_mid,) = call(
        upstream_kernel,
        (CHUNKS,),
        [(cotangent, (half, width), lambda i, p: (2 * i + p[0], 0)), whole(w_fc2), whole(fc2_near)],
        [((CHUNKS * half, 2 * units), F32, (half, 2 * units), lambda i, p: (i, 0))],
        prefetch=(place,),
        name="upstream",
    )
    (wo_far,) = call(
        far_kernel,
        (1,),
        [whole(a) for a in (far_half, far_rest, diag_half, diag_rest)],
        [fix((width, 2 * hw), BF)],
        prefetch=(side,),
        name="far",
    )

    mixed, stream, inner, hidden, stats, far_stats, fsums, near_inner = {}, {}, {}, {}, {}, {}, {}, {}
    for c in order:
        mixed[c], stream[c], inner[c], share, hidden[c], stats[c], fsums[c] = call(
            forward_kernel,
            (1,),
            [own_seg(c)]
            + [whole(a) for a in (ctx[c], far_ctx[c], wo_chip, wo_far, out_b)]
            + [own(tokens, c)]
            + [whole(a) for a in (post_g, post_b, ln2_g, ln2_b, w_fc1, fc1_near, fc1_b, mid_g, near)]
            + [own(cotangent, c), (grad_mid, (half, 2 * units), at0(c))],
            [fix((half, width), F32)] * 2
            + [fix((half, width), BF), fix((half, width), F32), fix((half, 2 * units), F32)]
            + [fix((8, half), F32), fix((8, width), F32)],
            prefetch=(place,),
            name="forward",
        )
        far_stats[c] = swap(stats[c], "tensor", tp, 2)
        near_inner[c] = swap(share, "tensor", tp, 1)

    middle, grad_hid, ffn, back, far_back, gsums, nsums = {}, {}, {}, {}, {}, {}, {}
    near_mid, near_hid = {}, {}
    for c in order:
        mid, hid, share, ffn[c], back[c], gsums[c], nsums[c] = call(
            functools.partial(middle_kernel, units * tp),
            (1,),
            [whole(hidden[c]), (grad_mid, (half, 2 * units), at0(c))]
            + [whole(a) for a in (stats[c], far_stats[c], mid_g, mid_b, near)]
            + [whole(a) for a in (w_fc1, fc1_near, w_fc2, fc2_near)],
            [fix((half, units), BF)] * 2
            + [fix((half, 2 * units), F32)]
            + [fix((half, width), F32), fix((half + PAD, width), F32)]
            + [fix((8, units), F32)] * 2,
            name="middle",
        )
        middle[c], grad_hid[c] = mid, hid
        far_back[c] = swap(back[c], "tensor", tp, 2)
        near_both = swap(share, "tensor", tp, 1)
        near_mid[c] = (near_both, (half, units), lambda *_: (0, 0))
        near_hid[c] = (near_both, (half, units), lambda *_: (0, 1))

    near_blocks = width // dp == LANES and dp == 8
    if near_blocks:
        depth = dp // 2
        me = lax.axis_index("dp")
        ring, across = me // 2, me & 1
        lines = [depth - 1 - (ring ^ 1), ring ^ 1, depth - 1 - ring, ring]
        opposite = [(i, dp - 2 - i + 2 * (i & 1)) for i in range(dp)]
        pairs = [[(i, i ^ bit) for i in range(dp)] for bit in (1, 2)]
        orders = {
            "first": ([2 * at + 1 - across for at in lines] + [2 * at + across for at in lines], pairs + [opposite]),
            "last": (
                [2 * at + side for at in lines for side in (1 - across, across)],
                [pairs[1], opposite, pairs[0]],
            ),
        }

    def weight(plan, items, columns, name, columns_at="first"):
        arrays = [item for group in items for operand in group for item in operand]
        kinds = [kind for product in plan for kind in product]
        holds = [
            pltpu.VMEM((rows, operand[0][1][1]), BF)
            for kind, operand in zip(kinds, [o for g in items for o in g])
            if kind != "all"
        ]
        if not near_blocks:
            results = []
            for product, group in zip(plan, items):
                full = []
                for kind, operand in zip(product, group):
                    if kind == "all":
                        full.append(operand[0][0])
                        continue
                    n = operand[0][1][1]
                    (lined,) = call(
                        functools.partial(line_kernel, kind, CHUNKS, half),
                        (1,),
                        operand,
                        [fix((rows, n), BF)],
                        prefetch=(place,),
                        name=name,
                    )
                    full.append(lined)
                results += [
                    lax.psum_scatter(dot_tn(full[0], right), "dp", scatter_dimension=0, tiled=True)
                    for right in full[1:]
                ]
            return lambda: results
        blocks, perms = orders[columns_at]
        blocks = jnp.stack(blocks).astype(jnp.int32)
        send, keep = call(
            functools.partial(weight_kernel, plan, CHUNKS, half),
            (2,),
            arrays,
            [fix((depth, LANES, columns), F32)] * 2,
            prefetch=(blocks, place),
            scratch=holds,
            name=name,
        )
        got = lax.ppermute(send, "dp", perms[0])

        lanes = min(1024, columns)
        by_lanes = lambda array, count, first: (array, (count, LANES, lanes), lambda i: (first, 0, i))

        def first():
            (send,) = call(
                first_kernel,
                (columns // lanes,),
                [by_lanes(a, 2, 0) for a in (keep, got)],
                [((2, LANES, columns), F32, (2, LANES, lanes), lambda i: (0, 0, i))],
                name="first",
            )
            return lax.ppermute(send, "dp", perms[1])

        def second(near):
            (send,) = call(
                second_kernel,
                (columns // lanes,),
                [by_lanes(a, 1, 2) for a in (keep, got)] + [by_lanes(near, 1, 0)],
                [((LANES, columns), F32, (LANES, lanes), lambda i: (0, i))],
                name="second",
            )
            return lax.ppermute(send, "dp", perms[2])

        def third(near, far):
            return call(
                third_kernel,
                (1,),
                [(a, (1, LANES, columns), lambda *_, f=f: (f, 0, 0)) for a, f in ((keep, 3), (got, 3), (near, 1))]
                + [whole(far)],
                [fix((LANES, operand[0][1][1]), F32) for group in items for operand in group[1:]],
                name="third",
            )

        return first, second, third

    halves = lambda mine, wide_near: [item for c in chunks for item in (whole(mine[c]), wide_near[c])]
    fc2_sum = weight(
        [("all", "halves")],
        [[[whole(cotangent)], halves(middle, near_mid)]],
        units,
        "weight_fc2",
        "last",
    )
    fc1_sum = weight(
        [("halves", "halves")],
        [
            [
                halves(inner, {c: whole(near_inner[c]) for c in chunks}),
                halves(grad_hid, near_hid),
            ]
        ],
        units,
        "weight_fc1",
    )

    own_out = lambda kind, c: ((rows, width), kind, (half, width), lambda i, p, c=c: (2 * c + p[0], 0))
    grown = {"tokens": None, "output": None}

    def grow(which, ins, outs, kernel):
        aliases = None
        if grown[which] is not None:
            aliases = {1 + len(ins): 0}
            ins = ins + [(grown[which], None, None)]
        results = call(kernel, (1,), ins, outs, prefetch=(place,), aliases=aliases, name=which)
        grown[which] = results[0]
        return results[1:]

    def put(which, kind, value, c):
        grow(which, [whole(value)], [((rows, width), kind, (half, width), lambda i, p: (2 * c + p[1], 0))], put_kernel)

    def token(c):
        ins = [(a, (half, width), at0(0)) for a in (chip[c], far_chip[c])]
        ins += [own(tokens, c), whole(grad_stream[c]), whole(ln1_g)]
        (value,) = grow("tokens", ins, [own_out(F32, c), fix((half, width), F32)], token_kernel)
        return swap(value, "tensor", tp, 1)

    def result(c):
        ins = [whole(ffn[c]), whole(far_ffn[c]), whole(stream[c]), whole(fc2_b), own_seg(c)]
        value, osums[c] = grow(
            "output", ins, [own_out(BF, c), fix((half, width), F32), fix((8, width), F32)], output_kernel
        )
        return swap(value, "tensor", tp, 1)

    grad_stream, grad_mix, near_mix, grad_q, grad_k, grad_v, chip, far_chip = {}, {}, {}, {}, {}, {}, {}, {}
    hsums, qsums, esums, far_ffn = {}, {}, {}, {}
    osums, wide_tok, wide_out = {}, {}, {}
    carry = None
    fc2_part = fc1_part = attn_part = None
    for c in order:
        end = (c + 1) * size
        last = c == CHUNKS - 1
        by_half = lambda a: (a, (half, a.shape[1]), lambda i, p: (p[1 - i], 0))
        grad_stream[c], grad_mix[c], wide_mix, ctx_own, ctx_near, hsums[c] = call(
            stream_kernel,
            (1,),
            [whole(a) for a in (back[c], far_back[c], mixed[c], stream[c])]
            + [own(cotangent, c), whole(ln2_g), whole(post_g), whole(wo_chip)],
            [fix((half, width), F32), fix((half, width), BF), fix((half, width), F32)]
            + [fix((half, hw), F32)] * 2
            + [fix((8, width), F32)],
            prefetch=(place,),
            name="stream",
        )
        ctx_near = swap(ctx_near, "tensor", tp, 1)
        near_mix[c] = swap(wide_mix, "tensor", tp, 1)
        results = call(
            functools.partial(attend_back_kernel, c * size, block, last),
            (1,),
            [
                (query, (size, hw), at0(c)),
                (keys, (end, hw), at0(0)),
                (values, (end, hw), at0(0)),
                (seg, (1, size), at1(c)),
                (seg, (1, end), at1(0)),
            ]
            + [whole(a) for a in (ctx_own, ctx_near, attended[c], scale, logsum[c])]
            + ([] if last else [whole(a) for a in carry]),
            [fix((size, hw), BF)] * 3 + [fix((8, hw), F32)] + ([fix((c * size, hw), F32)] * 2 if c else []),
            prefetch=(place,),
            scratch=[pltpu.VMEM((end, hw), F32)] * 2
            + [pltpu.VMEM((end, heads * block), BF)] * 2
            + [pltpu.VMEM((size, hw), BF)],
            name="attend_back",
        )
        grad_q[c], grad_k[c], grad_v[c], qsums[c] = results[:4]
        carry = results[4:]
        if c == order[-1] and near_blocks:
            fc2_part = fc2_sum[0]()
        count = 1 if c == order[-1] else 2
        *sends, keep, esums[c] = call(
            entry_kernel,
            (2,),
            [by_half(a) for a in (grad_q[c], grad_k[c], grad_v[c])]
            + [whole(a) for a in (w_query, w_key, w_value)]
            + [(tokens, (half, width), lambda i, p, c=c: (2 * c + p[1 - i], 0))],
            [fix((half, width // count), F32)] * count + [fix((half, width), F32), fix((8, width), F32)],
            prefetch=(place,),
            name="entry",
        )
        gots = [swap(send, "tensor", tp, 1) for send in sends]
        if c == order[-1]:
            attn_sum = weight(
                [("halves", "chunks"), ("all", "chunks", "chunks", "chunks")],
                [
                    [
                        halves(grad_mix, {c: whole(near_mix[c]) for c in chunks}),
                        [whole(low_ctx[c]) for c in chunks],
                    ],
                    [[whole(entry)]] + [[whole(g[c]) for c in chunks] for g in (grad_q, grad_k, grad_v)],
                ],
                4 * hw,
                "weight_attn",
            )
            for d in order[:-1]:
                far_ffn[d] = swap(ffn[d], "tensor", tp, 2)
                wide_out[d] = result(d)
            far_ffn[c] = swap(line.after(ffn[c]), "tensor", tp, 2)
        (chip[c],) = call(
            chip_kernel,
            (1,),
            [whole(a) for a in (keep, *gots)],
            [fix((half, width), F32)],
            name="chip",
        )
        far_chip[c] = swap(chip[c], "tensor", tp, 2)

    last = order[-1]
    if near_blocks:
        fc1_part = fc1_sum[0]()
    for c in order[:-1]:
        wide_tok[c] = token(c)
    if near_blocks:
        fc2_last = fc2_sum[1](fc2_part)
    wide_out[last] = result(last)
    if near_blocks:
        fc1_last = fc1_sum[1](fc1_part)

    add = lambda parts: functools.reduce(lambda a, b: a + b, [parts[c] for c in chunks])
    fs, gs, ns, hs, qs, es, os = (add(p) for p in (fsums, gsums, nsums, hsums, qsums, esums, osums))
    own_part = jnp.concatenate([hs[:5], fs[:3], os[:2], es[:2], gs[:3]], 0)
    near_part = jnp.concatenate([hs[:5], fs[:3], os[:2], es[:2], ns[:3]], 0)
    packed = own_part + swap(near_part, "tensor", tp, 1)
    far = swap(packed[10:12], "tensor", tp, 2)
    tail = jnp.concatenate([qs[0], qs[1], qs[2], qs[2]]).reshape(1, -1)[:, :width]
    packed = jnp.concatenate([packed[:10], packed[10:12] + far, packed[12:], tail], 0)
    wide_tok[last] = token(last)
    if near_blocks:
        (grad_w_fc1,) = fc1_sum[2](fc1_part, fc1_last)
        attn_part = attn_sum[0]()
        packed = line.after(packed)
        packed = packed + swap(packed, "dp", dp, 1)
        packed = packed + swap(packed, "dp", dp, 2)
    else:
        packed = lax.psum(packed, "dp")
    wides = line.wait([wide[c] for wide in (wide_tok, wide_out) for c in order])
    for index, c in enumerate(order):
        put("tokens", F32, wides[index], c)
        put("output", BF, wides[len(order) + index], c)
    if near_blocks:
        packed = line.keep(line.after(packed))
        attn_last = attn_sum[1](attn_part)
        packed = line.after(packed)
        packed = packed + lax.ppermute(packed, "dp", opposite)
        (grad_w_fc2,) = fc2_sum[2](fc2_part, fc2_last)
        grad_w_out, grad_w_query, grad_w_key, grad_w_value = attn_sum[2](attn_part, attn_last)
    else:
        (grad_w_fc2,), (grad_w_fc1,) = fc2_sum(), fc1_sum()
        grad_w_out, grad_w_query, grad_w_key, grad_w_value = attn_sum()
    grad_tokens, output = grown["tokens"], grown["output"]

    last_row = packed[15]
    counted = packed[7, 0]
    squares = jnp.stack([jnp.sum(packed[5]), jnp.sum(packed[8]), jnp.sum(packed[9])])
    rms = jnp.sqrt(squares / (counted * width))
    grad_head = jnp.sum(last_row[2 * hw : 3 * hw].reshape(heads, HEAD_DIM), axis=1)
    return (
        output,
        grad_tokens,
        grad_w_query,
        grad_w_key,
        grad_w_value,
        grad_w_out,
        grad_w_fc1,
        grad_w_fc2,
        packed[10],
        packed[11],
        packed[2],
        packed[3],
        packed[0],
        packed[1],
        packed[12],
        packed[13],
        last_row[:hw],
        last_row[hw : 2 * hw],
        packed[4],
        packed[14],
        packed[6],
        grad_head,
        rms,
    )


def solution(mesh):
    cut = P(None, "tensor")
    part = P("tensor")
    rows = P("dp", None)
    both = P("dp", "tensor")
    return jax.shard_map(
        functools.partial(body, mesh.shape["dp"], mesh.shape["tensor"]),
        mesh=mesh,
        in_specs=(rows, rows) + (cut,) * 6 + (P(),) * 6 + (part,) * 4 + (P(), part, P(), part, rows),
        out_specs=(rows, rows) + (both,) * 6 + (P(),) * 6 + (part,) * 4 + (P(), part, P(), part, P()),
        check_vma=False,
    )
```

```python
import functools

import jax
import jax.numpy as jnp
from jax import lax
from jax.experimental import pallas as pl
from jax.experimental.pallas import tpu as pltpu
from jax.sharding import PartitionSpec as P

HEAD_DIM = 64
EPSILON = 1e-05
EXCLUDED = -1e30
LANES = 128
CHUNKS = 2
PAD = 16
BF = jnp.bfloat16
F32 = jnp.float32


def dot_nn(a, b):
    return lax.dot_general(a, b, (((1,), (0,)), ((), ())), preferred_element_type=F32)


def dot_nt(a, b):
    return lax.dot_general(a, b, (((1,), (1,)), ((), ())), preferred_element_type=F32)


def dot_tn(a, b):
    return lax.dot_general(a, b, (((0,), (0,)), ((), ())), preferred_element_type=F32)


def normalize(v):
    mean = jnp.mean(v, axis=-1, keepdims=True)
    centred = v - mean
    factor = lax.rsqrt(jnp.mean(centred * centred, axis=-1, keepdims=True) + EPSILON)
    return centred * factor, factor


def norm_back(scaled, normed, factor):
    return factor * (
        scaled
        - jnp.mean(scaled, axis=-1, keepdims=True)
        - normed * jnp.mean(scaled * normed, axis=-1, keepdims=True)
    )


def col_sum(v):
    return jnp.sum(v, axis=0, keepdims=True)


def tanh_inner(v):
    return 0.7978845608028654 * (v + 0.044715 * (v * v * v))


def columns_to_rows(columns):
    n = columns[0].shape[0]
    lane = lax.broadcasted_iota(jnp.int32, (n, LANES), 1)
    tile = jnp.zeros((n, LANES), F32)
    for index, column in enumerate(columns):
        tile = jnp.where(lane == index, column, tile)
    return jnp.transpose(tile)[:8]


def rows_to_columns(rows):
    n = rows[0].shape[1]
    sub = lax.broadcasted_iota(jnp.int32, (LANES, n), 0)
    tile = jnp.zeros((LANES, n), F32)
    for index, row in enumerate(rows):
        tile = jnp.where(sub == index, row, tile)
    tile = jnp.transpose(tile)
    return [tile[:, index : index + 1] for index in range(len(rows))]


def stack_rows(rows, width):
    sub = lax.broadcasted_iota(jnp.int32, (8, width), 0)
    tile = jnp.zeros((8, width), F32)
    for index, row in enumerate(rows):
        tile = jnp.where(sub == index, row, tile)
    return tile


def head_masks(width, kind):
    lane = lax.broadcasted_iota(jnp.int32, (1, width), 1) // HEAD_DIM
    return [(lane == head).astype(F32).astype(kind) for head in range(width // HEAD_DIM)]


def qkv_kernel(tok, gain, bias, wq, wk, wv, qb, vb, entry, q, k, v):
    normed, _ = normalize(tok[...].astype(F32))
    low = (normed * gain[...] + bias[...]).astype(BF)
    entry[...] = low
    q[...] = ((dot_nn(low, wq[...]) + qb[...]) * HEAD_DIM**-0.5).astype(BF)
    k[...] = dot_nn(low, wk[...]).astype(BF)
    v[...] = (dot_nn(low, wv[...]) + vb[...]).astype(BF)


def attend_kernel(first, block, place, q, k, v, segq, segk, scale, attended, low, mine, theirs, logsum, hold):
    rows, width = q.shape
    half = rows // 2
    masks = head_masks(width, BF)
    for at in range(0, rows, block):
        length = first + at + block
        query = q[at : at + block, :]
        keys = k[:length, :]
        (seg,) = rows_to_columns([segq[:, at : at + block].astype(F32)])
        place_q = first + at + lax.broadcasted_iota(jnp.int32, (block, length), 0)
        place_k = lax.broadcasted_iota(jnp.int32, (block, length), 1)
        allowed = (seg == segk[:, :length].astype(F32)) & (place_k <= place_q)
        shift = jnp.where(allowed, 0.0, EXCLUDED)
        total = jnp.zeros((block, width), F32)
        sums = []
        for mask in masks:
            scores = dot_nt(query * mask, keys) + shift
            top = jnp.max(scores, axis=-1, keepdims=True)
            expo = jnp.exp(scores - top)
            norm = jnp.sum(expo, axis=-1, keepdims=True)
            weights = (expo * (1.0 / norm)).astype(BF)
            total = total + dot_nn(weights, v[:length, :] * mask)
            sums.append(top + jnp.log(norm))
        attended[at : at + block, :] = total
        context = (total * scale[...]).astype(BF)
        low[at : at + block, :] = context
        hold[at : at + block, :] = context.astype(F32)
        logsum[:, at : at + block] = columns_to_rows(sums)
    mine[...] = hold[pl.ds(pl.multiple_of(place[0] * half, half), half), :]
    theirs[...] = hold[pl.ds(pl.multiple_of(place[1] * half, half), half), :]


def pack_kernel(wide, near_out, out_pair, fc1, fc2):
    width, units = near_out.shape[1], fc1.shape[1]
    out_pair[:, :width] = near_out[...]
    out_pair[:, width:] = wide[:, :width].astype(BF)
    fc1[...] = wide[:, width : width + units].astype(BF)
    fc2[...] = wide[:, width + units :].astype(BF)


def far_kernel(side, far_half, far_rest, diag_half, diag_rest, out):
    rows, width = far_half.shape
    here = pl.ds(pl.multiple_of(side[0] * rows, rows), rows)
    there = pl.ds(pl.multiple_of((1 - side[0]) * rows, rows), rows)
    out[here, :width] = far_half[...].astype(BF)
    out[there, :width] = far_rest[...].astype(BF)
    out[here, width:] = diag_half[...].astype(BF)
    out[there, width:] = diag_rest[...].astype(BF)


def upstream_kernel(place, cot, own, near, out):
    units = own.shape[1]
    out[:, :units] = dot_nn(cot[...], own[...])
    out[:, units:] = dot_nn(cot[...], near[...])


def forward_kernel(
    place, seg, ctx_chip, ctx_far, wo_chip, wo_far, out_bias, tok, post_gain, post_bias, ln2_gain, ln2_bias,
    fc1_own, fc1_near, fc1_bias, mid_gain, near, cot, grad_middle,
    mixed, stream, inner, share, hidden, stats, sums,
):
    units = fc1_own.shape[1]
    mix = (
        dot_nt(ctx_chip[...].astype(BF), wo_chip[...]) + dot_nt(ctx_far[...].astype(BF), wo_far[...])
    ) + out_bias[...]
    mixed[...] = mix
    normed, _ = normalize(mix)
    branch = normed * post_gain[...] + post_bias[...]
    resid = tok[...].astype(F32) + branch
    stream[...] = resid
    normed2, _ = normalize(resid)
    low = (normed2 * ln2_gain[...] + ln2_bias[...]).astype(BF)
    inner[...] = low
    share[...] = low.astype(F32)
    actives, scaleds = [], []
    for part, (weight, bias, gain) in enumerate(
        ((fc1_own, fc1_bias[...], mid_gain[...]), (fc1_near, near[0:1, :], near[1:2, :]))
    ):
        hid = dot_nn(low, weight[...]) + bias
        hidden[:, part * units : (part + 1) * units] = hid
        actives.append(0.5 * hid * (1.0 + jnp.tanh(tanh_inner(hid))))
        scaleds.append(grad_middle[:, part * units : (part + 1) * units] * gain)

    def both(left, right):
        return jnp.sum(left, axis=-1, keepdims=True) + jnp.sum(right, axis=-1, keepdims=True)

    mean = both(*actives) / (2 * units)
    centred = [active - mean for active in actives]
    stats[...] = columns_to_rows(
        [
            mean,
            both(*[c * c for c in centred]),
            both(*scaleds),
            both(*[s * c for s, c in zip(scaleds, centred)]),
        ]
    )
    (which,) = rows_to_columns([seg[...].astype(F32)])
    valid = (which >= 0).astype(F32)
    sums[...] = stack_rows(
        [
            col_sum(valid * branch * branch),
            col_sum(cot[...].astype(F32)),
            col_sum(valid * jnp.ones_like(branch)),
        ],
        branch.shape[1],
    )


def middle_kernel(
    total, hidden, grad_middle, st0, st1, mid_gain, mid_bias, near,
    fc1_own, fc1_near, fc2_own, fc2_near,
    middle, grad_hidden, share, ffn, back, sums_own, sums_near,
):
    units = fc1_own.shape[1]
    n = 2 * units
    mean = (st0[0:1, :] + st1[0:1, :]) * 0.5
    apart = [s[0:1, :] - mean for s in (st0, st1)]
    spread = (st0[1:2, :] + n * (apart[0] * apart[0])) + (st1[1:2, :] + n * (apart[1] * apart[1]))
    factor = lax.rsqrt(spread / total + EPSILON)
    plain = (st0[2:3, :] + st1[2:3, :]) / total
    along = (st0[3:4, :] + apart[0] * st0[2:3, :]) + (st1[3:4, :] + apart[1] * st1[2:3, :])
    mean, factor, plain, along = rows_to_columns([mean, factor, plain, factor * along / total])
    parts = (
        (mid_gain[...], mid_bias[...], fc1_own, fc2_own, sums_own),
        (near[1:2, :], near[2:3, :], fc1_near, fc2_near, sums_near),
    )
    ffn_parts, back_parts = [], []
    for part, (gain, bias, fc1, fc2, sums) in enumerate(parts):
        hid = hidden[:, part * units : (part + 1) * units]
        bend = jnp.tanh(tanh_inner(hid))
        active = 0.5 * hid * (1.0 + bend)
        slope = 0.5 * (1.0 + bend) + 0.5 * hid * (1.0 - bend * bend) * (
            0.7978845608028654 * (1.0 + 3 * 0.044715 * (hid * hid))
        )
        normed = (active - mean) * factor
        mid = (normed * gain + bias).astype(BF)
        grad = grad_middle[:, part * units : (part + 1) * units]
        low = (factor * (grad * gain - plain - normed * along) * slope).astype(BF)
        if part == 0:
            middle[...] = mid
            grad_hidden[...] = low
        else:
            share[:, :units] = mid.astype(F32)
            share[:, units:] = low.astype(F32)
        sums[...] = stack_rows([col_sum(grad * normed), col_sum(grad), col_sum(low.astype(F32))], units)
        ffn_parts.append(dot_nt(mid, fc2[...]))
        back_parts.append(dot_nt(low, fc1[...]))
    ffn[...] = ffn_parts[0] + ffn_parts[1]
    back[: hidden.shape[0], :] = back_parts[0] + back_parts[1]
    back[hidden.shape[0] :, :] = jnp.zeros((PAD, back.shape[1]), F32)


def stream_kernel(
    place, mine, far, mixed, stream, cot, ln2_gain, post_gain, w_out,
    grad_stream, grad_mixed, wide, context_own, context_near, sums,
):
    grad = mine[: stream.shape[0], :] + far[: stream.shape[0], :]
    normed2, factor2 = normalize(stream[...])
    back = cot[...].astype(F32) + norm_back(grad * ln2_gain[...], normed2, factor2)
    grad_stream[...] = back
    normedp, factorp = normalize(mixed[...])
    low = norm_back(back * post_gain[...], normedp, factorp).astype(BF)
    grad_mixed[...] = low
    wide[...] = low.astype(F32)
    context = dot_nn(low, w_out[...])
    width = context_own.shape[1]
    context_own[...] = context[:, :width]
    context_near[...] = context[:, width:]
    sums[...] = stack_rows(
        [
            col_sum(grad * normed2),
            col_sum(grad),
            col_sum(back * normedp),
            col_sum(back),
            col_sum(low.astype(F32)),
        ],
        back.shape[1],
    )


def attend_back_kernel(first, block, last, place, *refs):
    q, k, v, segq, segk, context_own, context_near, attended, scale, logsum = refs[:10]
    rest = list(refs[10:])
    if not last:
        key_in, value_in = rest[:2]
        rest = rest[2:]
    grad_q, grad_k, grad_v, sums = rest[:4]
    rest = rest[4:]
    if first:
        key_out, value_out = rest[:2]
        rest = rest[2:]
    key_sum, value_sum, low_probs, low_scores, grads = rest
    rows, width = q.shape
    half = rows // 2
    end = first + rows
    masks = head_masks(width, BF)
    wide_masks = head_masks(width, F32)
    if last:
        key_sum[...] = jnp.zeros_like(key_sum)
        value_sum[...] = jnp.zeros_like(value_sum)
    else:
        key_sum[...] = key_in[...]
        value_sum[...] = value_in[...]
    head_sum = jnp.zeros((1, width), F32)
    for part, source in enumerate((context_own, context_near)):
        at = pl.ds(pl.multiple_of(place[part] * half, half), half)
        grad_context = source[...]
        head_sum = head_sum + col_sum(grad_context * attended[at, :])
        grads[at, :] = (grad_context * scale[...]).astype(BF)
    (seg,) = rows_to_columns([segk[:, :end].astype(F32)])
    query_sum = jnp.zeros((1, width), F32)
    for at in range(0, rows, block):
        length = first + at + block
        query = q[at : at + block, :]
        grad = grads[at : at + block, :]
        product = grad.astype(F32) * attended[at : at + block, :]
        delta = columns_to_rows([jnp.sum(product * mask, axis=-1, keepdims=True) for mask in wide_masks])
        place_k = lax.broadcasted_iota(jnp.int32, (length, block), 0)
        place_q = first + at + lax.broadcasted_iota(jnp.int32, (length, block), 1)
        allowed = (seg[:length] == segq[:, at : at + block].astype(F32)) & (place_k <= place_q)
        shift = jnp.where(allowed, 0.0, EXCLUDED)
        queries = [query * mask for mask in masks]
        grad_parts = [grad * mask for mask in masks]
        grad_query = jnp.zeros((block, width), F32)
        for head, mask in enumerate(masks):
            scores = dot_nt(k[:length, :], queries[head]) + shift
            probs = jnp.exp(scores - logsum[head : head + 1, at : at + block])
            low_probs[:length, head * block : (head + 1) * block] = probs.astype(BF)
            grad_probs = dot_nt(v[:length, :], grad_parts[head])
            low = (probs * (grad_probs - delta[head : head + 1, :])).astype(BF)
            low_scores[:length, head * block : (head + 1) * block] = low
            grad_query = grad_query + dot_tn(low, k[:length, :] * mask)
        value_sum[:length, :] += dot_nn(low_probs[:length, :], jnp.concatenate(grad_parts, axis=0))
        key_sum[:length, :] += dot_nn(low_scores[:length, :], jnp.concatenate(queries, axis=0))
        low_query = (grad_query * HEAD_DIM**-0.5).astype(BF)
        grad_q[at : at + block, :] = low_query
        query_sum = query_sum + col_sum(low_query.astype(F32))
    grad_k[...] = key_sum[first:end, :].astype(BF)
    low_value = value_sum[first:end, :].astype(BF)
    grad_v[...] = low_value
    sums[...] = stack_rows([query_sum, col_sum(low_value.astype(F32)), head_sum], width)
    if first:
        key_out[...] = key_sum[:first, :]
        value_out[...] = value_sum[:first, :]


def entry_kernel(place, grad_q, grad_k, grad_v, wq, wk, wv, tok, *refs):
    sends, (keep, sums) = refs[:-2], refs[-2:]
    step = pl.program_id(0)
    part = dot_nt(grad_q[...], wq[...]) + dot_nt(grad_k[...], wk[...]) + dot_nt(grad_v[...], wv[...])
    normed, _ = normalize(tok[...].astype(F32))
    fresh = stack_rows([col_sum(part * normed), col_sum(part)], part.shape[1])

    @pl.when(step == 0)
    def _():
        sums[...] = fresh
        cut = sends[0].shape[1]
        for j, send in enumerate(sends):
            send[...] = part[:, j * cut : (j + 1) * cut]

    @pl.when(step != 0)
    def _():
        sums[...] += fresh
        keep[...] = part


def chip_kernel(keep, *refs):
    gots, out = refs[:-1], refs[-1]
    cut = gots[0].shape[1]
    for j, got in enumerate(gots):
        out[:, j * cut : (j + 1) * cut] = keep[:, j * cut : (j + 1) * cut] + got[...]


def token_kernel(place, mine, far, tok, grad_stream, gain, *refs):
    out, wide = refs[-2:]
    normed, factor = normalize(tok[...].astype(F32))
    grad = grad_stream[...] + norm_back((mine[...] + far[...]) * gain[...], normed, factor)
    out[...] = grad
    wide[...] = grad


def output_kernel(place, mine, far, stream, bias, seg, *refs):
    out, wide, sums = refs[-3:]
    ffn = (mine[...] + far[...]) + bias[...]
    result = stream[...] + ffn
    low = result.astype(BF)
    out[...] = low
    wide[...] = low.astype(F32)
    (which,) = rows_to_columns([seg[...].astype(F32)])
    valid = (which >= 0).astype(F32)
    sums[...] = stack_rows([col_sum(valid * ffn * ffn), col_sum(valid * result * result)], ffn.shape[1])


def put_kernel(place, value, full, out):
    out[...] = value[...].astype(out.dtype)


def line_kernel(kind, chunks, half, place, *refs):
    items, out = refs[:-1], refs[-1]
    for c in range(chunks):
        if kind == "chunks":
            out[2 * c * half : 2 * (c + 1) * half, :] = items[c][...]
        else:
            for part in range(2):
                at = pl.ds(pl.multiple_of((2 * c + place[part]) * half, half), half)
                out[at, :] = items[2 * c + part][...].astype(BF)


def weight_kernel(plan, chunks, half, blocks, place, *refs):
    step = pl.program_id(0)
    refs = list(refs)
    count = {"all": 1, "halves": 2 * chunks, "chunks": chunks}
    sources = [[(kind, [refs.pop(0) for _ in range(count[kind])]) for kind in product] for product in plan]
    send, keep = refs[:2]
    holds = refs[2:]
    depth = send.shape[0]
    operands, fills = [], []
    for product in sources:
        row = []
        for kind, items in product:
            if kind == "all":
                row.append(items[0])
            else:
                hold = holds.pop(0)
                fills.append((kind, items, hold))
                row.append(hold)
        operands.append(row)

    @pl.when(step == 0)
    def _():
        for kind, items, hold in fills:
            line_kernel(kind, chunks, half, place, *items, hold)

    def fill(target):
        offset = 0
        for row in operands:
            left = row[0]
            columns = jnp.concatenate(
                [
                    left[:, pl.ds(pl.multiple_of(blocks[step * depth + j] * LANES, LANES), LANES)]
                    for j in range(depth)
                ],
                axis=1,
            )
            for right in row[1:]:
                total = dot_tn(columns, right[...])
                width = total.shape[1]
                target[:, :, offset : offset + width] = total.reshape(depth, LANES, width)
                offset += width

    @pl.when(step == 0)
    def _():
        fill(send)

    @pl.when(step != 0)
    def _():
        fill(keep)


def first_kernel(keep, got, out):
    out[...] = keep[...] + got[...]


def second_kernel(keep, got, near, out):
    out[...] = (keep[0] + got[0]) + near[0]


def third_kernel(keep, got, near, far, *outs):
    at = 0
    for out in outs:
        cut = slice(at, at + out.shape[1])
        out[...] = ((keep[0, :, cut] + got[0, :, cut]) + near[0, :, cut]) + far[:, cut]
        at += out.shape[1]


def whole(array):
    shape = array.shape
    return (array, shape, lambda *_: (0,) * len(shape))


def swap(value, axis, size, bit):
    return lax.ppermute(value, axis, [(i, i ^ bit) for i in range(size)])


class Order:
    def __init__(self):
        self.last = None

    def after(self, value):
        if self.last is None:
            return value
        return lax.optimization_barrier((value, self.last))[0]

    def keep(self, value):
        self.last = value
        return value

    def wait(self, values):
        tied = lax.optimization_barrier((tuple(values), self.last))
        self.last = tied[1]
        return list(tied[0])

    def call(self, kernel, grid, ins, outs, prefetch=(), scratch=(), aliases=None, vmem=16 << 20, name=None):
        arrays = [item[0] for item in ins]
        specs = [
            pl.BlockSpec(memory_space=pl.ANY) if block is None else pl.BlockSpec(block, place)
            for _, block, place in ins
        ]
        body_of = kernel
        if self.last is not None:
            at = len(prefetch) + len(arrays)
            arrays.append(self.last)
            specs.append(pl.BlockSpec(memory_space=pl.ANY))

            def body_of(*refs):
                return kernel(*refs[:at], *refs[at + 1 :])

        results = pl.pallas_call(
            body_of,
            grid_spec=pltpu.PrefetchScalarGridSpec(
                num_scalar_prefetch=len(prefetch),
                grid=grid,
                in_specs=specs,
                out_specs=[pl.BlockSpec(block, place) for _, _, block, place in outs],
                scratch_shapes=list(scratch),
            ),
            out_shape=[jax.ShapeDtypeStruct(shape, kind) for shape, kind, _, _ in outs],
            input_output_aliases=aliases or {},
            compiler_params=pltpu.CompilerParams(
                dimension_semantics=("arbitrary",) * len(grid), vmem_limit_bytes=vmem
            ),
            cost_estimate=pl.CostEstimate(flops=1000, bytes_accessed=1000, transcendentals=0),
            name=name,
        )(*prefetch, *arrays)
        self.last = min(results, key=lambda r: r.size)
        return results


def body(
    dp, tp, tokens, segments, w_query, w_key, w_value, w_out, w_fc1, w_fc2, ln1_gain, ln1_bias, post_gain, post_bias,
    ln2_gain, ln2_bias, mid_gain, mid_bias, query_bias, value_bias, out_bias, fc1_bias, fc2_bias, head_scale, cotangent,
):
    rows, width = tokens.shape
    hw = w_query.shape[1]
    units = w_fc1.shape[1]
    heads = hw // HEAD_DIM
    size = rows // CHUNKS
    half = size // 2
    block = min(256, size)
    line = Order()
    call = line.call
    row = lambda v: v.reshape(1, -1)
    seg = segments.reshape(1, rows)
    ln1_g, ln1_b, post_g, post_b = row(ln1_gain), row(ln1_bias), row(post_gain), row(post_bias)
    ln2_g, ln2_b, mid_g, mid_b = row(ln2_gain), row(ln2_bias), row(mid_gain), row(mid_bias)
    q_b, v_b, out_b, fc1_b, fc2_b = row(query_bias), row(value_bias), row(out_bias), row(fc1_bias), row(fc2_bias)
    scale = row(jnp.repeat(head_scale, HEAD_DIM))
    core = lax.axis_index("tensor") & 1
    place = (core + jnp.arange(2, dtype=jnp.int32)) & 1
    dp_side = lax.axis_index("dp") & 1
    side = dp_side.astype(jnp.int32).reshape(1)
    chunks = list(range(CHUNKS))
    order = chunks[::-1]

    half_rows = width // 2
    part = lax.dynamic_slice_in_dim(w_out, dp_side * half_rows, half_rows, 0).astype(F32)
    far_half = swap(part, "tensor", tp, 2)
    wide = swap(jnp.concatenate([w_out, w_fc1, w_fc2], 1).astype(F32), "tensor", tp, 1)
    pad = jnp.zeros((5, units), F32)
    near = swap(jnp.concatenate([fc1_b, mid_g, mid_b, pad], 0), "tensor", tp, 1)

    step = min(256, rows)
    entry, query, keys, values = call(
        qkv_kernel,
        (rows // step,),
        [(tokens, (step, width), lambda i: (i, 0))]
        + [whole(a) for a in (ln1_g, ln1_b, w_query, w_key, w_value, q_b, v_b)],
        [((rows, width), BF, (step, width), lambda i: (i, 0))]
        + [((rows, hw), BF, (step, hw), lambda i: (i, 0))] * 3,
        name="qkv",
    )

    at0 = lambda c: (lambda *_: (c, 0))
    at1 = lambda c: (lambda *_: (0, c))
    fix = lambda shape, kind: (shape, kind, shape, lambda *_: (0,) * len(shape))
    own = lambda a, c: (a, (half, a.shape[1]), lambda i, p, c=c: (2 * c + p[0], 0))
    own_seg = lambda c: (seg, (1, half), lambda i, p, c=c: (0, 2 * c + p[0]))

    (far_half,) = line.wait([far_half])
    far_rest = swap(far_half, "dp", dp, 1)
    attended, low_ctx, ctx, logsum = {}, {}, {}, {}
    for c in order:
        end = (c + 1) * size
        attended[c], low_ctx[c], mine, theirs, logsum[c] = call(
            functools.partial(attend_kernel, c * size, block),
            (1,),
            [
                (query, (size, hw), at0(c)),
                (keys, (end, hw), at0(0)),
                (values, (end, hw), at0(0)),
                (seg, (1, size), at1(c)),
                (seg, (1, end), at1(0)),
                whole(scale),
            ],
            [fix((size, hw), F32), fix((size, hw), BF), fix((half, hw), F32), fix((half, hw), F32), fix((8, size), F32)],
            prefetch=(place,),
            scratch=[pltpu.VMEM((size, hw), F32)],
            name="attend",
        )
        ctx[c] = (mine, swap(theirs, "tensor", tp, 1))
    far_ctx = {}
    for c in order:
        mine, got = ctx[c]
        ctx[c] = line.keep(jnp.concatenate([line.after(mine), got], 1))
        far_ctx[c] = swap(ctx[c], "tensor", tp, 2)

    step = min(256, width)
    wo_chip, fc1_near, fc2_near = call(
        pack_kernel,
        (width // step,),
        [(a, (step, a.shape[1]), lambda i: (i, 0)) for a in (wide, w_out)],
        [((width, n), BF, (step, n), lambda i: (i, 0)) for n in (2 * hw, units, units)],
        name="pack",
    )
    diag_half = swap(far_half, "tensor", tp, 1)
    diag_rest = swap(far_rest, "tensor", tp, 1)
    (grad_mid,) = call(
        upstream_kernel,
        (CHUNKS,),
        [(cotangent, (half, width), lambda i, p: (2 * i + p[0], 0)), whole(w_fc2), whole(fc2_near)],
        [((CHUNKS * half, 2 * units), F32, (half, 2 * units), lambda i, p: (i, 0))],
        prefetch=(place,),
        name="upstream",
    )
    (wo_far,) = call(
        far_kernel,
        (1,),
        [whole(a) for a in (far_half, far_rest, diag_half, diag_rest)],
        [fix((width, 2 * hw), BF)],
        prefetch=(side,),
        name="far",
    )

    mixed, stream, inner, hidden, stats, far_stats, fsums, near_inner = {}, {}, {}, {}, {}, {}, {}, {}
    for c in order:
        mixed[c], stream[c], inner[c], share, hidden[c], stats[c], fsums[c] = call(
            forward_kernel,
            (1,),
            [own_seg(c)]
            + [whole(a) for a in (ctx[c], far_ctx[c], wo_chip, wo_far, out_b)]
            + [own(tokens, c)]
            + [whole(a) for a in (post_g, post_b, ln2_g, ln2_b, w_fc1, fc1_near, fc1_b, mid_g, near)]
            + [own(cotangent, c), (grad_mid, (half, 2 * units), at0(c))],
            [fix((half, width), F32)] * 2
            + [fix((half, width), BF), fix((half, width), F32), fix((half, 2 * units), F32)]
            + [fix((8, half), F32), fix((8, width), F32)],
            prefetch=(place,),
            name="forward",
        )
        far_stats[c] = swap(stats[c], "tensor", tp, 2)
        near_inner[c] = swap(share, "tensor", tp, 1)

    middle, grad_hid, ffn, back, far_back, gsums, nsums = {}, {}, {}, {}, {}, {}, {}
    near_mid, near_hid = {}, {}
    for c in order:
        mid, hid, share, ffn[c], back[c], gsums[c], nsums[c] = call(
            functools.partial(middle_kernel, units * tp),
            (1,),
            [whole(hidden[c]), (grad_mid, (half, 2 * units), at0(c))]
            + [whole(a) for a in (stats[c], far_stats[c], mid_g, mid_b, near)]
            + [whole(a) for a in (w_fc1, fc1_near, w_fc2, fc2_near)],
            [fix((half, units), BF)] * 2
            + [fix((half, 2 * units), F32)]
            + [fix((half, width), F32), fix((half + PAD, width), F32)]
            + [fix((8, units), F32)] * 2,
            name="middle",
        )
        middle[c], grad_hid[c] = mid, hid
        far_back[c] = swap(back[c], "tensor", tp, 2)
        near_both = swap(share, "tensor", tp, 1)
        near_mid[c] = (near_both, (half, units), lambda *_: (0, 0))
        near_hid[c] = (near_both, (half, units), lambda *_: (0, 1))

    near_blocks = width // dp == LANES and dp == 8
    if near_blocks:
        depth = dp // 2
        me = lax.axis_index("dp")
        slot = jnp.arange(dp, dtype=jnp.int32)
        ring = me // 2
        at_ring = jnp.stack([depth - 1 - (ring ^ 1), ring ^ 1, depth - 1 - ring, ring] * 2)
        opposite = [(i, dp - 2 - i + 2 * (i & 1)) for i in range(dp)]
        blocks = (2 * at_ring + ((me + 1 + slot // depth) & 1)).astype(jnp.int32)

    def weight(plan, items, columns, name):
        arrays = [item for group in items for operand in group for item in operand]
        kinds = [kind for product in plan for kind in product]
        holds = [
            pltpu.VMEM((rows, operand[0][1][1]), BF)
            for kind, operand in zip(kinds, [o for g in items for o in g])
            if kind != "all"
        ]
        if not near_blocks:
            results = []
            for product, group in zip(plan, items):
                full = []
                for kind, operand in zip(product, group):
                    if kind == "all":
                        full.append(operand[0][0])
                        continue
                    n = operand[0][1][1]
                    (lined,) = call(
                        functools.partial(line_kernel, kind, CHUNKS, half),
                        (1,),
                        operand,
                        [fix((rows, n), BF)],
                        prefetch=(place,),
                        name=name,
                    )
                    full.append(lined)
                results += [
                    lax.psum_scatter(dot_tn(full[0], right), "dp", scatter_dimension=0, tiled=True)
                    for right in full[1:]
                ]
            return lambda: results
        send, keep = call(
            functools.partial(weight_kernel, plan, CHUNKS, half),
            (2,),
            arrays,
            [fix((depth, LANES, columns), F32)] * 2,
            prefetch=(blocks, place),
            scratch=holds,
            name=name,
        )
        got = swap(send, "dp", dp, 1)

        lanes = min(1024, columns)
        by_lanes = lambda array, count, first: (array, (count, LANES, lanes), lambda i: (first, 0, i))

        def first():
            (send,) = call(
                first_kernel,
                (columns // lanes,),
                [by_lanes(a, 2, 0) for a in (keep, got)],
                [((2, LANES, columns), F32, (2, LANES, lanes), lambda i: (0, 0, i))],
                name="first",
            )
            return swap(send, "dp", dp, 2)

        def second(near):
            (send,) = call(
                second_kernel,
                (columns // lanes,),
                [by_lanes(a, 1, 2) for a in (keep, got)] + [by_lanes(near, 1, 0)],
                [((LANES, columns), F32, (LANES, lanes), lambda i: (0, i))],
                name="second",
            )
            return lax.ppermute(send, "dp", opposite)

        def third(near, far):
            return call(
                third_kernel,
                (1,),
                [(a, (1, LANES, columns), lambda *_, f=f: (f, 0, 0)) for a, f in ((keep, 3), (got, 3), (near, 1))]
                + [whole(far)],
                [fix((LANES, operand[0][1][1]), F32) for group in items for operand in group[1:]],
                name="third",
            )

        return first, second, third

    halves = lambda mine, wide_near: [item for c in chunks for item in (whole(mine[c]), wide_near[c])]
    fc2_sum = weight(
        [("all", "halves")],
        [[[whole(cotangent)], halves(middle, near_mid)]],
        units,
        "weight_fc2",
    )
    fc1_sum = weight(
        [("halves", "halves")],
        [
            [
                halves(inner, {c: whole(near_inner[c]) for c in chunks}),
                halves(grad_hid, near_hid),
            ]
        ],
        units,
        "weight_fc1",
    )

    own_out = lambda kind, c: ((rows, width), kind, (half, width), lambda i, p, c=c: (2 * c + p[0], 0))
    grown = {"tokens": None, "output": None}

    def grow(which, ins, outs, kernel):
        aliases = None
        if grown[which] is not None:
            aliases = {1 + len(ins): 0}
            ins = ins + [(grown[which], None, None)]
        results = call(kernel, (1,), ins, outs, prefetch=(place,), aliases=aliases, name=which)
        grown[which] = results[0]
        return results[1:]

    def put(which, kind, value, c):
        grow(which, [whole(value)], [((rows, width), kind, (half, width), lambda i, p: (2 * c + p[1], 0))], put_kernel)

    def token(c):
        ins = [(a, (half, width), at0(0)) for a in (chip[c], far_chip[c])]
        ins += [own(tokens, c), whole(grad_stream[c]), whole(ln1_g)]
        (value,) = grow("tokens", ins, [own_out(F32, c), fix((half, width), F32)], token_kernel)
        return swap(value, "tensor", tp, 1)

    def result(c):
        ins = [whole(ffn[c]), whole(far_ffn[c]), whole(stream[c]), whole(fc2_b), own_seg(c)]
        value, osums[c] = grow(
            "output", ins, [own_out(BF, c), fix((half, width), F32), fix((8, width), F32)], output_kernel
        )
        return swap(value, "tensor", tp, 1)

    grad_stream, grad_mix, near_mix, grad_q, grad_k, grad_v, chip, far_chip = {}, {}, {}, {}, {}, {}, {}, {}
    hsums, qsums, esums, far_ffn = {}, {}, {}, {}
    osums, wide_tok, wide_out = {}, {}, {}
    carry = None
    fc2_part = fc1_part = attn_part = None
    for c in order:
        end = (c + 1) * size
        last = c == CHUNKS - 1
        by_half = lambda a: (a, (half, a.shape[1]), lambda i, p: (p[1 - i], 0))
        grad_stream[c], grad_mix[c], wide_mix, ctx_own, ctx_near, hsums[c] = call(
            stream_kernel,
            (1,),
            [whole(a) for a in (back[c], far_back[c], mixed[c], stream[c])]
            + [own(cotangent, c), whole(ln2_g), whole(post_g), whole(wo_chip)],
            [fix((half, width), F32), fix((half, width), BF), fix((half, width), F32)]
            + [fix((half, hw), F32)] * 2
            + [fix((8, width), F32)],
            prefetch=(place,),
            name="stream",
        )
        ctx_near = swap(ctx_near, "tensor", tp, 1)
        near_mix[c] = swap(wide_mix, "tensor", tp, 1)
        results = call(
            functools.partial(attend_back_kernel, c * size, block, last),
            (1,),
            [
                (query, (size, hw), at0(c)),
                (keys, (end, hw), at0(0)),
                (values, (end, hw), at0(0)),
                (seg, (1, size), at1(c)),
                (seg, (1, end), at1(0)),
            ]
            + [whole(a) for a in (ctx_own, ctx_near, attended[c], scale, logsum[c])]
            + ([] if last else [whole(a) for a in carry]),
            [fix((size, hw), BF)] * 3 + [fix((8, hw), F32)] + ([fix((c * size, hw), F32)] * 2 if c else []),
            prefetch=(place,),
            scratch=[pltpu.VMEM((end, hw), F32)] * 2
            + [pltpu.VMEM((end, heads * block), BF)] * 2
            + [pltpu.VMEM((size, hw), BF)],
            name="attend_back",
        )
        grad_q[c], grad_k[c], grad_v[c], qsums[c] = results[:4]
        carry = results[4:]
        if c == order[-1] and near_blocks:
            fc2_part = fc2_sum[0]()
        count = 1 if c == order[-1] else 2
        *sends, keep, esums[c] = call(
            entry_kernel,
            (2,),
            [by_half(a) for a in (grad_q[c], grad_k[c], grad_v[c])]
            + [whole(a) for a in (w_query, w_key, w_value)]
            + [(tokens, (half, width), lambda i, p, c=c: (2 * c + p[1 - i], 0))],
            [fix((half, width // count), F32)] * count + [fix((half, width), F32), fix((8, width), F32)],
            prefetch=(place,),
            name="entry",
        )
        gots = [swap(send, "tensor", tp, 1) for send in sends]
        if c == order[-1]:
            for d in order[:-1]:
                far_ffn[d] = swap(ffn[d], "tensor", tp, 2)
                wide_out[d] = result(d)
            far_ffn[c] = swap(line.after(ffn[c]), "tensor", tp, 2)
        (chip[c],) = call(
            chip_kernel,
            (1,),
            [whole(a) for a in (keep, *gots)],
            [fix((half, width), F32)],
            name="chip",
        )
        far_chip[c] = swap(chip[c], "tensor", tp, 2)

    attn_sum = weight(
        [("halves", "chunks"), ("all", "chunks", "chunks", "chunks")],
        [
            [
                halves(grad_mix, {c: whole(near_mix[c]) for c in chunks}),
                [whole(low_ctx[c]) for c in chunks],
            ],
            [[whole(entry)]] + [[whole(g[c]) for c in chunks] for g in (grad_q, grad_k, grad_v)],
        ],
        4 * hw,
        "weight_attn",
    )
    for c in order[:-1]:
        wide_tok[c] = token(c)
    last = order[-1]
    if near_blocks:
        fc2_last = fc2_sum[1](fc2_part)
        fc1_part = fc1_sum[0]()
        (grad_w_fc2,) = fc2_sum[2](fc2_part, fc2_last)
    wide_out[last] = result(last)
    if near_blocks:
        fc1_last = fc1_sum[1](fc1_part)

    add = lambda parts: functools.reduce(lambda a, b: a + b, [parts[c] for c in chunks])
    fs, gs, ns, hs, qs, es, os = (add(p) for p in (fsums, gsums, nsums, hsums, qsums, esums, osums))
    own_part = jnp.concatenate([hs[:5], fs[:3], os[:2], es[:2], gs[:3]], 0)
    near_part = jnp.concatenate([hs[:5], fs[:3], os[:2], es[:2], ns[:3]], 0)
    packed = own_part + swap(near_part, "tensor", tp, 1)
    far = swap(packed[10:12], "tensor", tp, 2)
    tail = jnp.concatenate([qs[0], qs[1], qs[2], qs[2]]).reshape(1, -1)[:, :width]
    packed = jnp.concatenate([packed[:10], packed[10:12] + far, packed[12:], tail], 0)
    wide_tok[last] = token(last)
    line.keep(packed)

    if near_blocks:
        attn_part = attn_sum[0]()
        packed = line.after(packed)
        packed = packed + swap(packed, "dp", dp, 1)
        packed = packed + swap(packed, "dp", dp, 2)
    else:
        packed = lax.psum(packed, "dp")
    wides = line.wait([wide[c] for wide in (wide_tok, wide_out) for c in order])
    for index, c in enumerate(order):
        put("tokens", F32, wides[index], c)
        put("output", BF, wides[len(order) + index], c)
    if near_blocks:
        (fc1_last,) = line.wait([fc1_last])
        packed = line.after(packed)
        attn_last = attn_sum[1](attn_part)
        packed = line.after(packed)
        packed = packed + lax.ppermute(packed, "dp", opposite)
        (grad_w_fc1,) = fc1_sum[2](fc1_part, fc1_last)
        grad_w_out, grad_w_query, grad_w_key, grad_w_value = attn_sum[2](attn_part, attn_last)
    else:
        (grad_w_fc2,), (grad_w_fc1,) = fc2_sum(), fc1_sum()
        grad_w_out, grad_w_query, grad_w_key, grad_w_value = attn_sum()
    grad_tokens, output = grown["tokens"], grown["output"]

    last_row = packed[15]
    counted = packed[7, 0]
    squares = jnp.stack([jnp.sum(packed[5]), jnp.sum(packed[8]), jnp.sum(packed[9])])
    rms = jnp.sqrt(squares / (counted * width))
    grad_head = jnp.sum(last_row[2 * hw : 3 * hw].reshape(heads, HEAD_DIM), axis=1)
    return (
        output,
        grad_tokens,
        grad_w_query,
        grad_w_key,
        grad_w_value,
        grad_w_out,
        grad_w_fc1,
        grad_w_fc2,
        packed[10],
        packed[11],
        packed[2],
        packed[3],
        packed[0],
        packed[1],
        packed[12],
        packed[13],
        last_row[:hw],
        last_row[hw : 2 * hw],
        packed[4],
        packed[14],
        packed[6],
        grad_head,
        rms,
    )


def solution(mesh):
    cut = P(None, "tensor")
    part = P("tensor")
    rows = P("dp", None)
    both = P("dp", "tensor")
    return jax.shard_map(
        functools.partial(body, mesh.shape["dp"], mesh.shape["tensor"]),
        mesh=mesh,
        in_specs=(rows, rows) + (cut,) * 6 + (P(),) * 6 + (part,) * 4 + (P(), part, P(), part, rows),
        out_specs=(rows, rows) + (both,) * 6 + (P(),) * 6 + (part,) * 4 + (P(), part, P(), part, P()),
        check_vma=False,
    )
```
